32 devices in a mesh: dp: 8 (over z, x), branch: 2 (over core), tensor: 2 (over y).
Axes of the slice: x: 2, y: 2, z: 4, core: 2. Of those that a mesh axis runs over, the one named last changes fastest.
Arguments:
- inputs: bfloat16 [13312, 1024], P('dp', ('branch', 'tensor')), may hold values from -6 to 6
- cotangent: bfloat16 [13312, 1024], P('dp', ('branch', 'tensor')), may hold values from -6 to 6
- seg_ids: int32 [13312], P('dp'), may hold values from -1 to 2, as said below
- pad_mask: int32 [13312], P('dp'), may hold values from 0 to 1, as said below
- positions: int32 [13312], P('dp'), may hold values from 0 to 1023, as said below
- ln_gain: bfloat16 [1024], P(('branch', 'tensor')), may hold values from 0.5 to 1.5
- ln_bias: bfloat16 [1024], P(('branch', 'tensor')), may hold values from -1.75 to 1.75
- w_qkv: bfloat16 [1024, 3, 1024], P('branch', None, 'tensor'), may hold values from -0.1875 to 0.1875
- w_attn_out: bfloat16 [1024, 1024], P('tensor', 'branch'), may hold values from -0.75 to 0.75
- w_up: bfloat16 [1024, 4096], P('branch', 'tensor'), may hold values from -0.1875 to 0.1875
- b_up: bfloat16 [4096], P('tensor'), may hold values from -3 to 3
- w_down: bfloat16 [4096, 1024], P('tensor', 'branch'), may hold values from -0.09375 to 0.09375
- b_down: bfloat16 [1024], P(('branch', 'tensor')), may hold values from -3 to 3
Outputs:
- output: bfloat16 [13312, 1024], P('dp', ('branch', 'tensor'))
- input_grad: float32 [13312, 1024], P('dp', ('branch', 'tensor'))
- grad_gain: float32 [1024], P(('branch', 'tensor'))
- grad_bias: float32 [1024], P(('branch', 'tensor'))
- grad_qkv: float32 [1024, 3, 1024], P('branch', None, 'tensor')
- grad_attn_out: float32 [1024, 1024], P('tensor', 'branch')
- grad_up: float32 [1024, 4096], P('branch', 'tensor')
- grad_up_bias: float32 [4096], P('tensor')
- grad_down: float32 [4096, 1024], P('tensor', 'branch')
- grad_down_bias: float32 [1024], P(('branch', 'tensor'))
The draws below stay inside these ranges and needn't reach their ends.
Inputs may be any that keep to these rules, and one draw needn't show every extreme that they name: `seg_ids`: each row of 1664 slots (one row an index of dp) holds exactly 3 whole proteins from its first slot on, numbered 0, 1, ... in order; one protein of every row has exactly 1024 residues, the others 30 to 256; the slots after the last protein, one or more, are padding and carry -1. `pad_mask`: 1 exactly where seg_ids is not -1. `positions`: the slot's index within its protein, from 0; 0 on padding.
All inputs are finite; a program needn't handle non-finite values.
Results may differ from the reference program's by a relative error of at most 0.0059.
Values may be sent and summed in bfloat16 or wider, within the bound.
No kernel may reach another device: no remote copies, remote signals or barrier semaphores. Data moves between devices by JAX's collectives and lax.ppermute only.
A program may use at most 256 MiB of HBM per device.

```python
import jax
import jax.numpy as jnp
from jax import lax

D = 1024
HEADS = 16
ROTARY = 32
FF = 4096
LONGEST = 1024
SHORTEST = 30
ROW = 1664
PIECES = 2
TOKENS = 13312


def protein_layout(key):
    row_count = TOKENS // ROW
    row_keys = jax.random.split(jax.random.fold_in(key, 7), row_count)

    def one_row(row_key):
        len_key, place_key = jax.random.split(row_key)
        short_lengths = jax.random.randint(len_key, (PIECES + 1,), SHORTEST, LONGEST // 4 + 1, dtype=jnp.int32)
        long_place = jax.random.randint(place_key, (), 0, PIECES + 1, dtype=jnp.int32)
        order_idx = jnp.arange(PIECES + 1, dtype=jnp.int32)
        lengths = jnp.where(order_idx == long_place, LONGEST, short_lengths).astype(jnp.int32)
        end_slots = jnp.cumsum(lengths).astype(jnp.int32)
        slot_index = jnp.arange(ROW, dtype=jnp.int32)
        finished = end_slots[None, :] <= slot_index[:, None]
        done_count = jnp.sum(finished.astype(jnp.int32), axis=1)
        start_slot = jnp.max(jnp.where(finished, end_slots[None, :], 0), axis=1)
        used_slots = end_slots[PIECES]
        live_slot = slot_index < used_slots
        return (jnp.where(live_slot, done_count, -1), live_slot.astype(jnp.int32), jnp.where(live_slot, slot_index - start_slot, 0))
    seg_rows, mask_rows, pos_rows = jax.vmap(one_row)(row_keys)
    return (seg_rows.reshape(-1), mask_rows.reshape(-1), pos_rows.reshape(-1))


def draw_seg_ids(key, part):
    return protein_layout(key)[0]


def draw_pad_mask(key, part):
    return protein_layout(key)[1]


def draw_positions(key, part):
    return protein_layout(key)[2]


def block_scale(stream_key, dims, shards, smallest, high):
    def one(dim, parts):
        heights = jax.random.uniform(jax.random.fold_in(jax.random.fold_in(stream_key, 6), dim), (parts,), jnp.float32, smallest / len(shards), high / len(shards))
        return jnp.repeat(jnp.exp(heights), dims[dim] // parts).reshape((-1,) + (1,) * (len(dims) - dim - 1))

    factor_of = one(*shards[0])
    for cut in shards[1:]:
        factor_of = factor_of * one(*cut)
    return factor_of


def bell_draw(own_key, shape, width, limit, cuts=(), kind=jnp.bfloat16):
    values = width * jax.random.normal(own_key, shape, jnp.float32)
    if cuts:
        values = values * block_scale(own_key, shape, cuts, -0.22, 0.18)
    return jnp.clip(values, -limit, limit).astype(kind)


def setup_inputs(seed: int = 0) -> dict:
    splits = jax.random.split(jax.random.key(seed), 14)
    return {
        "inputs": bell_draw(splits[0], (TOKENS, D), 1.0, 6.0, ((0, 8), (1, 4))),
        "cotangent": bell_draw(splits[1], (TOKENS, D), 1.0, 6.0, ((0, 8), (1, 4))),
        "seg_ids": draw_seg_ids(jax.random.fold_in(splits[13], 71), 0),
        "pad_mask": draw_pad_mask(jax.random.fold_in(splits[13], 71), 0),
        "positions": draw_positions(jax.random.fold_in(splits[13], 71), 0),
        "ln_gain": jnp.clip(1.0 + 0.1 * jax.random.normal(splits[5], (D,), jnp.float32), 0.5, 1.5).astype(jnp.bfloat16),
        "ln_bias": bell_draw(splits[6], (D,), 0.3, 1.75, ((0, 4),)),
        "w_qkv": bell_draw(splits[7], (D, 3, D), D ** -0.5, 0.1875, ((0, 2), (2, 2))),
        "w_attn_out": bell_draw(splits[8], (D, D), (D // 16) ** -0.5, 0.75, ((0, 2), (1, 2))),
        "w_up": bell_draw(splits[9], (D, FF), D ** -0.5, 0.1875, ((0, 2), (1, 2))),
        "b_up": bell_draw(splits[10], (FF,), 0.5, 3.0, ((0, 2),)),
        "w_down": bell_draw(splits[11], (FF, D), FF ** -0.5, 0.09375, ((0, 2), (1, 2))),
        "b_down": bell_draw(splits[12], (D,), 0.5, 3.0, ((0, 4),)),
    }


@jax.custom_vjp
def low(v):
    return lax.optimization_barrier(v.astype(jnp.bfloat16)).astype(jnp.float32)

@jax.custom_vjp
def low_back(v):
    return v

def low_keep(v):
    return (low(v), None)

def low_pass(kept, grad):
    return (grad,)

def back_keep(v):
    return (v, None)

def back_low(kept, grad):
    return (low(grad),)
low.defvjp(low_keep, low_pass)
low_back.defvjp(back_keep, back_low)
eps_norm = 1e-05
neg_big = -1e+30
HIGH = lax.Precision.HIGHEST

def frequencies():
    return 10000.0 ** (-(2.0 * jnp.arange(ROTARY // 2, dtype=jnp.float32)) / ROTARY)

def rotate(tensor_in, cosines, sine_table):
    row_count, head_count, head_width = tensor_in.shape
    pair_view = tensor_in[..., :ROTARY].reshape(row_count, head_count, ROTARY // 2, 2)
    first = pair_view[..., 0]
    second = pair_view[..., 1]
    turned = jnp.stack([first * cosines - second * sine_table, second * cosines + first * sine_table], axis=-1)
    return jnp.concatenate([turned.reshape(row_count, head_count, ROTARY), tensor_in[..., ROTARY:]], axis=-1)

def allowed_table(row_seg, row_mask):
    slot_index = jnp.arange(ROW, dtype=jnp.int32)
    same_seg = row_seg[:, None] == row_seg[None, :]
    causal = slot_index[None, :] <= slot_index[:, None]
    live_key = (row_mask[None, :] == 1) | (slot_index[:, None] == slot_index[None, :])
    return same_seg & causal & live_key

def row_layer(param_set, row_item):
    gain, shift, w_qkv, w_attn_out, w_up, b_up, w_down, b_down = param_set
    row_x, row_seg, row_mask, row_pos = row_item
    head_dim = D // HEADS
    center = row_x - lax.optimization_barrier(jnp.mean(row_x, axis=1, keepdims=True))
    inv_root = lax.rsqrt(lax.optimization_barrier(jnp.mean(center * center, axis=1, keepdims=True)) + eps_norm)
    normed = low(center * inv_root * gain + shift)
    qkv_joint = low_back(jnp.dot(normed, w_qkv.reshape(D, 3 * D), precision=HIGH)).reshape(ROW, 3, HEADS, head_dim)
    angles = row_pos.astype(jnp.float32)[:, None] * frequencies()[None, :]
    cosines = jnp.cos(angles)[:, None, :]
    sine_table = jnp.sin(angles)[:, None, :]
    queries = low(rotate(qkv_joint[:, 0], cosines, sine_table))
    keys_rot = low(rotate(qkv_joint[:, 1], cosines, sine_table))
    values = low(qkv_joint[:, 2])
    allowed = allowed_table(row_seg, row_mask)
    raw_scores = low_back(jnp.einsum('qhd,khd->hqk', queries, keys_rot, precision=HIGH))
    logits = jnp.where(allowed[None], raw_scores * head_dim ** (-0.5), neg_big)
    attn_probs = low(jax.nn.softmax(logits, axis=-1))
    mixed_heads = low(low_back(jnp.einsum('hqk,khd->qhd', attn_probs, values, precision=HIGH))).reshape(ROW, D)
    attn_term = jnp.dot(mixed_heads, w_attn_out, precision=HIGH)
    hidden = low_back(jnp.dot(normed, w_up, precision=HIGH) + b_up)
    active = low(jax.nn.gelu(hidden, approximate=True))
    mlp_term = jnp.dot(active, w_down, precision=HIGH)
    return row_x + attn_term + mlp_term + b_down

def reference(inputs, cotangent, seg_ids, pad_mask, positions, ln_gain, ln_bias, w_qkv, w_attn_out, w_up, b_up, w_down, b_down):
    row_count = TOKENS // ROW
    param_set = (ln_gain.astype(jnp.float32), ln_bias.astype(jnp.float32), w_qkv.astype(jnp.float32), w_attn_out.astype(jnp.float32), w_up.astype(jnp.float32), b_up.astype(jnp.float32), w_down.astype(jnp.float32), b_down.astype(jnp.float32))
    seg_rows = seg_ids.reshape(row_count, ROW)
    mask_rows = pad_mask.reshape(row_count, ROW)
    pos_rows = positions.reshape(row_count, ROW)

    def forward(inputs_f, params_f):

        def one_row(row_item):
            return row_layer(params_f, row_item)
        stacked = lax.map(jax.checkpoint(one_row), (inputs_f.reshape(row_count, ROW, D), seg_rows, mask_rows, pos_rows))
        return stacked.reshape(TOKENS, D)
    result, pullback = jax.vjp(forward, inputs.astype(jnp.float32), param_set)
    input_grad, param_grads = pullback(cotangent.astype(jnp.float32))
    grad_gain, grad_bias, grad_qkv, grad_attn_out, grad_up, grad_up_bias, grad_down, grad_down_bias = param_grads
    return (result.astype(jnp.bfloat16), input_grad, grad_gain, grad_bias, grad_qkv, grad_attn_out, grad_up, grad_up_bias, grad_down, grad_down_bias)
```

```python
import functools

import jax
import jax.numpy as jnp
from jax import lax
from jax.experimental import pallas as pl
from jax.experimental.pallas import tpu as pltpu
from jax.sharding import PartitionSpec as P

HEAD_DIM = 64
ROTARY = 32
PAIR = 2 * HEAD_DIM
QB = 128
KC = 256
EPS = 1e-05
NEG = -1e30
F32 = jnp.float32
BF16 = jnp.bfloat16
SWAP = [(0, 1), (1, 0)]
GELU_A = 0.7978845608028654
GELU_B = 0.044715


def nn(a, b):
    return lax.dot_general(a, b, (((1,), (0,)), ((), ())), preferred_element_type=F32)


def nt(a, b):
    return lax.dot_general(a, b, (((1,), (1,)), ((), ())), preferred_element_type=F32)


def tn(a, b):
    return lax.dot_general(a, b, (((0,), (0,)), ((), ())), preferred_element_type=F32)


def partner(x, even):
    width = x.shape[1]
    return jnp.where(even, pltpu.roll(x, width - 1, 1), pltpu.roll(x, 1, 1))


def attention_kernel(
    pairs,
    low_ref,
    joint_ref,
    dmix_ref,
    cos_ref,
    sin_ref,
    start_ref,
    mixed_ref,
    dj_ref,
    q_s,
    k_s,
    v_s,
    g_s,
    kt_s,
    vt_s,
    gt_s,
    s_s,
    ot_s,
    dq_s,
    dk_s,
    dv_s,
):
    rows = joint_ref.shape[0]
    padded = k_s.shape[1]
    width = pairs * PAIR
    lane = lax.broadcasted_iota(jnp.int32, (QB, PAIR), 1)
    even = lane % 2 == 0
    first = lane < HEAD_DIM

    for p in range(pairs):
        k_s[p, rows:, :] = jnp.zeros((padded - rows, PAIR), BF16)
        v_s[p, rows:, :] = jnp.zeros((padded - rows, PAIR), BF16)
        kt_s[p, :, rows:] = jnp.zeros((PAIR, padded - rows), BF16)
        vt_s[p, :, rows:] = jnp.zeros((PAIR, padded - rows), BF16)

    @pl.loop(0, rows // QB)
    def _(i):
        at = pl.ds(pl.multiple_of(i * QB, QB), QB)
        cosines = cos_ref[at, :]
        sines = sin_ref[at, :]
        for p in range(pairs):
            q = joint_ref[at, p * PAIR : (p + 1) * PAIR]
            k = joint_ref[at, width + p * PAIR : width + (p + 1) * PAIR]
            v = joint_ref[at, 2 * width + p * PAIR : 2 * width + (p + 1) * PAIR]
            g = dmix_ref[at, p * PAIR : (p + 1) * PAIR].astype(F32)
            q = (q * cosines + partner(q, even) * sines) * (HEAD_DIM**-0.5)
            k = k * cosines + partner(k, even) * sines
            q_s[p, i, :QB, :] = jnp.where(first, q, 0.0).astype(BF16)
            q_s[p, i, QB:, :] = jnp.where(first, 0.0, q).astype(BF16)
            g_s[p, i, :QB, :] = jnp.where(first, g, 0.0).astype(BF16)
            g_s[p, i, QB:, :] = jnp.where(first, 0.0, g).astype(BF16)
            k_s[p, at, :] = k.astype(BF16)
            v_s[p, at, :] = v.astype(BF16)
            kt_s[p, :, at] = k.T.astype(BF16)
            vt_s[p, :, at] = v.T.astype(BF16)
            gt_s[p, i] = g.T

    @pl.loop(0, padded // QB)
    def _(i):
        at = pl.ds(pl.multiple_of(i * QB, QB), QB)
        for p in range(pairs):
            dk_s[p, at, :] = jnp.zeros((QB, PAIR), F32)
            dv_s[p, at, :] = jnp.zeros((QB, PAIR), F32)

    top = lax.broadcasted_iota(jnp.int32, (PAIR, QB), 0) < HEAD_DIM
    key_slot = lax.broadcasted_iota(jnp.int32, (KC, 2 * QB), 0)
    query_slot = lax.broadcasted_iota(jnp.int32, (1, 2 * QB), 1) % QB

    @pl.loop(0, rows // QB)
    def _(i):
        begin = low_ref[i] // KC
        end = (i * QB + QB - 1) // KC + 1
        query = query_slot + i * QB
        start = start_ref[i]
        for p in range(pairs):
            ot_s[p] = jnp.zeros((PAIR, 2 * QB), F32)
            dq_s[p] = jnp.zeros((PAIR, 2 * QB), F32)

        def forward(c, carry):
            at = pl.ds(pl.multiple_of(c * KC, KC), KC)
            key = key_slot + c * KC
            ok = (key >= start) & (key <= query)
            out = []
            for p in range(pairs):
                peak, total = carry[2 * p], carry[2 * p + 1]
                s = jnp.where(ok, nt(k_s[p, at, :], q_s[p, i]), NEG)
                s_s[p, at, :] = s
                new = jnp.maximum(peak, jnp.max(s, axis=0, keepdims=True))
                e = jnp.exp(s - new)
                fade = jnp.exp(peak - new)
                ot_s[p] = ot_s[p] * fade + nn(vt_s[p, :, at], e.astype(BF16))
                out += [new, total * fade + jnp.sum(e, axis=0, keepdims=True)]
            return tuple(out)

        init = (jnp.full((1, 2 * QB), NEG, F32), jnp.zeros((1, 2 * QB), F32)) * pairs
        stats = lax.fori_loop(begin, end, forward, init)
        norm, delta = [], []
        here = pl.ds(pl.multiple_of(i * QB, QB), QB)
        for p in range(pairs):
            peak, total = stats[2 * p], stats[2 * p + 1]
            norm.append(peak + jnp.log(total))
            o = ot_s[p] * (1.0 / total)
            o = jnp.where(top, o[:, :QB], o[:, QB:])
            mixed_ref[here, p * PAIR : (p + 1) * PAIR] = o.T.astype(BF16)
            prod = o * gt_s[p, i]
            delta.append(
                jnp.concatenate(
                    [
                        jnp.sum(prod[:HEAD_DIM], axis=0, keepdims=True),
                        jnp.sum(prod[HEAD_DIM:], axis=0, keepdims=True),
                    ],
                    axis=1,
                )
            )

        def backward(c, carry):
            at = pl.ds(pl.multiple_of(c * KC, KC), KC)
            for p in range(pairs):
                prob = jnp.exp(s_s[p, at, :] - norm[p])
                ds = (prob * (nt(v_s[p, at, :], g_s[p, i]) - delta[p])).astype(BF16)
                dv_s[p, at, :] += nn(prob.astype(BF16), g_s[p, i])
                dk_s[p, at, :] += nn(ds, q_s[p, i])
                dq_s[p] += nn(kt_s[p, :, at], ds)
            return carry

        lax.fori_loop(begin, end, backward, 0)
        for p in range(pairs):
            d = dq_s[p]
            d = (jnp.where(top, d[:, :QB], d[:, QB:]) * (HEAD_DIM**-0.5)).T
            d = d * cos_ref[here, :] - partner(d, even) * sin_ref[here, :]
            dj_ref[here, p * PAIR : (p + 1) * PAIR] = d.astype(BF16)

    @pl.loop(0, rows // QB)
    def _(i):
        at = pl.ds(pl.multiple_of(i * QB, QB), QB)
        cosines = cos_ref[at, :]
        sines = sin_ref[at, :]
        for p in range(pairs):
            d = dk_s[p, at, :]
            d = d * cosines - partner(d, even) * sines
            dj_ref[at, width + p * PAIR : width + (p + 1) * PAIR] = d.astype(BF16)
            dj_ref[at, 2 * width + p * PAIR : 2 * width + (p + 1) * PAIR] = dv_s[p, at, :].astype(
                BF16
            )


def attention(joint, dmix, cosines, sines, positions):
    rows = joint.shape[0]
    pairs = dmix.shape[1] // PAIR
    blocks = rows // QB
    padded = -(-rows // KC) * KC
    start = jnp.arange(rows, dtype=jnp.int32) - positions
    low = start.reshape(blocks, QB)[:, 0]
    start = start.reshape(blocks, 1, QB)
    start = jnp.concatenate([start, start], axis=2)
    vmem = pl.BlockSpec(memory_space=pltpu.VMEM)
    return pl.pallas_call(
        functools.partial(attention_kernel, pairs),
        out_shape=(
            jax.ShapeDtypeStruct((rows, pairs * PAIR), BF16),
            jax.ShapeDtypeStruct((rows, 3 * pairs * PAIR), BF16),
        ),
        in_specs=[pl.BlockSpec(memory_space=pltpu.SMEM)] + [vmem] * 5,
        out_specs=(vmem, vmem),
        scratch_shapes=[
            pltpu.VMEM((pairs, blocks, 2 * QB, PAIR), BF16),
            pltpu.VMEM((pairs, padded, PAIR), BF16),
            pltpu.VMEM((pairs, padded, PAIR), BF16),
            pltpu.VMEM((pairs, blocks, 2 * QB, PAIR), BF16),
            pltpu.VMEM((pairs, PAIR, padded), BF16),
            pltpu.VMEM((pairs, PAIR, padded), BF16),
            pltpu.VMEM((pairs, blocks, PAIR, QB), F32),
            pltpu.VMEM((pairs, padded, 2 * QB), F32),
            pltpu.VMEM((pairs, PAIR, 2 * QB), F32),
            pltpu.VMEM((pairs, PAIR, 2 * QB), F32),
            pltpu.VMEM((pairs, padded, PAIR), F32),
            pltpu.VMEM((pairs, padded, PAIR), F32),
        ],
        compiler_params=pltpu.CompilerParams(vmem_limit_bytes=48 << 20),
        cost_estimate=pl.CostEstimate(
            flops=12 * rows * rows // 2 * pairs * PAIR,
            bytes_accessed=20 << 20,
            transcendentals=rows * rows * pairs,
        ),
        name="attention",
    )(low, joint, dmix, cosines, sines, start)


def rotary_tables(positions):
    lane = jnp.arange(PAIR, dtype=jnp.int32)
    feature = lane % HEAD_DIM
    inverse = 10000.0 ** (-(2.0 * (feature // 2).astype(F32)) / ROTARY)
    angle = positions.astype(F32)[:, None] * inverse[None, :]
    turned = (feature < ROTARY)[None, :]
    sign = jnp.where(feature % 2 == 0, -1.0, 1.0)[None, :]
    cosines = jnp.where(turned, jnp.cos(angle), 1.0)
    sines = jnp.where(turned, jnp.sin(angle) * sign, 0.0)
    return cosines, sines


def dp_sum(parts, dp_size, x_id, ring_id):
    pair = [(i, i ^ 1) for i in range(dp_size)]
    ring = dp_size // 2
    shift = [(i, (i + 2) % dp_size) for i in range(dp_size)]
    results = []
    for own, other in parts:
        got = lax.ppermute(other, "dp", pair)
        total = own.astype(F32) + got.astype(F32)
        step_rows = total.shape[0] // ring
        shards = total.reshape((ring, step_rows) + total.shape[1:])

        def shard(k):
            return lax.dynamic_index_in_dim(shards, lax.rem(ring_id + 2 * ring - k, ring), 0, False)

        moving = shard(1)
        for k in range(2, ring + 1):
            moving = lax.ppermute(moving.astype(BF16), "dp", shift).astype(F32) + shard(k)
        moving = moving.astype(BF16)
        full = jnp.zeros(shards.shape, BF16)
        full = lax.dynamic_update_index_in_dim(full, moving, ring_id, 0)
        for k in range(1, ring):
            moving = lax.ppermute(moving, "dp", shift)
            full = lax.dynamic_update_index_in_dim(
                full, moving, lax.rem(ring_id + 2 * ring - k, ring), 0
            )
        full = full.reshape(total.shape)
        far = lax.ppermute(full, "dp", pair)
        results.append((jnp.where(x_id == 0, full, far), jnp.where(x_id == 0, far, full)))
    return results


def shards(
    dp_size,
    inputs,
    cotangent,
    seg_ids,
    pad_mask,
    positions,
    ln_gain,
    ln_bias,
    w_qkv,
    w_attn_out,
    w_up,
    b_up,
    w_down,
    b_down,
):
    b = lax.axis_index("branch")
    t = lax.axis_index("tensor")
    dp = lax.axis_index("dp")
    x_id, ring_id = lax.rem(dp, 2), dp // 2
    rows, quarter = inputs.shape
    half = 2 * quarter
    full = 4 * quarter
    heads_w = w_qkv.shape[2] // 2
    units = w_up.shape[1] // 2

    def gathered(own):
        got = lax.ppermute(own, "tensor", SWAP)
        near = jnp.where(
            t == 0, jnp.concatenate([own, got], 1), jnp.concatenate([got, own], 1)
        )
        far = lax.ppermute(near, "branch", SWAP)
        return jnp.concatenate([near, far], 1), got

    def part(w, axis, index, size):
        return lax.dynamic_slice_in_dim(w, index * size, size, axis)

    aux = jnp.concatenate([ln_gain[None], ln_bias[None], jnp.zeros((14, quarter), BF16)], 0)
    x_all, x_got = gathered(jnp.concatenate([inputs, aux], 0))
    g_own, _ = lax.optimization_barrier((cotangent, x_got))
    g_all, _ = gathered(g_own)

    def first_weights(index):
        return jnp.concatenate(
            [
                part(w_qkv, 2, index, heads_w).reshape(half, 3 * heads_w),
                part(w_up, 1, index, units),
            ],
            1,
        )

    def second_weights(index):
        return jnp.concatenate(
            [part(w_attn_out, 0, index, heads_w), part(w_down, 0, index, units)], 0
        )

    w_in = jnp.concatenate(
        [first_weights(b), lax.ppermute(first_weights(1 - b), "branch", SWAP)], 0
    )
    w_out = jnp.concatenate(
        [second_weights(b), lax.ppermute(second_weights(1 - b), "branch", SWAP)], 1
    )
    w_q, w_u = w_in[:, : 3 * heads_w], w_in[:, 3 * heads_w :]
    w_a, w_d = w_out[:heads_w], w_out[heads_w:]
    bias_up = part(b_up, 0, b, units).astype(F32)
    cosines, sines = rotary_tables(positions)

    x_float = x_all[:rows].astype(F32)
    gain = x_all[rows].astype(F32)
    shift = x_all[rows + 1].astype(F32)
    mean = jnp.mean(x_float, axis=1, keepdims=True)
    center = x_float - mean
    inv_root = lax.rsqrt(jnp.mean(center * center, axis=1, keepdims=True) + EPS)
    unit = center * inv_root
    normed = (unit * gain + shift).astype(BF16)

    hidden = nn(normed, w_u) + bias_up
    bend = jnp.tanh(GELU_A * (hidden + GELU_B * hidden * hidden * hidden))
    active = (0.5 * hidden * (1.0 + bend)).astype(BF16)
    slope = 0.5 * (1.0 + bend) + 0.5 * hidden * (1.0 - bend * bend) * GELU_A * (
        1.0 + 3.0 * GELU_B * hidden * hidden
    )
    joint = nn(normed, w_q)
    d_hidden = (nt(g_all, w_d) * slope).astype(BF16)
    g_down = tn(active, g_all).astype(BF16)
    g_up = tn(normed, d_hidden).astype(BF16)
    down_far = lax.ppermute(g_down[:, half:], "branch", SWAP)
    up_far = lax.ppermute(g_up[half:], "branch", SWAP)

    same = b == x_id

    def split(mine, theirs):
        return jnp.where(same, mine, theirs), jnp.where(same, theirs, mine)

    (down_sum, up_sum) = dp_sum(
        [split(g_down[:, :half], down_far), split(g_up[:half], up_far)], dp_size, x_id, ring_id
    )

    d_mixed = nt(g_all, w_a).astype(BF16)
    mixed, d_joint = attention(joint, d_mixed, cosines, sines, positions)

    g_qkv = tn(normed, d_joint)
    g_attn = tn(g_all, mixed)
    g_late = jnp.concatenate([g_qkv, g_attn], 1).astype(BF16)
    late_far = lax.ppermute(g_late[half:], "branch", SWAP)
    (late_sum,) = dp_sum([split(g_late[:half], late_far)], dp_size, x_id, ring_id)

    d_normed = nt(d_joint, w_q) + nt(d_hidden, w_u)
    term = nn(mixed, w_a) + nn(active, w_d)

    def scattered(partial):
        near = partial[:, :half] + lax.ppermute(
            partial[:, half:].astype(BF16), "branch", SWAP
        ).astype(F32)
        own = part(near, 1, t, quarter)
        return own + lax.ppermute(part(near, 1, 1 - t, quarter).astype(BF16), "tensor", SWAP).astype(
            F32
        )

    d_unit = d_normed * gain
    sums = jnp.stack([jnp.sum(d_unit, axis=1), jnp.sum(d_unit * unit, axis=1)])
    sums = sums + lax.ppermute(sums, "branch", SWAP)
    sums = sums + lax.ppermute(sums, "tensor", SWAP)
    means = sums * (1.0 / full)

    d_own = scattered(d_normed)
    unit_own = (inputs.astype(F32) - mean) * inv_root
    g_float = cotangent.astype(F32)
    input_grad = g_float + inv_root * (
        d_own * ln_gain.astype(F32) - means[0][:, None] - unit_own * means[1][:, None]
    )
    output = (
        inputs.astype(F32) + scattered(term) + b_down.astype(F32)
    ).astype(BF16)
    small = jnp.concatenate(
        [
            jnp.sum(d_own * unit_own, axis=0),
            jnp.sum(d_own, axis=0),
            jnp.sum(g_float, axis=0),
            jnp.sum(d_hidden.astype(F32), axis=0),
        ]
    )
    small = lax.psum(small, "dp")
    bup = small[3 * quarter :]
    bup_far = lax.ppermute(bup, "branch", SWAP)
    grad_bup = jnp.where(b == 0, jnp.concatenate([bup, bup_far]), jnp.concatenate([bup_far, bup]))

    late0, late1 = late_sum
    qkv_w = 3 * heads_w
    grad_qkv = jnp.concatenate(
        [
            late0[:, :qkv_w].reshape(half, 3, heads_w),
            late1[:, :qkv_w].reshape(half, 3, heads_w),
        ],
        2,
    ).astype(F32)
    grad_aout = jnp.concatenate([late0[:, qkv_w:], late1[:, qkv_w:]], 1).T.astype(F32)
    grad_up = jnp.concatenate(up_sum, 1).astype(F32)
    grad_down = jnp.concatenate(down_sum, 0).astype(F32)
    return (
        output,
        input_grad,
        small[:quarter],
        small[quarter : 2 * quarter],
        grad_qkv,
        grad_aout,
        grad_up,
        grad_bup,
        grad_down,
        small[2 * quarter : 3 * quarter],
    )


def solution(mesh):
    features = ("branch", "tensor")
    in_specs = (
        P("dp", features),
        P("dp", features),
        P("dp"),
        P("dp"),
        P("dp"),
        P(features),
        P(features),
        P("branch", None, "tensor"),
        P("tensor", "branch"),
        P("branch", "tensor"),
        P("tensor"),
        P("tensor", "branch"),
        P(features),
    )
    out_specs = (
        P("dp", features),
        P("dp", features),
        P(features),
        P(features),
        P("branch", None, "tensor"),
        P("tensor", "branch"),
        P("branch", "tensor"),
        P("tensor"),
        P("tensor", "branch"),
        P(features),
    )
    return jax.shard_map(
        functools.partial(shards, mesh.shape["dp"]),
        mesh=mesh,
        in_specs=in_specs,
        out_specs=out_specs,
        check_vma=False,
    )
```

```python
import functools

import jax
import jax.numpy as jnp
from jax import lax
from jax.experimental import pallas as pl
from jax.experimental.pallas import tpu as pltpu
from jax.sharding import PartitionSpec as P

HEAD_DIM = 64
ROTARY = 32
PAIR = 2 * HEAD_DIM
QB = 128
KC = 256
LONGEST = 1024
EPS = 1e-05
NEG = -1e30
F32 = jnp.float32
BF16 = jnp.bfloat16
SWAP = [(0, 1), (1, 0)]
GELU_A = 0.7978845608028654
GELU_B = 0.044715


def nn(a, b):
    return lax.dot_general(a, b, (((1,), (0,)), ((), ())), preferred_element_type=F32)


def nt(a, b):
    return lax.dot_general(a, b, (((1,), (1,)), ((), ())), preferred_element_type=F32)


def tn(a, b):
    return lax.dot_general(a, b, (((0,), (0,)), ((), ())), preferred_element_type=F32)


def partner(x, even):
    width = x.shape[1]
    return jnp.where(even, pltpu.roll(x, width - 1, 1), pltpu.roll(x, 1, 1))


def attention_kernel(
    pairs,
    most,
    span_ref,
    joint_ref,
    dmix_ref,
    cos_ref,
    sin_ref,
    start_ref,
    mixed_ref,
    dj_ref,
    q_s,
    qt_s,
    g_s,
    gt_s,
    k_s,
    v_s,
    kt_s,
    vt_s,
    s_s,
    d_s,
    p_s,
    e_s,
    dk_s,
    dv_s,
):
    rows = joint_ref.shape[0]
    width = pairs * PAIR
    lane = lax.broadcasted_iota(jnp.int32, (QB, PAIR), 1)
    even = lane % 2 == 0
    first = lane < HEAD_DIM
    top = lax.broadcasted_iota(jnp.int32, (PAIR, QB), 0) < HEAD_DIM
    scale = HEAD_DIM**-0.5

    for p in range(pairs):
        k_s[p, :QB, :] = jnp.zeros((QB, PAIR), BF16)
        v_s[p, :QB, :] = jnp.zeros((QB, PAIR), BF16)
        kt_s[p, :, :QB] = jnp.zeros((PAIR, QB), BF16)
        vt_s[p, :, :QB] = jnp.zeros((PAIR, QB), BF16)
        dk_s[p, :QB, :] = jnp.zeros((QB, PAIR), F32)
        dv_s[p, :QB, :] = jnp.zeros((QB, PAIR), F32)

    @pl.loop(0, rows // QB)
    def _(i):
        at = pl.ds(pl.multiple_of(i * QB, QB), QB)
        to = pl.ds(pl.multiple_of(i * QB + QB, QB), QB)
        cosines = cos_ref[at, :]
        sines = sin_ref[at, :]
        for p in range(pairs):
            q = joint_ref[at, p * PAIR : (p + 1) * PAIR]
            k = joint_ref[at, width + p * PAIR : width + (p + 1) * PAIR]
            v = joint_ref[at, 2 * width + p * PAIR : 2 * width + (p + 1) * PAIR]
            g = dmix_ref[at, p * PAIR : (p + 1) * PAIR].astype(F32)
            q = (q * cosines + partner(q, even) * sines) * scale
            k = k * cosines + partner(k, even) * sines
            q_s[p, i, :QB, :] = jnp.where(first, q, 0.0).astype(BF16)
            q_s[p, i, QB:, :] = jnp.where(first, 0.0, q).astype(BF16)
            g_s[p, i, :QB, :] = jnp.where(first, g, 0.0).astype(BF16)
            g_s[p, i, QB:, :] = jnp.where(first, 0.0, g).astype(BF16)
            q, g = q.T, g.T
            qt_s[p, i, :, :QB] = jnp.where(top, q, 0.0).astype(BF16)
            qt_s[p, i, :, QB:] = jnp.where(top, 0.0, q).astype(BF16)
            gt_s[p, i, :, :QB] = jnp.where(top, g, 0.0).astype(BF16)
            gt_s[p, i, :, QB:] = jnp.where(top, 0.0, g).astype(BF16)
            k_s[p, to, :] = k.astype(BF16)
            v_s[p, to, :] = v.astype(BF16)
            kt_s[p, :, to] = k.T.astype(BF16)
            vt_s[p, :, to] = v.T.astype(BF16)
            dk_s[p, to, :] = jnp.zeros((QB, PAIR), F32)
            dv_s[p, to, :] = jnp.zeros((QB, PAIR), F32)

    key_slot = lax.broadcasted_iota(jnp.int32, (KC, 2 * QB), 0)
    query_slot = lax.broadcasted_iota(jnp.int32, (1, 2 * QB), 1) % QB

    def block(i, n):
        base = (i + 2) * QB - n * KC
        spots = [pl.ds(pl.multiple_of(base + j * KC, QB), KC) for j in range(n)]
        whole = pl.ds(pl.multiple_of(base, QB), n * KC)
        query = query_slot + (i * QB + QB - base)
        start = start_ref[i] + (QB - base)
        here = pl.ds(pl.multiple_of(i * QB, QB), QB)
        pr = range(pairs)
        peak = [None] * pairs
        for j in range(n):
            ok = (key_slot >= start - j * KC) & (key_slot <= query - j * KC)
            for p in pr:
                s = jnp.where(ok, nn(k_s[p, spots[j], :], qt_s[p, i]), NEG)
                s_s[p, j] = s
                m = jnp.max(s.reshape(KC // 8, 8, 2 * QB), axis=0)
                peak[p] = m if peak[p] is None else jnp.maximum(peak[p], m)
        for j in range(n):
            for p in pr:
                d_s[p, j] = nn(v_s[p, spots[j], :], gt_s[p, i])
        peak = [jnp.max(m, axis=0, keepdims=True) for m in peak]
        total = [0.0] * pairs
        delta = [0.0] * pairs
        for j in range(n):
            for p in pr:
                e = jnp.exp(s_s[p, j] - peak[p])
                s_s[p, j] = e
                total[p] += jnp.sum(e.reshape(KC // 8, 8, 2 * QB), axis=0)
                delta[p] += jnp.sum((e * d_s[p, j]).reshape(KC // 8, 8, 2 * QB), axis=0)
        inverse = [1.0 / jnp.sum(x, axis=0, keepdims=True) for x in total]
        delta = [jnp.sum(x, axis=0, keepdims=True) * r for x, r in zip(delta, inverse)]
        for j in range(n):
            for p in pr:
                prob = s_s[p, j] * inverse[p]
                p_s[p, j * KC : (j + 1) * KC, :] = prob.astype(BF16)
                e_s[p, j * KC : (j + 1) * KC, :] = (prob * (d_s[p, j] - delta[p])).astype(BF16)
        for p in pr:
            o = nn(vt_s[p, :, whole], p_s[p, : n * KC, :])
            mixed_ref[here, p * PAIR : (p + 1) * PAIR] = (
                jnp.where(top, o[:, :QB], o[:, QB:]).T.astype(BF16)
            )
            dv_s[p, whole, :] += nn(p_s[p, : n * KC, :], g_s[p, i])
            dk_s[p, whole, :] += nn(e_s[p, : n * KC, :], q_s[p, i])
            d = nn(kt_s[p, :, whole], e_s[p, : n * KC, :])
            d = (jnp.where(top, d[:, :QB], d[:, QB:]) * scale).T
            d = d * cos_ref[here, :] - partner(d, even) * sin_ref[here, :]
            dj_ref[here, p * PAIR : (p + 1) * PAIR] = d.astype(BF16)

    @pl.loop(0, rows // QB)
    def _(i):
        for n in range(1, most + 1):
            pl.when(span_ref[i] == n)(functools.partial(block, i, n))

    @pl.loop(0, rows // QB)
    def _(i):
        at = pl.ds(pl.multiple_of(i * QB, QB), QB)
        to = pl.ds(pl.multiple_of(i * QB + QB, QB), QB)
        cosines = cos_ref[at, :]
        sines = sin_ref[at, :]
        for p in range(pairs):
            d = dk_s[p, to, :]
            d = d * cosines - partner(d, even) * sines
            dj_ref[at, width + p * PAIR : width + (p + 1) * PAIR] = d.astype(BF16)
            dj_ref[at, 2 * width + p * PAIR : 2 * width + (p + 1) * PAIR] = dv_s[p, to, :].astype(
                BF16
            )


def attention(joint, dmix, cosines, sines, positions):
    rows = joint.shape[0]
    pairs = dmix.shape[1] // PAIR
    blocks = rows // QB
    padded = rows + QB
    most = LONGEST // KC + 1
    start = (jnp.arange(rows, dtype=jnp.int32) - positions).reshape(blocks, 1, QB)
    span = (jnp.arange(blocks, dtype=jnp.int32) - start[:, 0, 0] // QB + 2) // 2
    start = jnp.concatenate([start, start], axis=2)
    vmem = pl.BlockSpec(memory_space=pltpu.VMEM)
    return pl.pallas_call(
        functools.partial(attention_kernel, pairs, most),
        out_shape=(
            jax.ShapeDtypeStruct((rows, pairs * PAIR), BF16),
            jax.ShapeDtypeStruct((rows, 3 * pairs * PAIR), BF16),
        ),
        in_specs=[pl.BlockSpec(memory_space=pltpu.SMEM)] + [vmem] * 5,
        out_specs=(vmem, vmem),
        scratch_shapes=[
            pltpu.VMEM((pairs, blocks, 2 * QB, PAIR), BF16),
            pltpu.VMEM((pairs, blocks, PAIR, 2 * QB), BF16),
            pltpu.VMEM((pairs, blocks, 2 * QB, PAIR), BF16),
            pltpu.VMEM((pairs, blocks, PAIR, 2 * QB), BF16),
            pltpu.VMEM((pairs, padded, PAIR), BF16),
            pltpu.VMEM((pairs, padded, PAIR), BF16),
            pltpu.VMEM((pairs, PAIR, padded), BF16),
            pltpu.VMEM((pairs, PAIR, padded), BF16),
            pltpu.VMEM((pairs, most, KC, 2 * QB), F32),
            pltpu.VMEM((pairs, most, KC, 2 * QB), F32),
            pltpu.VMEM((pairs, most * KC, 2 * QB), BF16),
            pltpu.VMEM((pairs, most * KC, 2 * QB), BF16),
            pltpu.VMEM((pairs, padded, PAIR), F32),
            pltpu.VMEM((pairs, padded, PAIR), F32),
        ],
        compiler_params=pltpu.CompilerParams(vmem_limit_bytes=48 << 20),
        cost_estimate=pl.CostEstimate(
            flops=12 * rows * rows // 2 * pairs * PAIR,
            bytes_accessed=20 << 20,
            transcendentals=rows * rows * pairs,
        ),
        name="attention",
    )(span, joint, dmix, cosines, sines, start)


def rotary_tables(positions):
    lane = jnp.arange(PAIR, dtype=jnp.int32)
    feature = lane % HEAD_DIM
    inverse = 10000.0 ** (-(2.0 * (feature // 2).astype(F32)) / ROTARY)
    angle = positions.astype(F32)[:, None] * inverse[None, :]
    turned = (feature < ROTARY)[None, :]
    sign = jnp.where(feature % 2 == 0, -1.0, 1.0)[None, :]
    cosines = jnp.where(turned, jnp.cos(angle), 1.0)
    sines = jnp.where(turned, jnp.sin(angle) * sign, 0.0)
    return cosines, sines


def line_sum(value, size, place):
    def hop(v, pairs):
        perm = [(2 * i + x, 2 * j + x) for i, j in pairs for x in range(2)]
        return lax.ppermute(v, "dp", perm)

    def add(v, got):
        return (v.astype(F32) + got.astype(F32)).astype(v.dtype)

    if size == 1:
        return value
    steps = size // 2 - 1
    for k in range(steps):
        value = add(value, hop(value, [(k, k + 1), (size - 1 - k, size - 2 - k)]))
    middle = size // 2
    value = add(value, hop(value, [(middle - 1, middle), (middle, middle - 1)]))
    for k in reversed(range(steps)):
        got = hop(value, [(k + 1, k), (size - 2 - k, size - 1 - k)])
        value = jnp.where((place == k) | (place == size - 1 - k), got, value)
    return value


def dp_sum(mine, far, dp_size, x_id, ring_id):
    pair = [(i, i ^ 1) for i in range(dp_size)]
    low = x_id == 0
    got = lax.ppermute(jnp.where(low, far, mine), "dp", pair)
    total = (jnp.where(low, mine, far).astype(F32) + got.astype(F32)).astype(BF16)
    total = line_sum(total, dp_size // 2, ring_id)
    return total, lax.ppermute(total, "dp", pair)


def place_kernel(emit, count, flag_ref, *refs):
    own, other, outs = refs[:count], refs[count : 2 * count], refs[2 * count :]
    k, s = pl.program_id(0), pl.program_id(1)
    for c in range(count):
        pl.when((s == c) & (k == flag_ref[0]))(functools.partial(emit, own[c], outs))
        pl.when((s == c) & (k != flag_ref[0]))(functools.partial(emit, other[c], outs))


def place(emit, flag, pieces, out_shapes, out_blocks, maps, name):
    count = len(pieces)
    arrays = [p[0] for p in pieces] + [p[1] for p in pieces]
    grid_spec = pltpu.PrefetchScalarGridSpec(
        num_scalar_prefetch=1,
        grid=(2, count),
        in_specs=[pl.BlockSpec(a.shape, lambda k, s, f: (0, 0)) for a in arrays],
        out_specs=[pl.BlockSpec(blk, m) for blk, m in zip(out_blocks, maps)],
    )
    return pl.pallas_call(
        functools.partial(place_kernel, emit, count),
        grid_spec=grid_spec,
        out_shape=[jax.ShapeDtypeStruct(o, F32) for o in out_shapes],
        compiler_params=pltpu.CompilerParams(vmem_limit_bytes=48 << 20),
        cost_estimate=pl.CostEstimate(
            flops=0, bytes_accessed=6 * 2 * count * arrays[0].size, transcendentals=0
        ),
        name=name,
    )(flag.reshape(1).astype(jnp.int32), *arrays)


def emit_plain(src, outs):
    outs[0][...] = src[...].astype(F32)


def emit_late(src, outs):
    width = outs[0].shape[2]
    for j in range(3):
        outs[0][j] = src[:, j * width : (j + 1) * width].astype(F32)
    outs[1][...] = src[:, 3 * width :].astype(F32).T


def shards(
    dp_size,
    inputs,
    cotangent,
    seg_ids,
    pad_mask,
    positions,
    ln_gain,
    ln_bias,
    w_qkv,
    w_attn_out,
    w_up,
    b_up,
    w_down,
    b_down,
):
    b = lax.axis_index("branch")
    t = lax.axis_index("tensor")
    dp = lax.axis_index("dp")
    x_id, ring_id = lax.rem(dp, 2), dp // 2
    rows, quarter = inputs.shape
    half = 2 * quarter
    full = 4 * quarter
    heads_w = w_qkv.shape[2] // 2
    units = w_up.shape[1] // 2
    chunks = 2

    def gathered(own, early):
        got = lax.ppermute(own, "tensor", SWAP)
        far_own = lax.ppermute(early, "branch", SWAP)
        far_got = lax.ppermute(got, "branch", SWAP)
        first = t == 0
        return (
            jnp.concatenate(
                [
                    jnp.where(first, own, got),
                    jnp.where(first, got, own),
                    jnp.where(first, far_own, far_got),
                    jnp.where(first, far_got, far_own),
                ],
                1,
            ),
            got,
        )

    def part(w, axis, index, size):
        return lax.dynamic_slice_in_dim(w, index * size, size, axis)

    aux = jnp.concatenate([ln_gain[None], ln_bias[None], jnp.zeros((14, quarter), BF16)], 0)
    x_all, x_got = gathered(inputs, inputs)
    aux_all, _ = gathered(aux, aux)
    g_own, _ = lax.optimization_barrier((cotangent, x_got))
    g_all, _ = gathered(g_own, cotangent)

    w_three = jnp.transpose(w_qkv, (1, 0, 2))

    def first_weights(index):
        return jnp.concatenate(
            [part(w_three[j], 1, index, heads_w) for j in range(3)] + [part(w_up, 1, index, units)],
            1,
        )

    def second_weights(index):
        return jnp.concatenate(
            [part(w_attn_out, 0, index, heads_w), part(w_down, 0, index, units)], 0
        )

    w_in = jnp.concatenate(
        [first_weights(b), lax.ppermute(first_weights(1 - b), "branch", SWAP)], 0
    )
    w_out = jnp.concatenate(
        [second_weights(b), lax.ppermute(second_weights(1 - b), "branch", SWAP)], 1
    )
    w_q, w_u = w_in[:, : 3 * heads_w], w_in[:, 3 * heads_w :]
    w_a, w_d = w_out[:heads_w], w_out[heads_w:]
    bias_up = part(b_up, 0, b, units).astype(F32)
    cosines, sines = rotary_tables(positions)

    x_float = x_all.astype(F32)
    gain = aux_all[0].astype(F32)
    shift = aux_all[1].astype(F32)
    mean = jnp.mean(x_float, axis=1, keepdims=True)
    center = x_float - mean
    inv_root = lax.rsqrt(jnp.mean(center * center, axis=1, keepdims=True) + EPS)
    unit = center * inv_root
    normed = (unit * gain + shift).astype(BF16)

    hidden = nn(normed, w_u) + bias_up
    bend = jnp.tanh(GELU_A * (hidden + GELU_B * hidden * hidden * hidden))
    active = (0.5 * hidden * (1.0 + bend)).astype(BF16)
    slope = 0.5 * (1.0 + bend) + 0.5 * hidden * (1.0 - bend * bend) * GELU_A * (
        1.0 + 3.0 * GELU_B * hidden * hidden
    )
    joint = nn(normed, w_q)
    g_down = tn(active, g_all).astype(BF16)
    g_all, g_down = lax.optimization_barrier((g_all, g_down))
    d_hidden = (nt(g_all, w_d) * slope).astype(BF16)
    g_up = tn(normed, d_hidden).astype(BF16)
    joint, g_all, g_up = lax.optimization_barrier((joint, g_all, g_up))
    down_far = lax.ppermute(g_down[:, half:], "branch", SWAP)
    up_far = lax.ppermute(g_up[half:], "branch", SWAP)

    def summed(mine, far):
        step = mine.shape[0] // chunks
        return [
            dp_sum(
                mine[c * step : (c + 1) * step],
                far[c * step : (c + 1) * step],
                dp_size,
                x_id,
                ring_id,
            )
            for c in range(chunks)
        ]

    down_sum = summed(g_down[:, :half], down_far)
    up_sum = summed(g_up[:half], up_far)

    d_mixed = nt(g_all, w_a).astype(BF16)
    mixed, d_joint = attention(joint, d_mixed, cosines, sines, positions)

    g_late = jnp.concatenate([tn(normed, d_joint), tn(g_all, mixed)], 1).astype(BF16)
    d_joint, mixed, g_late = lax.optimization_barrier((d_joint, mixed, g_late))
    late_far = lax.ppermute(g_late[half:], "branch", SWAP)
    late_sum = summed(g_late[:half], late_far)

    d_normed = nt(d_joint, w_q) + nt(d_hidden, w_u)
    term = nn(mixed, w_a) + nn(active, w_d)

    def scattered(partial):
        near = partial[:, :half] + lax.ppermute(
            partial[:, half:].astype(BF16), "branch", SWAP
        ).astype(F32)
        own = part(near, 1, t, quarter)
        return own + lax.ppermute(
            part(near, 1, 1 - t, quarter).astype(BF16), "tensor", SWAP
        ).astype(F32)

    d_unit = d_normed * gain
    sums = jnp.stack([jnp.sum(d_unit, axis=1), jnp.sum(d_unit * unit, axis=1)])
    sums = sums + lax.ppermute(sums, "branch", SWAP)
    sums = sums + lax.ppermute(sums, "tensor", SWAP)
    means = sums * (1.0 / full)

    d_own = scattered(d_normed)
    unit_own = (inputs.astype(F32) - mean) * inv_root
    g_float = cotangent.astype(F32)
    input_grad = g_float + inv_root * (
        d_own * ln_gain.astype(F32) - means[0][:, None] - unit_own * means[1][:, None]
    )
    output = (inputs.astype(F32) + scattered(term) + b_down.astype(F32)).astype(BF16)
    small = jnp.concatenate(
        [
            jnp.sum(d_own * unit_own, axis=0)[None],
            jnp.sum(d_own, axis=0)[None],
            jnp.sum(g_float, axis=0)[None],
            jnp.sum(d_hidden.astype(F32), axis=0).reshape(units // quarter, quarter),
        ]
    )
    small = small + lax.ppermute(small, "dp", [(i, i ^ 1) for i in range(dp_size)])
    small = line_sum(small, dp_size // 2, ring_id)
    bup = small[3:].reshape(units)
    bup_far = lax.ppermute(bup, "branch", SWAP)
    grad_bup = jnp.where(b == 0, jnp.concatenate([bup, bup_far]), jnp.concatenate([bup_far, bup]))

    flag = b ^ x_id
    (grad_down,) = place(
        emit_plain,
        flag,
        down_sum,
        [(2 * units, half)],
        [(units // chunks, half)],
        [lambda k, s, f: (k * chunks + s, 0)],
        "place_down",
    )
    (grad_up,) = place(
        emit_plain,
        flag,
        up_sum,
        [(half, 2 * units)],
        [(half // chunks, units)],
        [lambda k, s, f: (s, k)],
        "place_up",
    )
    grad_qkv, grad_aout = place(
        emit_late,
        flag,
        late_sum,
        [(3, half, 2 * heads_w), (2 * heads_w, half)],
        [(3, half // chunks, heads_w), (heads_w, half // chunks)],
        [lambda k, s, f: (0, s, k), lambda k, s, f: (k, s)],
        "place_late",
    )
    return (
        output,
        input_grad,
        small[0],
        small[1],
        jnp.transpose(grad_qkv, (1, 0, 2)),
        grad_aout,
        grad_up,
        grad_bup,
        grad_down,
        small[2],
    )


def solution(mesh):
    features = ("branch", "tensor")
    in_specs = (
        P("dp", features),
        P("dp", features),
        P("dp"),
        P("dp"),
        P("dp"),
        P(features),
        P(features),
        P("branch", None, "tensor"),
        P("tensor", "branch"),
        P("branch", "tensor"),
        P("tensor"),
        P("tensor", "branch"),
        P(features),
    )
    out_specs = (
        P("dp", features),
        P("dp", features),
        P(features),
        P(features),
        P("branch", None, "tensor"),
        P("tensor", "branch"),
        P("branch", "tensor"),
        P("tensor"),
        P("tensor", "branch"),
        P(features),
    )
    return jax.shard_map(
        functools.partial(shards, mesh.shape["dp"]),
        mesh=mesh,
        in_specs=in_specs,
        out_specs=out_specs,
        check_vma=False,
    )
```

```python
import functools

import jax
import jax.numpy as jnp
from jax import lax
from jax.experimental import pallas as pl
from jax.experimental.pallas import tpu as pltpu
from jax.sharding import PartitionSpec as P

HEAD_DIM = 64
ROTARY = 32
PAIR = 2 * HEAD_DIM
QB = 128
KC = 256
LONGEST = 1024
EPS = 1e-05
NEG = -1e30
F32 = jnp.float32
BF16 = jnp.bfloat16
SWAP = [(0, 1), (1, 0)]
GELU_A = 0.7978845608028654
GELU_B = 0.044715


def nn(a, b):
    return lax.dot_general(a, b, (((1,), (0,)), ((), ())), preferred_element_type=F32)


def nt(a, b):
    return lax.dot_general(a, b, (((1,), (1,)), ((), ())), preferred_element_type=F32)


def tn(a, b):
    return lax.dot_general(a, b, (((0,), (0,)), ((), ())), preferred_element_type=F32)


def partner(x, even):
    width = x.shape[1]
    return jnp.where(even, pltpu.roll(x, width - 1, 1), pltpu.roll(x, 1, 1))


def attention_kernel(
    pairs,
    most,
    span_ref,
    qkv_ref,
    dmix_ref,
    cos_ref,
    sin_ref,
    start_ref,
    mixed_ref,
    dj_ref,
    q_s,
    qt_s,
    g_s,
    gt_s,
    k_s,
    v_s,
    kt_s,
    vt_s,
    s_s,
    d_s,
    p_s,
    e_s,
    dk_s,
    dv_s,
):
    rows = qkv_ref.shape[0]
    width = pairs * PAIR
    lane = lax.broadcasted_iota(jnp.int32, (QB, PAIR), 1)
    even = lane % 2 == 0
    first = lane < HEAD_DIM
    top = lax.broadcasted_iota(jnp.int32, (PAIR, QB), 0) < HEAD_DIM
    scale = HEAD_DIM**-0.5

    for p in range(pairs):
        k_s[p, :QB, :] = jnp.zeros((QB, PAIR), BF16)
        v_s[p, :QB, :] = jnp.zeros((QB, PAIR), BF16)
        kt_s[p, :, :QB] = jnp.zeros((PAIR, QB), BF16)
        vt_s[p, :, :QB] = jnp.zeros((PAIR, QB), BF16)
        dk_s[p, :QB, :] = jnp.zeros((QB, PAIR), F32)
        dv_s[p, :QB, :] = jnp.zeros((QB, PAIR), F32)

    @pl.loop(0, rows // QB)
    def _(i):
        at = pl.ds(pl.multiple_of(i * QB, QB), QB)
        to = pl.ds(pl.multiple_of(i * QB + QB, QB), QB)
        for p in range(pairs):
            q = qkv_ref[at, p * PAIR : (p + 1) * PAIR].astype(F32)
            k = qkv_ref[at, width + p * PAIR : width + (p + 1) * PAIR]
            v = qkv_ref[at, 2 * width + p * PAIR : 2 * width + (p + 1) * PAIR]
            g = dmix_ref[at, p * PAIR : (p + 1) * PAIR].astype(F32)
            q_s[p, i, :QB, :] = jnp.where(first, q, 0.0).astype(BF16)
            q_s[p, i, QB:, :] = jnp.where(first, 0.0, q).astype(BF16)
            g_s[p, i, :QB, :] = jnp.where(first, g, 0.0).astype(BF16)
            g_s[p, i, QB:, :] = jnp.where(first, 0.0, g).astype(BF16)
            q, g = q.T, g.T
            qt_s[p, i, :, :QB] = jnp.where(top, q, 0.0).astype(BF16)
            qt_s[p, i, :, QB:] = jnp.where(top, 0.0, q).astype(BF16)
            gt_s[p, i, :, :QB] = jnp.where(top, g, 0.0).astype(BF16)
            gt_s[p, i, :, QB:] = jnp.where(top, 0.0, g).astype(BF16)
            k_s[p, to, :] = k
            v_s[p, to, :] = v
            kt_s[p, :, to] = k.astype(F32).T.astype(BF16)
            vt_s[p, :, to] = v.astype(F32).T.astype(BF16)
            dk_s[p, to, :] = jnp.zeros((QB, PAIR), F32)
            dv_s[p, to, :] = jnp.zeros((QB, PAIR), F32)

    key_slot = lax.broadcasted_iota(jnp.int32, (KC, 2 * QB), 0)
    query_slot = lax.broadcasted_iota(jnp.int32, (1, 2 * QB), 1) % QB

    def block(i, n):
        base = (i + 2) * QB - n * KC
        spots = [pl.ds(pl.multiple_of(base + j * KC, QB), KC) for j in range(n)]
        whole = pl.ds(pl.multiple_of(base, QB), n * KC)
        query = query_slot + (i * QB + QB - base)
        start = start_ref[i] + (QB - base)
        here = pl.ds(pl.multiple_of(i * QB, QB), QB)
        pr = range(pairs)
        peak = [None] * pairs
        for j in range(n):
            ok = (key_slot >= start - j * KC) & (key_slot <= query - j * KC)
            for p in pr:
                s = jnp.where(ok, nn(k_s[p, spots[j], :], qt_s[p, i]), NEG)
                s_s[p, j] = s
                m = jnp.max(s.reshape(KC // 8, 8, 2 * QB), axis=0)
                peak[p] = m if peak[p] is None else jnp.maximum(peak[p], m)
        for j in range(n):
            for p in pr:
                d_s[p, j] = nn(v_s[p, spots[j], :], gt_s[p, i])
        peak = [jnp.max(m, axis=0, keepdims=True) for m in peak]
        total = [0.0] * pairs
        delta = [0.0] * pairs
        for j in range(n):
            for p in pr:
                e = jnp.exp(s_s[p, j] - peak[p])
                s_s[p, j] = e
                total[p] += jnp.sum(e.reshape(KC // 8, 8, 2 * QB), axis=0)
                delta[p] += jnp.sum((e * d_s[p, j]).reshape(KC // 8, 8, 2 * QB), axis=0)
        inverse = [1.0 / jnp.sum(x, axis=0, keepdims=True) for x in total]
        delta = [jnp.sum(x, axis=0, keepdims=True) * r for x, r in zip(delta, inverse)]
        for j in range(n):
            for p in pr:
                prob = s_s[p, j] * inverse[p]
                p_s[p, j * KC : (j + 1) * KC, :] = prob.astype(BF16)
                e_s[p, j * KC : (j + 1) * KC, :] = (prob * (d_s[p, j] - delta[p])).astype(BF16)
        for p in pr:
            o = nn(vt_s[p, :, whole], p_s[p, : n * KC, :])
            mixed_ref[here, p * PAIR : (p + 1) * PAIR] = (
                jnp.where(top, o[:, :QB], o[:, QB:]).T.astype(BF16)
            )
            dv_s[p, whole, :] += nn(p_s[p, : n * KC, :], g_s[p, i])
            dk_s[p, whole, :] += nn(e_s[p, : n * KC, :], q_s[p, i])
            d = nn(kt_s[p, :, whole], e_s[p, : n * KC, :])
            d = (jnp.where(top, d[:, :QB], d[:, QB:]) * scale).T
            d = d * cos_ref[here, :] - partner(d, even) * sin_ref[here, :]
            dj_ref[here, p * PAIR : (p + 1) * PAIR] = d.astype(BF16)

    @pl.loop(0, rows // QB)
    def _(i):
        for n in range(1, most + 1):
            pl.when(span_ref[i] == n)(functools.partial(block, i, n))

    @pl.loop(0, rows // QB)
    def _(i):
        at = pl.ds(pl.multiple_of(i * QB, QB), QB)
        to = pl.ds(pl.multiple_of(i * QB + QB, QB), QB)
        cosines = cos_ref[at, :]
        sines = sin_ref[at, :]
        for p in range(pairs):
            d = dk_s[p, to, :]
            d = d * cosines - partner(d, even) * sines
            dj_ref[at, width + p * PAIR : width + (p + 1) * PAIR] = d.astype(BF16)
            dj_ref[at, 2 * width + p * PAIR : 2 * width + (p + 1) * PAIR] = dv_s[p, to, :].astype(
                BF16
            )


def attention(qkv, dmix, cosines, sines, positions, pair):
    rows = qkv.shape[0]
    pairs = 1
    blocks = rows // QB
    padded = rows + QB
    most = LONGEST // KC + 1
    start = (jnp.arange(rows, dtype=jnp.int32) - positions).reshape(blocks, 1, QB)
    span = (jnp.arange(blocks, dtype=jnp.int32) - start[:, 0, 0] // QB + 2) // 2
    start = jnp.concatenate([start, start], axis=2)
    vmem = pl.BlockSpec(memory_space=pltpu.VMEM)
    return pl.pallas_call(
        functools.partial(attention_kernel, pairs, most),
        grid=(1,),
        out_shape=(
            jax.ShapeDtypeStruct((rows, pairs * PAIR), BF16),
            jax.ShapeDtypeStruct((rows, 3 * pairs * PAIR), BF16),
        ),
        in_specs=[
            pl.BlockSpec(memory_space=pltpu.SMEM),
            pl.BlockSpec((rows, 3 * pairs * PAIR), lambda i: (0, pair)),
            pl.BlockSpec((rows, pairs * PAIR), lambda i: (0, pair)),
            vmem,
            vmem,
            vmem,
        ],
        out_specs=(
            pl.BlockSpec((rows, pairs * PAIR), lambda i: (0, 0)),
            pl.BlockSpec((rows, 3 * pairs * PAIR), lambda i: (0, 0)),
        ),
        scratch_shapes=[
            pltpu.VMEM((pairs, blocks, 2 * QB, PAIR), BF16),
            pltpu.VMEM((pairs, blocks, PAIR, 2 * QB), BF16),
            pltpu.VMEM((pairs, blocks, 2 * QB, PAIR), BF16),
            pltpu.VMEM((pairs, blocks, PAIR, 2 * QB), BF16),
            pltpu.VMEM((pairs, padded, PAIR), BF16),
            pltpu.VMEM((pairs, padded, PAIR), BF16),
            pltpu.VMEM((pairs, PAIR, padded), BF16),
            pltpu.VMEM((pairs, PAIR, padded), BF16),
            pltpu.VMEM((pairs, most, KC, 2 * QB), F32),
            pltpu.VMEM((pairs, most, KC, 2 * QB), F32),
            pltpu.VMEM((pairs, most * KC, 2 * QB), BF16),
            pltpu.VMEM((pairs, most * KC, 2 * QB), BF16),
            pltpu.VMEM((pairs, padded, PAIR), F32),
            pltpu.VMEM((pairs, padded, PAIR), F32),
        ],
        compiler_params=pltpu.CompilerParams(vmem_limit_bytes=40 << 20),
        cost_estimate=pl.CostEstimate(
            flops=0, bytes_accessed=0, transcendentals=0
        ),
        name="attention",
    )(span, qkv, dmix, cosines, sines, start)


def picked(first, own, got, far_own, far_got):
    own, got, far_own, far_got = (v[...].astype(F32) for v in (own, got, far_own, far_got))
    return jnp.concatenate(
        [
            jnp.where(first, own, got),
            jnp.where(first, got, own),
            jnp.where(first, far_own, far_got),
            jnp.where(first, far_got, far_own),
        ],
        1,
    )


def resident(shape):
    return pl.BlockSpec(shape, lambda i: (0,) * len(shape), pipeline_mode=pl.Buffered(1))


def enter_kernel(
    ids,
    own,
    got,
    far_own,
    far_got,
    aux_ref,
    near_q,
    far_q,
    near_u,
    far_u,
    near_d,
    far_d,
    bias_ref,
    cos_ref,
    sin_ref,
    normed_ref,
    active_ref,
    slope_ref,
    qkv_ref,
    term_ref,
    stat_ref,
):
    x = picked(ids[0] == 0, own, got, far_own, far_got)
    rows, full = x.shape
    half = full // 2
    mean = jnp.mean(x, axis=1, keepdims=True)
    center = x - mean
    inv_root = lax.rsqrt(jnp.mean(center * center, axis=1, keepdims=True) + EPS)
    normed = (
        center * inv_root * aux_ref[0:1, :].astype(F32) + aux_ref[1:2, :].astype(F32)
    ).astype(BF16)
    normed_ref[...] = normed
    lane = lax.broadcasted_iota(jnp.int32, (rows, PAIR), 1)
    stat_ref[...] = jnp.where(lane == 0, mean, inv_root)
    near, far = normed[:, :half], normed[:, half:]
    hidden = nn(near, near_u[...]) + nn(far, far_u[...]) + bias_ref[0:1, :].astype(F32)
    square = hidden * hidden
    bend = jnp.tanh(GELU_A * hidden * (1.0 + GELU_B * square))
    up = 0.5 * (1.0 + bend)
    active = (hidden * up).astype(BF16)
    active_ref[...] = active
    slope_ref[...] = up + (0.5 * GELU_A) * hidden * (1.0 - bend * bend) * (
        1.0 + 3.0 * GELU_B * square
    )
    even = lane % 2 == 0
    cosines, sines = cos_ref[...], sin_ref[...]
    for j in range(3):
        joint = nn(near, near_q[j]) + nn(far, far_q[j])
        for p in range(joint.shape[1] // PAIR):
            v = joint[:, p * PAIR : (p + 1) * PAIR]
            if j < 2:
                v = v * cosines + partner(v, even) * sines
            if j == 0:
                v = v * HEAD_DIM**-0.5
            at = (3 * p + j) * PAIR
            qkv_ref[:, at : at + PAIR] = v.astype(BF16)
    term_ref[:, :half] = nn(active, near_d[...])
    term_ref[:, half:] = nn(active, far_d[...])


def rows_of(step, width):
    return pl.BlockSpec((step, width), lambda i, ids: (i, 0))


def fixed(shape, index=None):
    if index is None:
        return pl.BlockSpec(
            shape, lambda i, ids: (0,) * len(shape), pipeline_mode=pl.Buffered(1)
        )
    return pl.BlockSpec(shape, lambda i, ids: index(ids), pipeline_mode=pl.Buffered(1))


def by_rows(kernel, steps, ids, ins, outs, name, flops, scratch=()):
    return pl.pallas_call(
        kernel,
        grid_spec=pltpu.PrefetchScalarGridSpec(
            num_scalar_prefetch=1,
            grid=(steps,),
            in_specs=[s for _, s in ins],
            out_specs=[s for _, _, s in outs],
            scratch_shapes=scratch,
        ),
        out_shape=[jax.ShapeDtypeStruct(s, d) for s, d, _ in outs],
        compiler_params=pltpu.CompilerParams(vmem_limit_bytes=50 << 20),
        cost_estimate=pl.CostEstimate(flops=0, bytes_accessed=0, transcendentals=0),
        name=name,
    )(ids, *[a for a, _ in ins])


def enter(ids, pieces, aux, w_three, far_q, w_up, far_u, w_down, far_d, bias, cosines, sines):
    rows, quarter = pieces[0].shape
    full, half = 4 * quarter, 2 * quarter
    units, heads_w = far_u.shape[1], far_q.shape[2]
    step = rows // 8
    ins = [(v, rows_of(step, quarter)) for v in pieces] + [
        (aux, fixed(aux.shape)),
        (w_three, fixed((3, half, heads_w), lambda ids: (0, 0, ids[1]))),
        (far_q, fixed(far_q.shape)),
        (w_up, fixed((half, units), lambda ids: (0, ids[1]))),
        (far_u, fixed(far_u.shape)),
        (w_down, fixed((units, half), lambda ids: (ids[1], 0))),
        (far_d, fixed(far_d.shape)),
        (bias, fixed((1, units), lambda ids: (0, ids[1]))),
        (cosines, rows_of(step, PAIR)),
        (sines, rows_of(step, PAIR)),
    ]
    outs = [
        ((rows, full), BF16, rows_of(step, full)),
        ((rows, units), BF16, rows_of(step, units)),
        ((rows, units), F32, rows_of(step, units)),
        ((rows, 3 * heads_w), BF16, rows_of(step, 3 * heads_w)),
        ((rows, full), F32, rows_of(step, full)),
        ((rows, PAIR), F32, rows_of(step, PAIR)),
    ]
    return by_rows(
        enter_kernel, 8, ids, ins, outs, "enter", 2 * rows * full * (3 * heads_w + 2 * units)
    )


def down_kernel(
    ids,
    own,
    got,
    far_own,
    far_got,
    active_ref,
    near_a,
    far_a,
    g_ref,
    dm_ref,
    near_ref,
    far_ref,
    total_s,
):
    i = pl.program_id(0)
    g = picked(ids[0] == 0, own, got, far_own, far_got).astype(BF16)
    half = g.shape[1] // 2
    g_ref[...] = g
    dm_ref[...] = (nt(g[:, :half], near_a[...]) + nt(g[:, half:], far_a[...])).astype(BF16)

    @pl.when(i == 0)
    def _():
        total_s[...] = tn(active_ref[...], g)

    @pl.when(i > 0)
    def _():
        total_s[...] += tn(active_ref[...], g)

    @pl.when(i == pl.num_programs(0) - 1)
    def _():
        near_ref[...] = total_s[:, :half].astype(BF16)
        far_ref[...] = total_s[:, half:].astype(BF16)


def down_grads(ids, pieces, active, w_attn_out, far_a):
    rows, quarter = pieces[0].shape
    full, half, units = 4 * quarter, 2 * quarter, active.shape[1]
    heads_w = far_a.shape[0]
    step = rows // 4
    ins = [(v, rows_of(step, quarter)) for v in pieces] + [
        (active, rows_of(step, units)),
        (w_attn_out, fixed((heads_w, half), lambda ids: (ids[1], 0))),
        (far_a, fixed(far_a.shape)),
    ]
    outs = [
        ((rows, full), BF16, rows_of(step, full)),
        ((rows, heads_w), BF16, rows_of(step, heads_w)),
        ((units, half), BF16, fixed((units, half))),
        ((units, half), BF16, fixed((units, half))),
    ]
    return by_rows(
        down_kernel,
        4,
        ids,
        ins,
        outs,
        "down_grads",
        2 * rows * full * (units + heads_w),
        [pltpu.VMEM((units, full), F32)],
    )


def up_kernel(
    ids,
    g_ref,
    normed_ref,
    slope_ref,
    near_d,
    far_d,
    dh_ref,
    near_ref,
    far_ref,
    sum_ref,
    total_s,
):
    i = pl.program_id(0)
    half = g_ref.shape[1] // 2
    da = nt(g_ref[:, :half], near_d[...]) + nt(g_ref[:, half:], far_d[...])
    dh = (da * slope_ref[...]).astype(BF16)
    dh_ref[...] = dh
    sums = jnp.sum(dh.astype(F32), axis=0, keepdims=True)

    @pl.when(i == 0)
    def _():
        total_s[...] = tn(normed_ref[...], dh)
        sum_ref[...] = sums

    @pl.when(i > 0)
    def _():
        total_s[...] += tn(normed_ref[...], dh)
        sum_ref[...] += sums

    @pl.when(i == pl.num_programs(0) - 1)
    def _():
        near_ref[...] = total_s[:half, :].astype(BF16)
        far_ref[...] = total_s[half:, :].astype(BF16)


def up_grads(ids, g_all, normed, slope, w_down, far_d):
    rows, full = g_all.shape
    half, units = full // 2, slope.shape[1]
    step = rows // 4
    ins = [
        (g_all, rows_of(step, full)),
        (normed, rows_of(step, full)),
        (slope, rows_of(step, units)),
        (w_down, fixed((units, half), lambda ids: (ids[1], 0))),
        (far_d, fixed(far_d.shape)),
    ]
    outs = [
        ((rows, units), BF16, rows_of(step, units)),
        ((half, units), BF16, fixed((half, units))),
        ((half, units), BF16, fixed((half, units))),
        ((1, units), F32, fixed((1, units))),
    ]
    return by_rows(
        up_kernel,
        4,
        ids,
        ins,
        outs,
        "up_grads",
        4 * rows * full * units,
        [pltpu.VMEM((full, units), F32)],
    )


def late_kernel(ids, normed_ref, g_ref, dj_ref, mixed_ref, near_ref, far_ref):
    width = dj_ref.shape[1]

    def grads(out):
        out[:, :width] = tn(normed_ref[...], dj_ref[...]).astype(BF16)
        out[:, width:] = tn(g_ref[...], mixed_ref[...]).astype(BF16)

    pl.when(pl.program_id(0) == 0)(lambda: grads(far_ref))
    pl.when(pl.program_id(0) == 1)(lambda: grads(near_ref))


def late_grads(ids, normed, g_all, d_joint, mixed):
    rows, full = normed.shape
    half, width = full // 2, d_joint.shape[1] + mixed.shape[1]
    cols = pl.BlockSpec((rows, half), lambda i, ids: (0, 1 - i))
    ins = [
        (normed, cols),
        (g_all, cols),
        (d_joint, fixed(d_joint.shape)),
        (mixed, fixed(mixed.shape)),
    ]
    outs = [((half, width), BF16, fixed((half, width)))] * 2
    return by_rows(late_kernel, 2, ids, ins, outs, "late_grads", 2 * rows * full * width)


def leave_kernel(
    ids,
    own,
    got,
    far_own,
    far_got,
    stat_ref,
    aux_ref,
    dj0_ref,
    dj1_ref,
    dh_ref,
    near_q,
    far_q,
    near_u,
    far_u,
    mixed0_ref,
    mixed1_ref,
    near_a,
    far_a,
    term_ref,
    near_ref,
    far_ref,
    row_ref,
    sum_ref,
    term_near,
    term_far,
):
    i = pl.program_id(0)
    half = near_ref.shape[1]
    mixed = jnp.concatenate([mixed0_ref[...], mixed1_ref[...]], 1)
    term_near[...] = term_ref[:, :half] + nn(mixed, near_a[...])
    term_far[...] = (term_ref[:, half:] + nn(mixed, far_a[...])).astype(BF16)
    x = picked(ids[0] == 0, own, got, far_own, far_got)
    unit = (x - stat_ref[:, 0:1]) * stat_ref[:, 1:2]
    dh = dh_ref[...]
    near = nt(dh, near_u[...])
    far = nt(dh, far_u[...])
    for j in range(3):
        cut = slice(j * PAIR, (j + 1) * PAIR)
        dj = jnp.concatenate([dj0_ref[:, cut], dj1_ref[:, cut]], 1)
        near += nt(dj, near_q[j])
        far += nt(dj, far_q[j])
    near_ref[...] = near
    far_ref[...] = far.astype(BF16)
    both = jnp.concatenate([near, far], 1)
    scaled = both * aux_ref[0:1, :].astype(F32)
    first = jnp.sum(scaled, axis=1, keepdims=True)
    second = jnp.sum(scaled * unit, axis=1, keepdims=True)
    lane = lax.broadcasted_iota(jnp.int32, (x.shape[0], PAIR), 1)
    row_ref[0] = jnp.where(lane == 0, first, second).T[:8]
    sums = jnp.concatenate(
        [
            jnp.sum(both * unit, axis=0, keepdims=True),
            jnp.sum(both, axis=0, keepdims=True),
        ],
        0,
    )

    @pl.when(i == 0)
    def _():
        sum_ref[...] = sums

    @pl.when(i > 0)
    def _():
        sum_ref[...] += sums


def leave(
    ids,
    pieces,
    stat,
    aux,
    d_joints,
    d_hidden,
    w_three,
    far_q,
    w_up,
    far_u,
    mixed,
    w_attn_out,
    far_a,
    term,
):
    rows, quarter = pieces[0].shape
    full, half = 4 * quarter, 2 * quarter
    units, heads_w = far_u.shape[1], far_q.shape[2]
    step = rows // 4
    ins = (
        [(v, rows_of(step, quarter)) for v in pieces]
        + [(stat, rows_of(step, PAIR)), (aux, fixed(aux.shape))]
        + [(d, rows_of(step, 3 * PAIR)) for d in d_joints]
        + [
            (d_hidden, rows_of(step, units)),
            (w_three, fixed((3, half, heads_w), lambda ids: (0, 0, ids[1]))),
            (far_q, fixed(far_q.shape)),
            (w_up, fixed((half, units), lambda ids: (0, ids[1]))),
            (far_u, fixed(far_u.shape)),
        ]
        + [(m, rows_of(step, PAIR)) for m in mixed]
        + [
            (w_attn_out, fixed((heads_w, half), lambda ids: (ids[1], 0))),
            (far_a, fixed(far_a.shape)),
            (term, rows_of(step, full)),
        ]
    )
    outs = [
        ((rows, half), F32, rows_of(step, half)),
        ((rows, half), BF16, rows_of(step, half)),
        ((4, 8, step), F32, pl.BlockSpec((1, 8, step), lambda i, ids: (i, 0, 0))),
        ((2, full), F32, fixed((2, full))),
        ((rows, half), F32, rows_of(step, half)),
        ((rows, half), BF16, rows_of(step, half)),
    ]
    return by_rows(
        leave_kernel, 4, ids, ins, outs, "leave", 2 * rows * full * (3 * heads_w + units)
    )


def rotary_tables(positions):
    lane = jnp.arange(PAIR, dtype=jnp.int32)
    feature = lane % HEAD_DIM
    inverse = 10000.0 ** (-(2.0 * (feature // 2).astype(F32)) / ROTARY)
    angle = positions.astype(F32)[:, None] * inverse[None, :]
    turned = (feature < ROTARY)[None, :]
    sign = jnp.where(feature % 2 == 0, -1.0, 1.0)[None, :]
    cosines = jnp.where(turned, jnp.cos(angle), 1.0)
    sines = jnp.where(turned, jnp.sin(angle) * sign, 0.0)
    return cosines, sines


class Chain:
    def __init__(self, value, far, size, x_id, place):
        self.low, self.place = x_id == 0, place
        self.value, self.far, self.keep = jnp.where(self.low, far, value), far, value
        self.moving = self.other = self.crossed = None
        line = size // 2
        steps = line // 2 - 1

        def perm(pairs):
            return [(2 * i + x, 2 * j + x) for i, j in pairs for x in range(2)]

        self.pair = [(i, i ^ 1) for i in range(size)]
        self.hops = [(self.pair, None)]
        if line > 1:
            for k in range(steps):
                self.hops.append((perm([(k, k + 1), (line - 1 - k, line - 2 - k)]), None))
            mid = line // 2
            self.hops.append((perm([(mid - 1, mid), (mid, mid - 1)]), None))
            for k in reversed(range(steps)):
                self.hops.append((perm([(k + 1, k), (line - 2 - k, line - 1 - k)]), (k, line - 1 - k)))
        self.hops.append((self.pair, None))
        self.stage = 0
        self.cross = [
            (2 * i + c, 2 * (i ^ 1) + (c if i % 2 else 1 - c)) for i in range(size) for c in range(2)
        ]
        self.trade = [(2 * i + c, 2 * i + 1 - c) for i in range(1, size, 2) for c in range(2)]

    def busy(self):
        return self.stage < len(self.hops)

    def start(self):
        if self.stage == 0:
            self.moving = lax.ppermute(self.value, ("dp", "branch"), self.cross)
            self.crossed = lax.ppermute(self.far, ("dp", "branch"), self.trade)
        else:
            self.moving = lax.ppermute(self.value, "dp", self.hops[self.stage][0])

    def finish(self):
        got, self.moving = self.moving, None
        ends = self.hops[self.stage][1]
        if self.stage == len(self.hops) - 1:
            self.other = got
        elif ends is None:
            base = self.value
            if self.stage == 0:
                base = jnp.where(self.low, self.keep, self.crossed)
            self.value = (base.astype(F32) + got.astype(F32)).astype(base.dtype)
        else:
            here = (self.place == ends[0]) | (self.place == ends[1])
            self.value = jnp.where(here, got, self.value)
        self.stage += 1

    def pieces(self):
        return (self.value, self.other)


class Scatter:
    hops = (0, 1)

    def __init__(self, near, far, t):
        self.near, self.value, self.low = near, far, t == 0
        self.moving = self.far = None
        self.stage = 0

    def busy(self):
        return self.stage < 2

    def start(self):
        self.moving = lax.ppermute(self.value, ("branch", "tensor")[self.stage], SWAP)

    def finish(self):
        got, self.moving = self.moving, None
        if self.stage == 0:
            total = self.near + got.astype(F32)
            low, high = jnp.split(total, 2, axis=1)
            self.value = jnp.where(self.low, high, low).astype(BF16)
            self.near = jnp.where(self.low, low, high)
        else:
            self.near = self.near + got.astype(F32)
        self.stage += 1


class Doubling:
    def __init__(self, value, size):
        self.value, self.far, self.moving = value, None, None
        self.hops = [1 << k for k in range(size.bit_length() - 1)]
        self.size, self.stage = size, 0

    def busy(self):
        return self.stage < len(self.hops)

    def start(self):
        away = self.hops[self.stage]
        self.moving = lax.ppermute(self.value, "dp", [(i, i ^ away) for i in range(self.size)])

    def finish(self):
        self.value = self.value + self.moving
        self.moving = None
        self.stage += 1


class Steps:
    def __init__(self):
        self.before = []

    def run(self, finish, start, compute=None, *operands):
        for c in finish:
            c.finish()
        touched = list({id(c): c for c in [*finish, *start]}.values())
        values, fars, operands, _ = lax.optimization_barrier(
            (
                [c.value for c in touched],
                [c.far for c in start if c.far is not None],
                operands,
                self.before,
            )
        )
        for c, v in zip(touched, values):
            c.value = v
        for c, v in zip([c for c in start if c.far is not None], fars):
            c.far = v
        for c in start:
            c.start()
        out = compute(*operands) if compute is not None else ()
        self.before = list(out)
        return out


def place_kernel(emit, count, flag_ref, *refs):
    own, other, outs = refs[:count], refs[count : 2 * count], refs[2 * count :]
    k, s = pl.program_id(0), pl.program_id(1)
    for c in range(count):
        pl.when((s == c) & (k == flag_ref[0]))(functools.partial(emit, own[c], outs))
        pl.when((s == c) & (k != flag_ref[0]))(functools.partial(emit, other[c], outs))


def place(emit, flag, pieces, out_shapes, out_blocks, maps, name):
    count = len(pieces)
    arrays = [p[0] for p in pieces] + [p[1] for p in pieces]
    grid_spec = pltpu.PrefetchScalarGridSpec(
        num_scalar_prefetch=1,
        grid=(2, count),
        in_specs=[pl.BlockSpec(a.shape, lambda k, s, f: (0, 0)) for a in arrays],
        out_specs=[pl.BlockSpec(blk, m) for blk, m in zip(out_blocks, maps)],
    )
    return pl.pallas_call(
        functools.partial(place_kernel, emit, count),
        grid_spec=grid_spec,
        out_shape=[jax.ShapeDtypeStruct(o, F32) for o in out_shapes],
        compiler_params=pltpu.CompilerParams(vmem_limit_bytes=48 << 20),
        cost_estimate=pl.CostEstimate(
            flops=0, bytes_accessed=6 * 2 * count * arrays[0].size, transcendentals=0
        ),
        name=name,
    )(flag.reshape(1).astype(jnp.int32), *arrays)


def emit_plain(src, outs):
    outs[0][...] = src[...].astype(F32)


def emit_late(src, outs):
    for j in range(3):
        outs[0][j] = src[:, j * PAIR : (j + 1) * PAIR].astype(F32)
    outs[1][...] = src[:, 3 * PAIR :].astype(F32).T


def shards(
    dp_size,
    inputs,
    cotangent,
    seg_ids,
    pad_mask,
    positions,
    ln_gain,
    ln_bias,
    w_qkv,
    w_attn_out,
    w_up,
    b_up,
    w_down,
    b_down,
):
    b = lax.axis_index("branch")
    t = lax.axis_index("tensor")
    dp = lax.axis_index("dp")
    x_id, ring_id = lax.rem(dp, 2), dp // 2
    rows, quarter = inputs.shape
    half = 2 * quarter
    full = 4 * quarter
    heads_w = w_qkv.shape[2] // 2
    units = w_up.shape[1] // 2
    chunks = 2
    ids = jnp.stack([t, b]).astype(jnp.int32)

    def over_branch(v):
        return lax.ppermute(v, "branch", SWAP)

    def over_tensor(v):
        return lax.ppermute(v, "tensor", SWAP)

    def part(w, axis, index, size):
        return lax.dynamic_slice_in_dim(w, index * size, size, axis)

    aux = jnp.concatenate([ln_gain[None], ln_bias[None], jnp.zeros((14, quarter), BF16)], 0)
    x_got, x_far = over_tensor(inputs), over_branch(inputs)
    g_own, _ = lax.optimization_barrier((cotangent, x_far))
    g_got, g_far = over_tensor(g_own), over_branch(g_own)
    aux_got = over_tensor(aux)
    w_three = jnp.transpose(w_qkv, (1, 0, 2))
    far_q = over_branch(part(w_three, 2, 1 - b, heads_w))
    far_u = over_branch(part(w_up, 1, 1 - b, units))
    far_a = over_branch(part(w_attn_out, 0, 1 - b, heads_w))
    far_d = over_branch(part(w_down, 0, 1 - b, units))
    bias_up = b_up.reshape(1, 2 * units)
    cosines, sines = rotary_tables(positions)
    aux_half = jnp.where(
        t == 0, jnp.concatenate([aux, aux_got], 1), jnp.concatenate([aux_got, aux], 1)
    )
    aux_all = jnp.concatenate([aux_half, over_branch(aux_half)], 1)
    (x_got, x_far, g_far, aux_all, far_q, far_u, far_a, far_d, bias_up, cosines, sines) = (
        lax.optimization_barrier(
            (x_got, x_far, g_far, aux_all, far_q, far_u, far_a, far_d, bias_up, cosines, sines)
        )
    )
    x_pieces = (inputs, x_got, x_far, over_branch(x_got))
    normed, active, slope, qkv, term, stat = enter(
        ids, x_pieces, aux_all, w_three, far_q, w_up, far_u, w_down, far_d, bias_up, cosines, sines
    )
    g_got, active = lax.optimization_barrier((g_got, active))
    g_pieces = (cotangent, g_got, g_far, over_branch(g_got))
    g_all, d_mixed, down_near, down_send = down_grads(ids, g_pieces, active, w_attn_out, far_a)

    def chained(near, far):
        return Chain(near, far, dp_size, x_id, ring_id)

    def chunked(near, far):
        step = near.shape[0] // chunks
        return [
            chained(near[c * step : (c + 1) * step], far[c * step : (c + 1) * step])
            for c in range(chunks)
        ]

    def attend(pair):
        return lambda q, d: attention(q, d, cosines, sines, positions, pair)

    def late(*v):
        return late_grads(ids, *v)

    steps = Steps()
    d0, d1 = downs = chunked(down_near, down_send)
    d_hidden, up_near, up_send, bup = steps.run(
        [], [d0], lambda *v: up_grads(ids, *v, w_down, far_d), g_all, normed, slope
    )
    u0, u1 = ups = chunked(up_near, up_send)
    mixed0, d_joint0 = steps.run([d0], [d0, d1, u0], attend(0), qkv, d_mixed)
    l0 = chained(
        *steps.run([d0, d1, u0], [u1, d0, d1], late, normed, g_all, d_joint0, mixed0)
    )
    mixed1, d_joint1 = steps.run([u1, d0, d1], [l0, d0, d1, u0], attend(1), qkv, d_mixed)
    l1 = chained(
        *steps.run(
            [l0, d0, d1, u0], [d0, d1, u0, u1], late, normed, g_all, d_joint1, mixed1
        )
    )

    def finish(tm, m0, m1, dj0, dj1, dh):
        return leave(
            ids,
            x_pieces,
            stat,
            aux_all,
            (dj0, dj1),
            dh,
            w_three,
            far_q,
            w_up,
            far_u,
            (m0, m1),
            w_attn_out,
            far_a,
            tm,
        )

    d_near, d_far, row_sums, sums, term_near, term_far = steps.run(
        [d0, d1, u0, u1],
        [l1, d1, l0, u0, u1],
        finish,
        term,
        mixed0,
        mixed1,
        d_joint0,
        d_joint1,
        d_hidden,
    )
    g_float = cotangent.astype(F32)
    terms, grads = Scatter(term_near, term_far, t), Scatter(d_near, d_far, t)
    moving = [c for c in (d1, l1, l0, u0, u1) if c.moving is not None]

    def spread(rs, sm):
        own = part(sm, 1, t, quarter)
        got = [
            lax.ppermute(v, ("branch", "tensor"), [(i, i ^ k) for i in range(4)])
            for k, v in (
                (1, part(sm, 1, 1 - t, quarter)),
                (2, part(sm, 1, 2 + t, quarter)),
                (3, part(sm, 1, 3 - t, quarter)),
            )
        ]
        return rs + over_branch(rs), own + got[0] + got[1] + got[2]

    left = [c for c in (l1, l0, u0, u1, d0, d1) if c.stage + (c in moving) < len(c.hops)]
    row_sums, sums = steps.run(moving, [*left, terms, grads], spread, row_sums, sums)
    small = jnp.concatenate(
        [
            sums,
            jnp.sum(g_float, axis=0)[None],
            bup.reshape(units // quarter, quarter),
            jnp.zeros((1, quarter), F32),
        ]
    )
    small = Doubling(small, dp_size)
    moving = [*left, terms, grads]
    left = [c for c in left if c.stage + 1 < len(c.hops)]
    (row_sums,) = steps.run(
        moving, [*left, terms, small], lambda rs: (rs + over_tensor(rs),), row_sums
    )
    moving = [*left, terms, small]
    left = [c for c in left if c.stage + 1 < len(c.hops)] + [grads, small]
    while left:
        steps.run(moving, left)
        moving = left
        left = [c for c in left if c.stage + 1 < len(c.hops)]
    for c in moving:
        c.finish()

    row_sums = row_sums * (1.0 / full)
    output = (inputs.astype(F32) + terms.near + b_down.astype(F32)).astype(BF16)
    d_own = grads.near
    mean, inv_root = stat[:, 0:1], stat[:, 1:2]
    unit_own = (inputs.astype(F32) - mean) * inv_root
    input_grad = g_float + inv_root * (
        d_own * ln_gain.astype(F32)
        - row_sums[:, 0, :].reshape(rows, 1)
        - unit_own * row_sums[:, 1, :].reshape(rows, 1)
    )
    small = small.value
    bup = small[3:-1].reshape(units)
    bup_far = over_branch(bup)
    grad_bup = jnp.where(b == 0, jnp.concatenate([bup, bup_far]), jnp.concatenate([bup_far, bup]))

    flag = b ^ x_id
    (grad_down,) = place(
        emit_plain,
        flag,
        [c.pieces() for c in downs],
        [(2 * units, half)],
        [(units // chunks, half)],
        [lambda k, s, f: (k * chunks + s, 0)],
        "place_down",
    )
    (grad_up,) = place(
        emit_plain,
        flag,
        [c.pieces() for c in ups],
        [(half, 2 * units)],
        [(half // chunks, units)],
        [lambda k, s, f: (s, k)],
        "place_up",
    )
    grad_qkv, grad_aout = place(
        emit_late,
        flag,
        [c.pieces() for c in (l0, l1)],
        [(3, half, 2 * heads_w), (2 * heads_w, half)],
        [(3, half, PAIR), (PAIR, half)],
        [lambda k, s, f: (0, 0, 2 * k + s), lambda k, s, f: (2 * k + s, 0)],
        "place_late",
    )
    return (
        output,
        input_grad,
        small[0],
        small[1],
        jnp.transpose(grad_qkv, (1, 0, 2)),
        grad_aout,
        grad_up,
        grad_bup,
        grad_down,
        small[2],
    )


def solution(mesh):
    features = ("branch", "tensor")
    in_specs = (
        P("dp", features),
        P("dp", features),
        P("dp"),
        P("dp"),
        P("dp"),
        P(features),
        P(features),
        P("branch", None, "tensor"),
        P("tensor", "branch"),
        P("branch", "tensor"),
        P("tensor"),
        P("tensor", "branch"),
        P(features),
    )
    out_specs = (
        P("dp", features),
        P("dp", features),
        P(features),
        P(features),
        P("branch", None, "tensor"),
        P("tensor", "branch"),
        P("branch", "tensor"),
        P("tensor"),
        P("tensor", "branch"),
        P(features),
    )
    return jax.shard_map(
        functools.partial(shards, mesh.shape["dp"]),
        mesh=mesh,
        in_specs=in_specs,
        out_specs=out_specs,
        check_vma=False,
    )
```

```python
import functools

import jax
import jax.numpy as jnp
from jax import lax
from jax.experimental import pallas as pl
from jax.experimental.pallas import tpu as pltpu
from jax.sharding import PartitionSpec as P

HEAD_DIM = 64
ROTARY = 32
PAIR = 2 * HEAD_DIM
QB = 128
KC = 256
LONGEST = 1024
EPS = 1e-05
NEG = -1e30
F32 = jnp.float32
BF16 = jnp.bfloat16
SWAP = [(0, 1), (1, 0)]
GELU_A = 0.7978845608028654
GELU_B = 0.044715


def nn(a, b):
    return lax.dot_general(a, b, (((1,), (0,)), ((), ())), preferred_element_type=F32)


def nt(a, b):
    return lax.dot_general(a, b, (((1,), (1,)), ((), ())), preferred_element_type=F32)


def tn(a, b):
    return lax.dot_general(a, b, (((0,), (0,)), ((), ())), preferred_element_type=F32)


def partner(x, even):
    width = x.shape[1]
    return jnp.where(even, pltpu.roll(x, width - 1, 1), pltpu.roll(x, 1, 1))


def attention_kernel(
    pairs,
    most,
    span_ref,
    qkv_ref,
    dmix_ref,
    cos_ref,
    sin_ref,
    start_ref,
    normed_hbm,
    g_hbm,
    mixed_ref,
    dj_ref,
    near_ref,
    far_ref,
    q_s,
    qt_s,
    g_s,
    gt_s,
    k_s,
    v_s,
    kt_s,
    vt_s,
    s_s,
    d_s,
    p_s,
    e_s,
    dk_s,
    dv_s,
    normed_s,
    ct_s,
    arrived,
):
    fetch = [
        pltpu.make_async_copy(normed_hbm, normed_s, arrived.at[0]),
        pltpu.make_async_copy(g_hbm, ct_s, arrived.at[1]),
    ]
    for copy in fetch:
        copy.start()
    rows = qkv_ref.shape[0]
    width = pairs * PAIR
    lane = lax.broadcasted_iota(jnp.int32, (QB, PAIR), 1)
    even = lane % 2 == 0
    first = lane < HEAD_DIM
    top = lax.broadcasted_iota(jnp.int32, (PAIR, QB), 0) < HEAD_DIM
    scale = HEAD_DIM**-0.5

    for p in range(pairs):
        k_s[p, :QB, :] = jnp.zeros((QB, PAIR), BF16)
        v_s[p, :QB, :] = jnp.zeros((QB, PAIR), BF16)
        kt_s[p, :, :QB] = jnp.zeros((PAIR, QB), BF16)
        vt_s[p, :, :QB] = jnp.zeros((PAIR, QB), BF16)
        dk_s[p, :QB, :] = jnp.zeros((QB, PAIR), F32)
        dv_s[p, :QB, :] = jnp.zeros((QB, PAIR), F32)

    @pl.loop(0, rows // QB)
    def _(i):
        at = pl.ds(pl.multiple_of(i * QB, QB), QB)
        to = pl.ds(pl.multiple_of(i * QB + QB, QB), QB)
        for p in range(pairs):
            q = qkv_ref[at, p * PAIR : (p + 1) * PAIR].astype(F32)
            k = qkv_ref[at, width + p * PAIR : width + (p + 1) * PAIR]
            v = qkv_ref[at, 2 * width + p * PAIR : 2 * width + (p + 1) * PAIR]
            g = dmix_ref[at, p * PAIR : (p + 1) * PAIR].astype(F32)
            q_s[p, i, :QB, :] = jnp.where(first, q, 0.0).astype(BF16)
            q_s[p, i, QB:, :] = jnp.where(first, 0.0, q).astype(BF16)
            g_s[p, i, :QB, :] = jnp.where(first, g, 0.0).astype(BF16)
            g_s[p, i, QB:, :] = jnp.where(first, 0.0, g).astype(BF16)
            q, g = q.T, g.T
            qt_s[p, i, :, :QB] = jnp.where(top, q, 0.0).astype(BF16)
            qt_s[p, i, :, QB:] = jnp.where(top, 0.0, q).astype(BF16)
            gt_s[p, i, :, :QB] = jnp.where(top, g, 0.0).astype(BF16)
            gt_s[p, i, :, QB:] = jnp.where(top, 0.0, g).astype(BF16)
            k_s[p, to, :] = k
            v_s[p, to, :] = v
            kt_s[p, :, to] = k.astype(F32).T.astype(BF16)
            vt_s[p, :, to] = v.astype(F32).T.astype(BF16)
            dk_s[p, to, :] = jnp.zeros((QB, PAIR), F32)
            dv_s[p, to, :] = jnp.zeros((QB, PAIR), F32)

    key_slot = lax.broadcasted_iota(jnp.int32, (KC, 2 * QB), 0)
    query_slot = lax.broadcasted_iota(jnp.int32, (1, 2 * QB), 1) % QB

    def block(i, n):
        base = (i + 2) * QB - n * KC
        spots = [pl.ds(pl.multiple_of(base + j * KC, QB), KC) for j in range(n)]
        whole = pl.ds(pl.multiple_of(base, QB), n * KC)
        query = query_slot + (i * QB + QB - base)
        start = start_ref[i] + (QB - base)
        here = pl.ds(pl.multiple_of(i * QB, QB), QB)
        pr = range(pairs)
        peak = [None] * pairs
        for j in range(n):
            ok = (key_slot >= start - j * KC) & (key_slot <= query - j * KC)
            for p in pr:
                s = jnp.where(ok, nn(k_s[p, spots[j], :], qt_s[p, i]), NEG)
                s_s[p, j] = s
                m = jnp.max(s.reshape(KC // 8, 8, 2 * QB), axis=0)
                peak[p] = m if peak[p] is None else jnp.maximum(peak[p], m)
        for j in range(n):
            for p in pr:
                d_s[p, j] = nn(v_s[p, spots[j], :], gt_s[p, i])
        peak = [jnp.max(m, axis=0, keepdims=True) for m in peak]
        total = [0.0] * pairs
        delta = [0.0] * pairs
        for j in range(n):
            for p in pr:
                e = jnp.exp(s_s[p, j] - peak[p])
                s_s[p, j] = e
                total[p] += jnp.sum(e.reshape(KC // 8, 8, 2 * QB), axis=0)
                delta[p] += jnp.sum((e * d_s[p, j]).reshape(KC // 8, 8, 2 * QB), axis=0)
        inverse = [1.0 / jnp.sum(x, axis=0, keepdims=True) for x in total]
        delta = [jnp.sum(x, axis=0, keepdims=True) * r for x, r in zip(delta, inverse)]
        for j in range(n):
            for p in pr:
                prob = s_s[p, j] * inverse[p]
                p_s[p, j * KC : (j + 1) * KC, :] = prob.astype(BF16)
                e_s[p, j * KC : (j + 1) * KC, :] = (prob * (d_s[p, j] - delta[p])).astype(BF16)
        for p in pr:
            o = nn(vt_s[p, :, whole], p_s[p, : n * KC, :])
            mixed_ref[here, p * PAIR : (p + 1) * PAIR] = (
                jnp.where(top, o[:, :QB], o[:, QB:]).T.astype(BF16)
            )
            dv_s[p, whole, :] += nn(p_s[p, : n * KC, :], g_s[p, i])
            dk_s[p, whole, :] += nn(e_s[p, : n * KC, :], q_s[p, i])
            d = nn(kt_s[p, :, whole], e_s[p, : n * KC, :])
            d = (jnp.where(top, d[:, :QB], d[:, QB:]) * scale).T
            d = d * cos_ref[here, :] - partner(d, even) * sin_ref[here, :]
            dj_ref[here, p * PAIR : (p + 1) * PAIR] = d.astype(BF16)

    @pl.loop(0, rows // QB)
    def _(i):
        for n in range(1, most + 1):
            pl.when(span_ref[i] == n)(functools.partial(block, i, n))

    @pl.loop(0, rows // QB)
    def _(i):
        at = pl.ds(pl.multiple_of(i * QB, QB), QB)
        to = pl.ds(pl.multiple_of(i * QB + QB, QB), QB)
        cosines = cos_ref[at, :]
        sines = sin_ref[at, :]
        for p in range(pairs):
            d = dk_s[p, to, :]
            d = d * cosines - partner(d, even) * sines
            dj_ref[at, width + p * PAIR : width + (p + 1) * PAIR] = d.astype(BF16)
            dj_ref[at, 2 * width + p * PAIR : 2 * width + (p + 1) * PAIR] = dv_s[p, to, :].astype(
                BF16
            )

    for copy in fetch:
        copy.wait()
    half, split = near_ref.shape[0], 3 * width
    for at, out in ((slice(half, 2 * half), far_ref), (slice(0, half), near_ref)):
        out[:, :split] = tn(normed_s[:, at], dj_ref[...]).astype(BF16)
        out[:, split:] = tn(ct_s[:, at], mixed_ref[...]).astype(BF16)


def attention(qkv, dmix, normed, g_all, cosines, sines, positions, pair):
    rows = qkv.shape[0]
    pairs = 1
    blocks = rows // QB
    padded = rows + QB
    most = LONGEST // KC + 1
    start = (jnp.arange(rows, dtype=jnp.int32) - positions).reshape(blocks, 1, QB)
    span = (jnp.arange(blocks, dtype=jnp.int32) - start[:, 0, 0] // QB + 2) // 2
    start = jnp.concatenate([start, start], axis=2)
    half, split = normed.shape[1] // 2, 3 * pairs * PAIR
    vmem = pl.BlockSpec(memory_space=pltpu.VMEM)
    return pl.pallas_call(
        functools.partial(attention_kernel, pairs, most),
        grid=(1,),
        out_shape=(
            jax.ShapeDtypeStruct((rows, pairs * PAIR), BF16),
            jax.ShapeDtypeStruct((rows, 3 * pairs * PAIR), BF16),
            jax.ShapeDtypeStruct((half, split + pairs * PAIR), BF16),
            jax.ShapeDtypeStruct((half, split + pairs * PAIR), BF16),
        ),
        in_specs=[
            pl.BlockSpec(memory_space=pltpu.SMEM),
            pl.BlockSpec((rows, 3 * pairs * PAIR), lambda i: (0, pair)),
            pl.BlockSpec((rows, pairs * PAIR), lambda i: (0, pair)),
            vmem,
            vmem,
            vmem,
            pl.BlockSpec(memory_space=pl.ANY),
            pl.BlockSpec(memory_space=pl.ANY),
        ],
        out_specs=(
            pl.BlockSpec((rows, pairs * PAIR), lambda i: (0, 0)),
            pl.BlockSpec((rows, 3 * pairs * PAIR), lambda i: (0, 0)),
            vmem,
            vmem,
        ),
        scratch_shapes=[
            pltpu.VMEM((pairs, blocks, 2 * QB, PAIR), BF16),
            pltpu.VMEM((pairs, blocks, PAIR, 2 * QB), BF16),
            pltpu.VMEM((pairs, blocks, 2 * QB, PAIR), BF16),
            pltpu.VMEM((pairs, blocks, PAIR, 2 * QB), BF16),
            pltpu.VMEM((pairs, padded, PAIR), BF16),
            pltpu.VMEM((pairs, padded, PAIR), BF16),
            pltpu.VMEM((pairs, PAIR, padded), BF16),
            pltpu.VMEM((pairs, PAIR, padded), BF16),
            pltpu.VMEM((pairs, most, KC, 2 * QB), F32),
            pltpu.VMEM((pairs, most, KC, 2 * QB), F32),
            pltpu.VMEM((pairs, most * KC, 2 * QB), BF16),
            pltpu.VMEM((pairs, most * KC, 2 * QB), BF16),
            pltpu.VMEM((pairs, padded, PAIR), F32),
            pltpu.VMEM((pairs, padded, PAIR), F32),
            pltpu.VMEM(normed.shape, BF16),
            pltpu.VMEM(g_all.shape, BF16),
            pltpu.SemaphoreType.DMA((2,)),
        ],
        compiler_params=pltpu.CompilerParams(vmem_limit_bytes=40 << 20),
        cost_estimate=pl.CostEstimate(
            flops=0, bytes_accessed=0, transcendentals=0
        ),
        name="attention",
    )(span, qkv, dmix, cosines, sines, start, normed, g_all)


def picked(first, own, got, far_own, far_got):
    own, got, far_own, far_got = (v[...].astype(F32) for v in (own, got, far_own, far_got))
    return jnp.concatenate(
        [
            jnp.where(first, own, got),
            jnp.where(first, got, own),
            jnp.where(first, far_own, far_got),
            jnp.where(first, far_got, far_own),
        ],
        1,
    )


def resident(shape):
    return pl.BlockSpec(shape, lambda i: (0,) * len(shape), pipeline_mode=pl.Buffered(1))


def enter_kernel(
    ids,
    own,
    got,
    far_own,
    far_got,
    aux_ref,
    near_q,
    far_q,
    near_u,
    far_u,
    bias_ref,
    cos_ref,
    sin_ref,
    normed_ref,
    active_ref,
    slope_ref,
    qkv_ref,
    stat_ref,
):
    x = picked(ids[0] == 0, own, got, far_own, far_got)
    rows, full = x.shape
    half = full // 2
    mean = jnp.mean(x, axis=1, keepdims=True)
    center = x - mean
    inv_root = lax.rsqrt(jnp.mean(center * center, axis=1, keepdims=True) + EPS)
    normed = (
        center * inv_root * aux_ref[0:1, :].astype(F32) + aux_ref[1:2, :].astype(F32)
    ).astype(BF16)
    normed_ref[...] = normed
    lane = lax.broadcasted_iota(jnp.int32, (rows, PAIR), 1)
    stat_ref[...] = jnp.where(lane == 0, mean, inv_root)
    near, far = normed[:, :half], normed[:, half:]
    hidden = nn(near, near_u[...]) + nn(far, far_u[...]) + bias_ref[0:1, :].astype(F32)
    square = hidden * hidden
    bend = jnp.tanh(GELU_A * hidden * (1.0 + GELU_B * square))
    up = 0.5 * (1.0 + bend)
    active = (hidden * up).astype(BF16)
    active_ref[...] = active
    slope_ref[...] = up + (0.5 * GELU_A) * hidden * (1.0 - bend * bend) * (
        1.0 + 3.0 * GELU_B * square
    )
    even = lane % 2 == 0
    cosines, sines = cos_ref[...], sin_ref[...]
    for j in range(3):
        joint = nn(near, near_q[j]) + nn(far, far_q[j])
        for p in range(joint.shape[1] // PAIR):
            v = joint[:, p * PAIR : (p + 1) * PAIR]
            if j < 2:
                v = v * cosines + partner(v, even) * sines
            if j == 0:
                v = v * HEAD_DIM**-0.5
            at = (3 * p + j) * PAIR
            qkv_ref[:, at : at + PAIR] = v.astype(BF16)


def rows_of(step, width):
    return pl.BlockSpec((step, width), lambda i, ids: (i, 0))


def fixed(shape, index=None):
    if index is None:
        return pl.BlockSpec(
            shape, lambda i, ids: (0,) * len(shape), pipeline_mode=pl.Buffered(1)
        )
    return pl.BlockSpec(shape, lambda i, ids: index(ids), pipeline_mode=pl.Buffered(1))


def by_rows(kernel, steps, ids, ins, outs, name, scratch=()):
    return pl.pallas_call(
        kernel,
        grid_spec=pltpu.PrefetchScalarGridSpec(
            num_scalar_prefetch=1,
            grid=(steps,),
            in_specs=[s for _, s in ins],
            out_specs=[s for _, _, s in outs],
            scratch_shapes=scratch,
        ),
        out_shape=[jax.ShapeDtypeStruct(s, d) for s, d, _ in outs],
        compiler_params=pltpu.CompilerParams(vmem_limit_bytes=50 << 20),
        cost_estimate=pl.CostEstimate(flops=0, bytes_accessed=0, transcendentals=0),
        name=name,
    )(ids, *[a for a, _ in ins])


def enter(ids, pieces, aux, w_three, far_q, w_up, far_u, bias, cosines, sines):
    rows, quarter = pieces[0].shape
    full, half = 4 * quarter, 2 * quarter
    units, heads_w = far_u.shape[1], far_q.shape[2]
    step = rows // 8
    ins = [(v, rows_of(step, quarter)) for v in pieces] + [
        (aux, fixed(aux.shape)),
        (w_three, fixed((3, half, heads_w), lambda ids: (0, 0, ids[1]))),
        (far_q, fixed(far_q.shape)),
        (w_up, fixed((half, units), lambda ids: (0, ids[1]))),
        (far_u, fixed(far_u.shape)),
        (bias, fixed((1, units), lambda ids: (0, ids[1]))),
        (cosines, rows_of(step, PAIR)),
        (sines, rows_of(step, PAIR)),
    ]
    outs = [
        ((rows, full), BF16, rows_of(step, full)),
        ((rows, units), BF16, rows_of(step, units)),
        ((rows, units), F32, rows_of(step, units)),
        ((rows, 3 * heads_w), BF16, rows_of(step, 3 * heads_w)),
        ((rows, PAIR), F32, rows_of(step, PAIR)),
    ]
    return by_rows(enter_kernel, 8, ids, ins, outs, "enter")


def down_kernel(
    ids,
    own,
    got,
    far_own,
    far_got,
    active_ref,
    near_a,
    far_a,
    g_ref,
    dm_ref,
    near_ref,
    far_ref,
    total_s,
):
    i = pl.program_id(0)
    g = picked(ids[0] == 0, own, got, far_own, far_got).astype(BF16)
    half = g.shape[1] // 2
    g_ref[...] = g
    dm_ref[...] = (nt(g[:, :half], near_a[...]) + nt(g[:, half:], far_a[...])).astype(BF16)

    @pl.when(i == 0)
    def _():
        total_s[...] = tn(active_ref[...], g)

    @pl.when(i > 0)
    def _():
        total_s[...] += tn(active_ref[...], g)

    @pl.when(i == pl.num_programs(0) - 1)
    def _():
        near_ref[...] = total_s[:, :half].astype(BF16)
        far_ref[...] = total_s[:, half:].astype(BF16)


def down_grads(ids, pieces, active, w_attn_out, far_a):
    rows, quarter = pieces[0].shape
    full, half, units = 4 * quarter, 2 * quarter, active.shape[1]
    heads_w = far_a.shape[0]
    step = rows // 4
    ins = [(v, rows_of(step, quarter)) for v in pieces] + [
        (active, rows_of(step, units)),
        (w_attn_out, fixed((heads_w, half), lambda ids: (ids[1], 0))),
        (far_a, fixed(far_a.shape)),
    ]
    outs = [
        ((rows, full), BF16, rows_of(step, full)),
        ((rows, heads_w), BF16, rows_of(step, heads_w)),
        ((units, half), BF16, fixed((units, half))),
        ((units, half), BF16, fixed((units, half))),
    ]
    return by_rows(
        down_kernel,
        4,
        ids,
        ins,
        outs,
        "down_grads",
        [pltpu.VMEM((units, full), F32)],
    )


def up_kernel(
    ids,
    g_ref,
    normed_ref,
    slope_ref,
    near_d,
    far_d,
    dh_ref,
    near_ref,
    far_ref,
    sum_ref,
    total_s,
):
    i = pl.program_id(0)
    half = g_ref.shape[1] // 2
    da = nt(g_ref[:, :half], near_d[...]) + nt(g_ref[:, half:], far_d[...])
    dh = (da * slope_ref[...]).astype(BF16)
    dh_ref[...] = dh
    sums = jnp.sum(dh.astype(F32), axis=0, keepdims=True)

    @pl.when(i == 0)
    def _():
        total_s[...] = tn(normed_ref[...], dh)
        sum_ref[...] = sums

    @pl.when(i > 0)
    def _():
        total_s[...] += tn(normed_ref[...], dh)
        sum_ref[...] += sums

    @pl.when(i == pl.num_programs(0) - 1)
    def _():
        near_ref[...] = total_s[:half, :].astype(BF16)
        far_ref[...] = total_s[half:, :].astype(BF16)


def up_grads(ids, g_all, normed, slope, w_down, far_d):
    rows, full = g_all.shape
    half, units = full // 2, slope.shape[1]
    step = rows // 4
    ins = [
        (g_all, rows_of(step, full)),
        (normed, rows_of(step, full)),
        (slope, rows_of(step, units)),
        (w_down, fixed((units, half), lambda ids: (ids[1], 0))),
        (far_d, fixed(far_d.shape)),
    ]
    outs = [
        ((rows, units), BF16, rows_of(step, units)),
        ((half, units), BF16, fixed((half, units))),
        ((half, units), BF16, fixed((half, units))),
        ((1, units), F32, fixed((1, units))),
    ]
    return by_rows(
        up_kernel,
        4,
        ids,
        ins,
        outs,
        "up_grads",
        [pltpu.VMEM((full, units), F32)],
    )


def leave_kernel(
    ids,
    own,
    got,
    far_own,
    far_got,
    stat_ref,
    aux_ref,
    dj0_ref,
    dj1_ref,
    dh_ref,
    near_q,
    far_q,
    near_u,
    far_u,
    mixed0_ref,
    mixed1_ref,
    near_a,
    far_a,
    active_ref,
    near_d,
    far_d,
    near_ref,
    far_ref,
    row_ref,
    sum_ref,
    term_near,
    term_far,
):
    i = pl.program_id(0)
    mixed = jnp.concatenate([mixed0_ref[...], mixed1_ref[...]], 1)
    active = active_ref[...]
    term_near[...] = nn(active, near_d[...]) + nn(mixed, near_a[...])
    term_far[...] = (nn(active, far_d[...]) + nn(mixed, far_a[...])).astype(BF16)
    x = picked(ids[0] == 0, own, got, far_own, far_got)
    unit = (x - stat_ref[:, 0:1]) * stat_ref[:, 1:2]
    dh = dh_ref[...]
    near = nt(dh, near_u[...])
    far = nt(dh, far_u[...])
    for j in range(3):
        cut = slice(j * PAIR, (j + 1) * PAIR)
        dj = jnp.concatenate([dj0_ref[:, cut], dj1_ref[:, cut]], 1)
        near += nt(dj, near_q[j])
        far += nt(dj, far_q[j])
    near_ref[...] = near
    far_ref[...] = far.astype(BF16)
    both = jnp.concatenate([near, far], 1)
    scaled = both * aux_ref[0:1, :].astype(F32)
    first = jnp.sum(scaled, axis=1, keepdims=True)
    second = jnp.sum(scaled * unit, axis=1, keepdims=True)
    lane = lax.broadcasted_iota(jnp.int32, (x.shape[0], PAIR), 1)
    row_ref[0] = jnp.where(lane == 0, first, second).T[:8]
    sums = jnp.concatenate(
        [
            jnp.sum(both * unit, axis=0, keepdims=True),
            jnp.sum(both, axis=0, keepdims=True),
        ],
        0,
    )

    @pl.when(i == 0)
    def _():
        sum_ref[...] = sums

    @pl.when(i > 0)
    def _():
        sum_ref[...] += sums


def leave(
    ids,
    pieces,
    stat,
    aux,
    d_joints,
    d_hidden,
    w_three,
    far_q,
    w_up,
    far_u,
    mixed,
    w_attn_out,
    far_a,
    active,
    w_down,
    far_d,
):
    rows, quarter = pieces[0].shape
    full, half = 4 * quarter, 2 * quarter
    units, heads_w = far_u.shape[1], far_q.shape[2]
    step = rows // 4
    ins = (
        [(v, rows_of(step, quarter)) for v in pieces]
        + [(stat, rows_of(step, PAIR)), (aux, fixed(aux.shape))]
        + [(d, rows_of(step, 3 * PAIR)) for d in d_joints]
        + [
            (d_hidden, rows_of(step, units)),
            (w_three, fixed((3, half, heads_w), lambda ids: (0, 0, ids[1]))),
            (far_q, fixed(far_q.shape)),
            (w_up, fixed((half, units), lambda ids: (0, ids[1]))),
            (far_u, fixed(far_u.shape)),
        ]
        + [(m, rows_of(step, PAIR)) for m in mixed]
        + [
            (w_attn_out, fixed((heads_w, half), lambda ids: (ids[1], 0))),
            (far_a, fixed(far_a.shape)),
            (active, rows_of(step, units)),
            (w_down, fixed((units, half), lambda ids: (ids[1], 0))),
            (far_d, fixed(far_d.shape)),
        ]
    )
    outs = [
        ((rows, half), F32, rows_of(step, half)),
        ((rows, half), BF16, rows_of(step, half)),
        ((4, 8, step), F32, pl.BlockSpec((1, 8, step), lambda i, ids: (i, 0, 0))),
        ((2, full), F32, fixed((2, full))),
        ((rows, half), F32, rows_of(step, half)),
        ((rows, half), BF16, rows_of(step, half)),
    ]
    return by_rows(leave_kernel, 4, ids, ins, outs, "leave")


def rotary_tables(positions):
    lane = jnp.arange(PAIR, dtype=jnp.int32)
    feature = lane % HEAD_DIM
    inverse = 10000.0 ** (-(2.0 * (feature // 2).astype(F32)) / ROTARY)
    angle = positions.astype(F32)[:, None] * inverse[None, :]
    turned = (feature < ROTARY)[None, :]
    sign = jnp.where(feature % 2 == 0, -1.0, 1.0)[None, :]
    cosines = jnp.where(turned, jnp.cos(angle), 1.0)
    sines = jnp.where(turned, jnp.sin(angle) * sign, 0.0)
    return cosines, sines


class Chain:
    def __init__(self, value, far, size, x_id, place):
        self.low, self.place = x_id == 0, place
        self.value, self.far, self.keep = jnp.where(self.low, far, value), far, value
        self.moving = self.other = self.crossed = None
        line = size // 2
        steps = line // 2 - 1

        def perm(pairs):
            return [(2 * i + x, 2 * j + x) for i, j in pairs for x in range(2)]

        self.pair = [(i, i ^ 1) for i in range(size)]
        self.hops = [(self.pair, None)]
        if line > 1:
            for k in range(steps):
                self.hops.append((perm([(k, k + 1), (line - 1 - k, line - 2 - k)]), None))
            mid = line // 2
            self.hops.append((perm([(mid - 1, mid), (mid, mid - 1)]), None))
            for k in reversed(range(steps)):
                self.hops.append((perm([(k + 1, k), (line - 2 - k, line - 1 - k)]), (k, line - 1 - k)))
        self.hops.append((self.pair, None))
        self.stage = 0
        self.cross = [
            (2 * i + c, 2 * (i ^ 1) + (c if i % 2 else 1 - c)) for i in range(size) for c in range(2)
        ]
        self.trade = [(2 * i + c, 2 * i + 1 - c) for i in range(1, size, 2) for c in range(2)]

    def busy(self):
        return self.stage < len(self.hops)

    def start(self):
        if self.stage == 0:
            self.moving = lax.ppermute(self.value, ("dp", "branch"), self.cross)
            self.crossed = lax.ppermute(self.far, ("dp", "branch"), self.trade)
        else:
            self.moving = lax.ppermute(self.value, "dp", self.hops[self.stage][0])

    def finish(self):
        got, self.moving = self.moving, None
        ends = self.hops[self.stage][1]
        if self.stage == len(self.hops) - 1:
            self.other = got
        elif ends is None:
            base = self.value
            if self.stage == 0:
                base = jnp.where(self.low, self.keep, self.crossed)
            self.value = (base.astype(F32) + got.astype(F32)).astype(base.dtype)
        else:
            here = (self.place == ends[0]) | (self.place == ends[1])
            self.value = jnp.where(here, got, self.value)
        self.stage += 1

    def pieces(self):
        return (self.value, self.other)


class Scatter:
    hops = (0, 1)

    def __init__(self, near, far, t):
        self.near, self.value, self.low = near, far, t == 0
        self.moving = self.far = None
        self.stage = 0

    def busy(self):
        return self.stage < 2

    def start(self):
        self.moving = lax.ppermute(self.value, ("branch", "tensor")[self.stage], SWAP)

    def finish(self):
        got, self.moving = self.moving, None
        if self.stage == 0:
            total = self.near + got.astype(F32)
            low, high = jnp.split(total, 2, axis=1)
            self.value = jnp.where(self.low, high, low).astype(BF16)
            self.near = jnp.where(self.low, low, high)
        else:
            self.near = self.near + got.astype(F32)
        self.stage += 1


class Doubling:
    def __init__(self, value, size):
        self.value, self.far, self.moving = value, None, None
        self.hops = [1 << k for k in range(size.bit_length() - 1)]
        self.size, self.stage = size, 0

    def busy(self):
        return self.stage < len(self.hops)

    def start(self):
        away = self.hops[self.stage]
        self.moving = lax.ppermute(self.value, "dp", [(i, i ^ away) for i in range(self.size)])

    def finish(self):
        self.value = self.value + self.moving
        self.moving = None
        self.stage += 1


class Steps:
    def __init__(self):
        self.before = []

    def run(self, finish, start, compute=None, *operands):
        for c in finish:
            c.finish()
        touched = list({id(c): c for c in [*finish, *start]}.values())
        values, fars, operands, _ = lax.optimization_barrier(
            (
                [c.value for c in touched],
                [c.far for c in start if c.far is not None],
                operands,
                self.before,
            )
        )
        for c, v in zip(touched, values):
            c.value = v
        for c, v in zip([c for c in start if c.far is not None], fars):
            c.far = v
        for c in start:
            c.start()
        out = compute(*operands) if compute is not None else ()
        self.before = list(out)
        return out


def place_kernel(emit, count, flag_ref, *refs):
    own, other, outs = refs[:count], refs[count : 2 * count], refs[2 * count :]
    k, s = pl.program_id(0), pl.program_id(1)
    for c in range(count):
        pl.when((s == c) & (k == flag_ref[0]))(functools.partial(emit, own[c], outs))
        pl.when((s == c) & (k != flag_ref[0]))(functools.partial(emit, other[c], outs))


def place(emit, flag, pieces, out_shapes, out_blocks, maps, name):
    count = len(pieces)
    arrays = [p[0] for p in pieces] + [p[1] for p in pieces]
    grid_spec = pltpu.PrefetchScalarGridSpec(
        num_scalar_prefetch=1,
        grid=(2, count),
        in_specs=[pl.BlockSpec(a.shape, lambda k, s, f: (0, 0)) for a in arrays],
        out_specs=[pl.BlockSpec(blk, m) for blk, m in zip(out_blocks, maps)],
    )
    return pl.pallas_call(
        functools.partial(place_kernel, emit, count),
        grid_spec=grid_spec,
        out_shape=[jax.ShapeDtypeStruct(o, F32) for o in out_shapes],
        compiler_params=pltpu.CompilerParams(vmem_limit_bytes=48 << 20),
        cost_estimate=pl.CostEstimate(
            flops=0, bytes_accessed=6 * 2 * count * arrays[0].size, transcendentals=0
        ),
        name=name,
    )(flag.reshape(1).astype(jnp.int32), *arrays)


def emit_plain(src, outs):
    outs[0][...] = src[...].astype(F32)


def emit_late(src, outs):
    for j in range(3):
        outs[0][j] = src[:, j * PAIR : (j + 1) * PAIR].astype(F32)
    outs[1][...] = src[:, 3 * PAIR :].astype(F32).T


def shards(
    dp_size,
    inputs,
    cotangent,
    seg_ids,
    pad_mask,
    positions,
    ln_gain,
    ln_bias,
    w_qkv,
    w_attn_out,
    w_up,
    b_up,
    w_down,
    b_down,
):
    b = lax.axis_index("branch")
    t = lax.axis_index("tensor")
    dp = lax.axis_index("dp")
    x_id, ring_id = lax.rem(dp, 2), dp // 2
    rows, quarter = inputs.shape
    half = 2 * quarter
    full = 4 * quarter
    heads_w = w_qkv.shape[2] // 2
    units = w_up.shape[1] // 2
    ids = jnp.stack([t, b]).astype(jnp.int32)

    def over_branch(v):
        return lax.ppermute(v, "branch", SWAP)

    def over_tensor(v):
        return lax.ppermute(v, "tensor", SWAP)

    def part(w, axis, index, size):
        return lax.dynamic_slice_in_dim(w, index * size, size, axis)

    x_got, x_far = over_tensor(inputs), over_branch(inputs)
    g_own, _ = lax.optimization_barrier((cotangent, x_far))
    g_got = over_tensor(g_own)
    aux = jnp.concatenate([ln_gain[None], ln_bias[None], jnp.zeros((14, quarter), BF16)], 0)
    aux_got = over_tensor(aux)
    w_three = jnp.transpose(w_qkv, (1, 0, 2))
    far_q = over_branch(part(w_three, 2, 1 - b, heads_w))
    far_u = over_branch(part(w_up, 1, 1 - b, units))
    bias_up = b_up.reshape(1, 2 * units)
    cosines, sines = rotary_tables(positions)
    aux_got, cosines, sines = lax.optimization_barrier((aux_got, cosines, sines))
    aux_half = jnp.where(
        t == 0, jnp.concatenate([aux, aux_got], 1), jnp.concatenate([aux_got, aux], 1)
    )
    aux_all = jnp.concatenate([aux_half, over_branch(aux_half)], 1)
    (x_got, x_far, aux_all, far_q, far_u, bias_up, cosines, sines) = lax.optimization_barrier(
        (x_got, x_far, aux_all, far_q, far_u, bias_up, cosines, sines)
    )
    x_pieces = (inputs, x_got, x_far, over_branch(x_got))
    normed, active, slope, qkv, stat = enter(
        ids, x_pieces, aux_all, w_three, far_q, w_up, far_u, bias_up, cosines, sines
    )
    g_far = over_branch(cotangent)
    far_a = over_branch(part(w_attn_out, 0, 1 - b, heads_w))
    far_d = over_branch(part(w_down, 0, 1 - b, units))
    g_got, g_far, far_a, far_d, active = lax.optimization_barrier(
        (g_got, g_far, far_a, far_d, active)
    )
    g_pieces = (cotangent, g_got, g_far, over_branch(g_got))
    g_all, d_mixed, down_near, down_send = down_grads(ids, g_pieces, active, w_attn_out, far_a)

    def chained(near, far):
        return Chain(near, far, dp_size, x_id, ring_id)

    def attend(pair):
        return lambda *v: attention(*v, cosines, sines, positions, pair)

    steps = Steps()
    down = chained(down_near, down_send)
    d_hidden, up_near, up_send, bup = steps.run(
        [], [down], lambda *v: up_grads(ids, *v, w_down, far_d), g_all, normed, slope
    )
    up = chained(up_near, up_send)
    mixed0, d_joint0, near0, send0 = steps.run(
        [down], [up, down], attend(0), qkv, d_mixed, normed, g_all
    )
    late0 = chained(near0, send0)
    mixed1, d_joint1, near1, send1 = steps.run(
        [up, down], [late0, down, up], attend(1), qkv, d_mixed, normed, g_all
    )
    late1 = chained(near1, send1)

    def finish(ac, m0, m1, dj0, dj1, dh):
        return leave(
            ids,
            x_pieces,
            stat,
            aux_all,
            (dj0, dj1),
            dh,
            w_three,
            far_q,
            w_up,
            far_u,
            (m0, m1),
            w_attn_out,
            far_a,
            ac,
            w_down,
            far_d,
        )

    d_near, d_far, row_sums, sums, term_near, term_far = steps.run(
        [late0, down, up],
        [late1, late0, down, up],
        finish,
        active,
        mixed0,
        mixed1,
        d_joint0,
        d_joint1,
        d_hidden,
    )
    g_float = cotangent.astype(F32)
    terms, grads = Scatter(term_near, term_far, t), Scatter(d_near, d_far, t)
    moving = [late1, late0, down, up]

    def spread(rs, sm):
        own = part(sm, 1, t, quarter)
        got = [
            lax.ppermute(v, ("branch", "tensor"), [(i, i ^ k) for i in range(4)])
            for k, v in (
                (1, part(sm, 1, 1 - t, quarter)),
                (2, part(sm, 1, 2 + t, quarter)),
                (3, part(sm, 1, 3 - t, quarter)),
            )
        ]
        return rs + over_branch(rs), own + got[0] + got[1] + got[2]

    left = [c for c in (down, up, late1, late0) if c.stage + 1 < len(c.hops)]
    row_sums, sums = steps.run(moving, [*left, terms, grads], spread, row_sums, sums)
    small = jnp.concatenate(
        [
            sums,
            jnp.sum(g_float, axis=0)[None],
            bup.reshape(units // quarter, quarter),
            jnp.zeros((1, quarter), F32),
        ]
    )
    small = Doubling(small, dp_size)
    moving = [*left, terms, grads]
    left = [c for c in left if c.stage + 1 < len(c.hops)]
    (row_sums,) = steps.run(
        moving, [*left, terms, small], lambda rs: (rs + over_tensor(rs),), row_sums
    )
    moving = [*left, terms, small]
    left = [c for c in left if c.stage + 1 < len(c.hops)] + [grads, small]
    while left:
        steps.run(moving, left)
        moving = left
        left = [c for c in left if c.stage + 1 < len(c.hops)]
    for c in moving:
        c.finish()

    row_sums = row_sums * (1.0 / full)
    output = (inputs.astype(F32) + terms.near + b_down.astype(F32)).astype(BF16)
    d_own = grads.near
    mean, inv_root = stat[:, 0:1], stat[:, 1:2]
    unit_own = (inputs.astype(F32) - mean) * inv_root
    input_grad = g_float + inv_root * (
        d_own * ln_gain.astype(F32)
        - row_sums[:, 0, :].reshape(rows, 1)
        - unit_own * row_sums[:, 1, :].reshape(rows, 1)
    )
    small = small.value
    bup = small[3:-1].reshape(units)
    bup_far = over_branch(bup)
    grad_bup = jnp.where(b == 0, jnp.concatenate([bup, bup_far]), jnp.concatenate([bup_far, bup]))

    flag = b ^ x_id
    (grad_down,) = place(
        emit_plain,
        flag,
        [down.pieces()],
        [(2 * units, half)],
        [(units, half)],
        [lambda k, s, f: (k, 0)],
        "place_down",
    )
    (grad_up,) = place(
        emit_plain,
        flag,
        [up.pieces()],
        [(half, 2 * units)],
        [(half, units)],
        [lambda k, s, f: (0, k)],
        "place_up",
    )
    grad_qkv, grad_aout = place(
        emit_late,
        flag,
        [c.pieces() for c in (late0, late1)],
        [(3, half, 2 * heads_w), (2 * heads_w, half)],
        [(3, half, PAIR), (PAIR, half)],
        [lambda k, s, f: (0, 0, 2 * k + s), lambda k, s, f: (2 * k + s, 0)],
        "place_late",
    )
    return (
        output,
        input_grad,
        small[0],
        small[1],
        jnp.transpose(grad_qkv, (1, 0, 2)),
        grad_aout,
        grad_up,
        grad_bup,
        grad_down,
        small[2],
    )


def solution(mesh):
    features = ("branch", "tensor")
    in_specs = (
        P("dp", features),
        P("dp", features),
        P("dp"),
        P("dp"),
        P("dp"),
        P(features),
        P(features),
        P("branch", None, "tensor"),
        P("tensor", "branch"),
        P("branch", "tensor"),
        P("tensor"),
        P("tensor", "branch"),
        P(features),
    )
    out_specs = (
        P("dp", features),
        P("dp", features),
        P(features),
        P(features),
        P("branch", None, "tensor"),
        P("tensor", "branch"),
        P("branch", "tensor"),
        P("tensor"),
        P("tensor", "branch"),
        P(features),
    )
    return jax.shard_map(
        functools.partial(shards, mesh.shape["dp"]),
        mesh=mesh,
        in_specs=in_specs,
        out_specs=out_specs,
        check_vma=False,
    )
```

```python
import functools
import itertools

import jax
import jax.numpy as jnp
from jax import lax
from jax.experimental import pallas as pl
from jax.experimental.pallas import tpu as pltpu
from jax.sharding import PartitionSpec as P

HEAD_DIM = 64
ROTARY = 32
PAIR = 2 * HEAD_DIM
QB = 128
KC = 256
LONGEST = 1024
EPS = 1e-05
NEG = -1e30
F32 = jnp.float32
BF16 = jnp.bfloat16
SWAP = [(0, 1), (1, 0)]
GELU_A = 0.7978845608028654
GELU_B = 0.044715


def nn(a, b):
    return lax.dot_general(a, b, (((1,), (0,)), ((), ())), preferred_element_type=F32)


def nt(a, b):
    return lax.dot_general(a, b, (((1,), (1,)), ((), ())), preferred_element_type=F32)


def tn(a, b):
    return lax.dot_general(a, b, (((0,), (0,)), ((), ())), preferred_element_type=F32)


def partner(x, even):
    width = x.shape[1]
    return jnp.where(even, pltpu.roll(x, width - 1, 1), pltpu.roll(x, 1, 1))


def attention_kernel(
    pairs,
    most,
    span_ref,
    qkv_ref,
    dmix_ref,
    cos_ref,
    sin_ref,
    start_ref,
    normed_hbm,
    g_hbm,
    mixed_ref,
    dj_ref,
    near_ref,
    far_ref,
    q_s,
    qt_s,
    g_s,
    gt_s,
    k_s,
    v_s,
    kt_s,
    vt_s,
    s_s,
    d_s,
    p_s,
    e_s,
    dk_s,
    dv_s,
    normed_s,
    ct_s,
    arrived,
):
    fetch = [
        pltpu.make_async_copy(normed_hbm, normed_s, arrived.at[0]),
        pltpu.make_async_copy(g_hbm, ct_s, arrived.at[1]),
    ]
    for copy in fetch:
        copy.start()
    rows = qkv_ref.shape[0]
    width = pairs * PAIR
    lane = lax.broadcasted_iota(jnp.int32, (QB, PAIR), 1)
    even = lane % 2 == 0
    first = lane < HEAD_DIM
    top = lax.broadcasted_iota(jnp.int32, (PAIR, QB), 0) < HEAD_DIM
    scale = HEAD_DIM**-0.5

    for p in range(pairs):
        k_s[p, :QB, :] = jnp.zeros((QB, PAIR), BF16)
        v_s[p, :QB, :] = jnp.zeros((QB, PAIR), BF16)
        kt_s[p, :, :QB] = jnp.zeros((PAIR, QB), BF16)
        vt_s[p, :, :QB] = jnp.zeros((PAIR, QB), BF16)
        dk_s[p, :QB, :] = jnp.zeros((QB, PAIR), F32)
        dv_s[p, :QB, :] = jnp.zeros((QB, PAIR), F32)

    @pl.loop(0, rows // QB)
    def _(i):
        at = pl.ds(pl.multiple_of(i * QB, QB), QB)
        to = pl.ds(pl.multiple_of(i * QB + QB, QB), QB)
        for p in range(pairs):
            q = qkv_ref[at, p * PAIR : (p + 1) * PAIR].astype(F32)
            k = qkv_ref[at, width + p * PAIR : width + (p + 1) * PAIR]
            v = qkv_ref[at, 2 * width + p * PAIR : 2 * width + (p + 1) * PAIR]
            g = dmix_ref[at, p * PAIR : (p + 1) * PAIR].astype(F32)
            q_s[p, i, :QB, :] = jnp.where(first, q, 0.0).astype(BF16)
            q_s[p, i, QB:, :] = jnp.where(first, 0.0, q).astype(BF16)
            g_s[p, i, :QB, :] = jnp.where(first, g, 0.0).astype(BF16)
            g_s[p, i, QB:, :] = jnp.where(first, 0.0, g).astype(BF16)
            q, g = q.T, g.T
            qt_s[p, i, :, :QB] = jnp.where(top, q, 0.0).astype(BF16)
            qt_s[p, i, :, QB:] = jnp.where(top, 0.0, q).astype(BF16)
            gt_s[p, i, :, :QB] = jnp.where(top, g, 0.0).astype(BF16)
            gt_s[p, i, :, QB:] = jnp.where(top, 0.0, g).astype(BF16)
            k_s[p, to, :] = k
            v_s[p, to, :] = v
            kt_s[p, :, to] = k.astype(F32).T.astype(BF16)
            vt_s[p, :, to] = v.astype(F32).T.astype(BF16)
            dk_s[p, to, :] = jnp.zeros((QB, PAIR), F32)
            dv_s[p, to, :] = jnp.zeros((QB, PAIR), F32)

    key_slot = lax.broadcasted_iota(jnp.int32, (KC, 2 * QB), 0)
    query_slot = lax.broadcasted_iota(jnp.int32, (1, 2 * QB), 1) % QB

    def block(i, n):
        base = (i + 2) * QB - n * KC
        spots = [pl.ds(pl.multiple_of(base + j * KC, QB), KC) for j in range(n)]
        whole = pl.ds(pl.multiple_of(base, QB), n * KC)
        query = query_slot + (i * QB + QB - base)
        start = start_ref[i] + (QB - base)
        here = pl.ds(pl.multiple_of(i * QB, QB), QB)
        pr = range(pairs)
        peak = [None] * pairs
        for j in range(n):
            ok = (key_slot >= start - j * KC) & (key_slot <= query - j * KC)
            for p in pr:
                s = jnp.where(ok, nn(k_s[p, spots[j], :], qt_s[p, i]), NEG)
                s_s[p, j] = s
                m = jnp.max(s.reshape(KC // 8, 8, 2 * QB), axis=0)
                peak[p] = m if peak[p] is None else jnp.maximum(peak[p], m)
        for j in range(n):
            for p in pr:
                d_s[p, j] = nn(v_s[p, spots[j], :], gt_s[p, i])
        peak = [jnp.max(m, axis=0, keepdims=True) for m in peak]
        total = [0.0] * pairs
        delta = [0.0] * pairs
        for j in range(n):
            for p in pr:
                e = jnp.exp(s_s[p, j] - peak[p])
                s_s[p, j] = e
                total[p] += jnp.sum(e.reshape(KC // 8, 8, 2 * QB), axis=0)
                delta[p] += jnp.sum((e * d_s[p, j]).reshape(KC // 8, 8, 2 * QB), axis=0)
        inverse = [1.0 / jnp.sum(x, axis=0, keepdims=True) for x in total]
        delta = [jnp.sum(x, axis=0, keepdims=True) * r for x, r in zip(delta, inverse)]
        for j in range(n):
            for p in pr:
                prob = s_s[p, j] * inverse[p]
                p_s[p, j * KC : (j + 1) * KC, :] = prob.astype(BF16)
                e_s[p, j * KC : (j + 1) * KC, :] = (prob * (d_s[p, j] - delta[p])).astype(BF16)
        for p in pr:
            o = nn(vt_s[p, :, whole], p_s[p, : n * KC, :])
            mixed_ref[here, p * PAIR : (p + 1) * PAIR] = (
                jnp.where(top, o[:, :QB], o[:, QB:]).T.astype(BF16)
            )
            dv_s[p, whole, :] += nn(p_s[p, : n * KC, :], g_s[p, i])
            dk_s[p, whole, :] += nn(e_s[p, : n * KC, :], q_s[p, i])
            d = nn(kt_s[p, :, whole], e_s[p, : n * KC, :])
            d = (jnp.where(top, d[:, :QB], d[:, QB:]) * scale).T
            d = d * cos_ref[here, :] - partner(d, even) * sin_ref[here, :]
            dj_ref[here, p * PAIR : (p + 1) * PAIR] = d.astype(BF16)

    @pl.loop(0, rows // QB)
    def _(i):
        for n in range(1, most + 1):
            pl.when(span_ref[i] == n)(functools.partial(block, i, n))

    @pl.loop(0, rows // QB)
    def _(i):
        at = pl.ds(pl.multiple_of(i * QB, QB), QB)
        to = pl.ds(pl.multiple_of(i * QB + QB, QB), QB)
        cosines = cos_ref[at, :]
        sines = sin_ref[at, :]
        for p in range(pairs):
            d = dk_s[p, to, :]
            d = d * cosines - partner(d, even) * sines
            dj_ref[at, width + p * PAIR : width + (p + 1) * PAIR] = d.astype(BF16)
            dj_ref[at, 2 * width + p * PAIR : 2 * width + (p + 1) * PAIR] = dv_s[p, to, :].astype(
                BF16
            )

    for copy in fetch:
        copy.wait()
    half, split = near_ref.shape[0], 3 * width
    for at, out in ((slice(half, 2 * half), far_ref), (slice(0, half), near_ref)):
        out[:, :split] = tn(normed_s[:, at], dj_ref[...]).astype(BF16)
        out[:, split:] = tn(ct_s[:, at], mixed_ref[...]).astype(BF16)


def attention(qkv, dmix, normed, g_all, cosines, sines, positions, pair):
    rows = qkv.shape[0]
    pairs = 1
    blocks = rows // QB
    padded = rows + QB
    most = LONGEST // KC + 1
    start = (jnp.arange(rows, dtype=jnp.int32) - positions).reshape(blocks, 1, QB)
    span = (jnp.arange(blocks, dtype=jnp.int32) - start[:, 0, 0] // QB + 2) // 2
    start = jnp.concatenate([start, start], axis=2)
    half, split = normed.shape[1] // 2, 3 * pairs * PAIR
    vmem = pl.BlockSpec(memory_space=pltpu.VMEM)
    return pl.pallas_call(
        functools.partial(attention_kernel, pairs, most),
        grid=(1,),
        out_shape=(
            jax.ShapeDtypeStruct((rows, pairs * PAIR), BF16),
            jax.ShapeDtypeStruct((rows, 3 * pairs * PAIR), BF16),
            jax.ShapeDtypeStruct((half, split + pairs * PAIR), BF16),
            jax.ShapeDtypeStruct((half, split + pairs * PAIR), BF16),
        ),
        in_specs=[
            pl.BlockSpec(memory_space=pltpu.SMEM),
            pl.BlockSpec((rows, 3 * pairs * PAIR), lambda i: (0, pair)),
            pl.BlockSpec((rows, pairs * PAIR), lambda i: (0, pair)),
            vmem,
            vmem,
            vmem,
            pl.BlockSpec(memory_space=pl.ANY),
            pl.BlockSpec(memory_space=pl.ANY),
        ],
        out_specs=(
            pl.BlockSpec((rows, pairs * PAIR), lambda i: (0, 0)),
            pl.BlockSpec((rows, 3 * pairs * PAIR), lambda i: (0, 0)),
            vmem,
            vmem,
        ),
        scratch_shapes=[
            pltpu.VMEM((pairs, blocks, 2 * QB, PAIR), BF16),
            pltpu.VMEM((pairs, blocks, PAIR, 2 * QB), BF16),
            pltpu.VMEM((pairs, blocks, 2 * QB, PAIR), BF16),
            pltpu.VMEM((pairs, blocks, PAIR, 2 * QB), BF16),
            pltpu.VMEM((pairs, padded, PAIR), BF16),
            pltpu.VMEM((pairs, padded, PAIR), BF16),
            pltpu.VMEM((pairs, PAIR, padded), BF16),
            pltpu.VMEM((pairs, PAIR, padded), BF16),
            pltpu.VMEM((pairs, most, KC, 2 * QB), F32),
            pltpu.VMEM((pairs, most, KC, 2 * QB), F32),
            pltpu.VMEM((pairs, most * KC, 2 * QB), BF16),
            pltpu.VMEM((pairs, most * KC, 2 * QB), BF16),
            pltpu.VMEM((pairs, padded, PAIR), F32),
            pltpu.VMEM((pairs, padded, PAIR), F32),
            pltpu.VMEM(normed.shape, BF16),
            pltpu.VMEM(g_all.shape, BF16),
            pltpu.SemaphoreType.DMA((2,)),
        ],
        compiler_params=pltpu.CompilerParams(vmem_limit_bytes=40 << 20),
        cost_estimate=pl.CostEstimate(
            flops=0, bytes_accessed=0, transcendentals=0
        ),
        name="attention",
    )(span, qkv, dmix, cosines, sines, start, normed, g_all)


def picked(first, own, got, far_own, far_got):
    own, got, far_own, far_got = (v[...].astype(F32) for v in (own, got, far_own, far_got))
    return jnp.concatenate(
        [
            jnp.where(first, own, got),
            jnp.where(first, got, own),
            jnp.where(first, far_own, far_got),
            jnp.where(first, far_got, far_own),
        ],
        1,
    )


def resident(shape):
    return pl.BlockSpec(shape, lambda i: (0,) * len(shape), pipeline_mode=pl.Buffered(1))


def enter_kernel(
    ids,
    own,
    got,
    far_own,
    far_got,
    aux_ref,
    near_q,
    far_q,
    near_u,
    far_u,
    bias_ref,
    cos_ref,
    sin_ref,
    normed_ref,
    active_ref,
    slope_ref,
    qkv_ref,
    stat_ref,
):
    x = picked(ids[0] == 0, own, got, far_own, far_got)
    rows, full = x.shape
    half = full // 2
    mean = jnp.mean(x, axis=1, keepdims=True)
    center = x - mean
    inv_root = lax.rsqrt(jnp.mean(center * center, axis=1, keepdims=True) + EPS)
    normed = (
        center * inv_root * aux_ref[0:1, :].astype(F32) + aux_ref[1:2, :].astype(F32)
    ).astype(BF16)
    normed_ref[...] = normed
    lane = lax.broadcasted_iota(jnp.int32, (rows, PAIR), 1)
    stat_ref[...] = jnp.where(lane == 0, mean, inv_root)
    near, far = normed[:, :half], normed[:, half:]
    hidden = nn(near, near_u[...]) + nn(far, far_u[...]) + bias_ref[0:1, :].astype(F32)
    square = hidden * hidden
    bend = jnp.tanh(GELU_A * hidden * (1.0 + GELU_B * square))
    up = 0.5 * (1.0 + bend)
    active = (hidden * up).astype(BF16)
    active_ref[...] = active
    slope_ref[...] = up + (0.5 * GELU_A) * hidden * (1.0 - bend * bend) * (
        1.0 + 3.0 * GELU_B * square
    )
    even = lane % 2 == 0
    cosines, sines = cos_ref[...], sin_ref[...]
    for j in range(3):
        joint = nn(near, near_q[j]) + nn(far, far_q[j])
        for p in range(joint.shape[1] // PAIR):
            v = joint[:, p * PAIR : (p + 1) * PAIR]
            if j < 2:
                v = v * cosines + partner(v, even) * sines
            if j == 0:
                v = v * HEAD_DIM**-0.5
            at = (3 * p + j) * PAIR
            qkv_ref[:, at : at + PAIR] = v.astype(BF16)


def rows_of(step, width):
    return pl.BlockSpec((step, width), lambda i, ids: (i, 0))


def fixed(shape, index=None):
    if index is None:
        return pl.BlockSpec(
            shape, lambda i, ids: (0,) * len(shape), pipeline_mode=pl.Buffered(1)
        )
    return pl.BlockSpec(shape, lambda i, ids: index(ids), pipeline_mode=pl.Buffered(1))


def by_rows(kernel, steps, ids, ins, outs, name, scratch=()):
    return pl.pallas_call(
        kernel,
        grid_spec=pltpu.PrefetchScalarGridSpec(
            num_scalar_prefetch=1,
            grid=(steps,),
            in_specs=[s for _, s in ins],
            out_specs=[s for _, _, s in outs],
            scratch_shapes=scratch,
        ),
        out_shape=[jax.ShapeDtypeStruct(s, d) for s, d, _ in outs],
        compiler_params=pltpu.CompilerParams(vmem_limit_bytes=50 << 20),
        cost_estimate=pl.CostEstimate(flops=0, bytes_accessed=0, transcendentals=0),
        name=name,
    )(ids, *[a for a, _ in ins])


def enter(ids, pieces, aux, w_three, far_q, w_up, far_u, bias, cosines, sines):
    rows, quarter = pieces[0].shape
    full, half = 4 * quarter, 2 * quarter
    units, heads_w = far_u.shape[1], far_q.shape[2]
    step = rows // 8
    ins = [(v, rows_of(step, quarter)) for v in pieces] + [
        (aux, fixed(aux.shape)),
        (w_three, fixed((3, half, heads_w), lambda ids: (0, 0, ids[1]))),
        (far_q, fixed(far_q.shape)),
        (w_up, fixed((half, units), lambda ids: (0, ids[1]))),
        (far_u, fixed(far_u.shape)),
        (bias, fixed((1, units), lambda ids: (0, ids[1]))),
        (cosines, rows_of(step, PAIR)),
        (sines, rows_of(step, PAIR)),
    ]
    outs = [
        ((rows, full), BF16, rows_of(step, full)),
        ((rows, units), BF16, rows_of(step, units)),
        ((rows, units), F32, rows_of(step, units)),
        ((rows, 3 * heads_w), BF16, rows_of(step, 3 * heads_w)),
        ((rows, PAIR), F32, rows_of(step, PAIR)),
    ]
    return by_rows(enter_kernel, 8, ids, ins, outs, "enter")


def down_kernel(
    ids,
    own,
    got,
    far_own,
    far_got,
    active_ref,
    near_a,
    far_a,
    g_ref,
    dm_ref,
    near_ref,
    far_ref,
    total_s,
):
    i = pl.program_id(0)
    g = picked(ids[0] == 0, own, got, far_own, far_got).astype(BF16)
    half = g.shape[1] // 2
    g_ref[...] = g
    dm_ref[...] = (nt(g[:, :half], near_a[...]) + nt(g[:, half:], far_a[...])).astype(BF16)

    @pl.when(i == 0)
    def _():
        total_s[...] = tn(active_ref[...], g)

    @pl.when(i > 0)
    def _():
        total_s[...] += tn(active_ref[...], g)

    @pl.when(i == pl.num_programs(0) - 1)
    def _():
        near_ref[...] = total_s[:, :half].astype(BF16)
        far_ref[...] = total_s[:, half:].astype(BF16)


def down_grads(ids, pieces, active, w_attn_out, far_a):
    rows, quarter = pieces[0].shape
    full, half, units = 4 * quarter, 2 * quarter, active.shape[1]
    heads_w = far_a.shape[0]
    step = rows // 4
    ins = [(v, rows_of(step, quarter)) for v in pieces] + [
        (active, rows_of(step, units)),
        (w_attn_out, fixed((heads_w, half), lambda ids: (ids[1], 0))),
        (far_a, fixed(far_a.shape)),
    ]
    outs = [
        ((rows, full), BF16, rows_of(step, full)),
        ((rows, heads_w), BF16, rows_of(step, heads_w)),
        ((units, half), BF16, fixed((units, half))),
        ((units, half), BF16, fixed((units, half))),
    ]
    return by_rows(
        down_kernel,
        4,
        ids,
        ins,
        outs,
        "down_grads",
        [pltpu.VMEM((units, full), F32)],
    )


def up_kernel(
    ids,
    g_ref,
    normed_ref,
    slope_ref,
    near_d,
    far_d,
    dh_ref,
    near_ref,
    far_ref,
    sum_ref,
    total_s,
):
    i = pl.program_id(0)
    half = g_ref.shape[1] // 2
    da = nt(g_ref[:, :half], near_d[...]) + nt(g_ref[:, half:], far_d[...])
    dh = (da * slope_ref[...]).astype(BF16)
    dh_ref[...] = dh
    sums = jnp.sum(dh.astype(F32), axis=0, keepdims=True)

    @pl.when(i == 0)
    def _():
        total_s[...] = tn(normed_ref[...], dh)
        sum_ref[...] = sums

    @pl.when(i > 0)
    def _():
        total_s[...] += tn(normed_ref[...], dh)
        sum_ref[...] += sums

    @pl.when(i == pl.num_programs(0) - 1)
    def _():
        near_ref[...] = total_s[:half, :].astype(BF16)
        far_ref[...] = total_s[half:, :].astype(BF16)


def up_grads(ids, g_all, normed, slope, w_down, far_d):
    rows, full = g_all.shape
    half, units = full // 2, slope.shape[1]
    step = rows // 4
    ins = [
        (g_all, rows_of(step, full)),
        (normed, rows_of(step, full)),
        (slope, rows_of(step, units)),
        (w_down, fixed((units, half), lambda ids: (ids[1], 0))),
        (far_d, fixed(far_d.shape)),
    ]
    outs = [
        ((rows, units), BF16, rows_of(step, units)),
        ((half, units), BF16, fixed((half, units))),
        ((half, units), BF16, fixed((half, units))),
        ((1, units), F32, fixed((1, units))),
    ]
    return by_rows(
        up_kernel,
        4,
        ids,
        ins,
        outs,
        "up_grads",
        [pltpu.VMEM((full, units), F32)],
    )


def leave_kernel(
    ids,
    own,
    got,
    far_own,
    far_got,
    stat_ref,
    aux_ref,
    dj0_ref,
    dj1_ref,
    dh_ref,
    near_q,
    far_q,
    near_u,
    far_u,
    mixed0_ref,
    mixed1_ref,
    near_a,
    far_a,
    active_ref,
    near_d,
    far_d,
    near_ref,
    far_ref,
    row_ref,
    sum_ref,
    term_near,
    term_far,
):
    i = pl.program_id(0)
    mixed = jnp.concatenate([mixed0_ref[...], mixed1_ref[...]], 1)
    active = active_ref[...]
    term_near[...] = nn(active, near_d[...]) + nn(mixed, near_a[...])
    term_far[...] = (nn(active, far_d[...]) + nn(mixed, far_a[...])).astype(BF16)
    x = picked(ids[0] == 0, own, got, far_own, far_got)
    unit = (x - stat_ref[:, 0:1]) * stat_ref[:, 1:2]
    dh = dh_ref[...]
    near = nt(dh, near_u[...])
    far = nt(dh, far_u[...])
    for j in range(3):
        cut = slice(j * PAIR, (j + 1) * PAIR)
        dj = jnp.concatenate([dj0_ref[:, cut], dj1_ref[:, cut]], 1)
        near += nt(dj, near_q[j])
        far += nt(dj, far_q[j])
    near_ref[...] = near
    far_ref[...] = far.astype(BF16)
    both = jnp.concatenate([near, far], 1)
    scaled = both * aux_ref[0:1, :].astype(F32)
    first = jnp.sum(scaled, axis=1, keepdims=True)
    second = jnp.sum(scaled * unit, axis=1, keepdims=True)
    lane = lax.broadcasted_iota(jnp.int32, (x.shape[0], PAIR), 1)
    row_ref[0] = jnp.where(lane == 0, first, second).T[:8]
    sums = jnp.concatenate(
        [
            jnp.sum(both * unit, axis=0, keepdims=True),
            jnp.sum(both, axis=0, keepdims=True),
        ],
        0,
    )

    @pl.when(i == 0)
    def _():
        sum_ref[...] = sums

    @pl.when(i > 0)
    def _():
        sum_ref[...] += sums


def leave(
    ids,
    pieces,
    stat,
    aux,
    d_joints,
    d_hidden,
    w_three,
    far_q,
    w_up,
    far_u,
    mixed,
    w_attn_out,
    far_a,
    active,
    w_down,
    far_d,
):
    rows, quarter = pieces[0].shape
    full, half = 4 * quarter, 2 * quarter
    units, heads_w = far_u.shape[1], far_q.shape[2]
    step = rows // 4
    ins = (
        [(v, rows_of(step, quarter)) for v in pieces]
        + [(stat, rows_of(step, PAIR)), (aux, fixed(aux.shape))]
        + [(d, rows_of(step, 3 * PAIR)) for d in d_joints]
        + [
            (d_hidden, rows_of(step, units)),
            (w_three, fixed((3, half, heads_w), lambda ids: (0, 0, ids[1]))),
            (far_q, fixed(far_q.shape)),
            (w_up, fixed((half, units), lambda ids: (0, ids[1]))),
            (far_u, fixed(far_u.shape)),
        ]
        + [(m, rows_of(step, PAIR)) for m in mixed]
        + [
            (w_attn_out, fixed((heads_w, half), lambda ids: (ids[1], 0))),
            (far_a, fixed(far_a.shape)),
            (active, rows_of(step, units)),
            (w_down, fixed((units, half), lambda ids: (ids[1], 0))),
            (far_d, fixed(far_d.shape)),
        ]
    )
    outs = [
        ((rows, half), F32, rows_of(step, half)),
        ((rows, half), BF16, rows_of(step, half)),
        ((4, 8, step), F32, pl.BlockSpec((1, 8, step), lambda i, ids: (i, 0, 0))),
        ((2, full), F32, fixed((2, full))),
        ((rows, half), F32, rows_of(step, half)),
        ((rows, half), BF16, rows_of(step, half)),
    ]
    return by_rows(leave_kernel, 4, ids, ins, outs, "leave")


def rotary_tables(positions):
    lane = jnp.arange(PAIR, dtype=jnp.int32)
    feature = lane % HEAD_DIM
    inverse = 10000.0 ** (-(2.0 * (feature // 2).astype(F32)) / ROTARY)
    angle = positions.astype(F32)[:, None] * inverse[None, :]
    turned = (feature < ROTARY)[None, :]
    sign = jnp.where(feature % 2 == 0, -1.0, 1.0)[None, :]
    cosines = jnp.where(turned, jnp.cos(angle), 1.0)
    sines = jnp.where(turned, jnp.sin(angle) * sign, 0.0)
    return cosines, sines


class Chain:
    held = ("value", "other", "far")

    def __init__(self, value, far, size, x_id, place):
        self.low, self.place = x_id == 0, place
        self.value, self.far, self.keep = jnp.where(self.low, far, value), far, value
        self.moving = self.other = self.crossed = None
        line = size // 2
        steps = line // 2 - 1

        def perm(pairs):
            return [(2 * i + x, 2 * j + x) for i, j in pairs for x in range(2)]

        self.pair = [(i, i ^ 1) for i in range(size)]
        self.hops = [(self.pair, None)]
        if line > 1:
            for k in range(steps):
                self.hops.append((perm([(k, k + 1), (line - 1 - k, line - 2 - k)]), None))
            mid = line // 2
            self.hops.append((perm([(mid - 1, mid), (mid, mid - 1)]), None))
            for k in reversed(range(steps)):
                self.hops.append((perm([(k + 1, k), (line - 2 - k, line - 1 - k)]), (k, line - 1 - k)))
        self.hops.append((self.pair, None))
        self.stage = 0
        self.cross = [
            (2 * i + c, 2 * (i ^ 1) + (c if i % 2 else 1 - c)) for i in range(size) for c in range(2)
        ]
        self.trade = [(2 * i + c, 2 * i + 1 - c) for i in range(1, size, 2) for c in range(2)]

    def busy(self):
        return self.stage < len(self.hops)

    def start(self):
        if self.stage == 0:
            self.moving = lax.ppermute(self.value, ("dp", "branch"), self.cross)
            self.crossed = lax.ppermute(self.far, ("dp", "branch"), self.trade)
        else:
            self.moving = lax.ppermute(self.value, "dp", self.hops[self.stage][0])

    def finish(self):
        got, self.moving = self.moving, None
        ends = self.hops[self.stage][1]
        if self.stage == len(self.hops) - 1:
            self.other = got
        elif ends is None:
            base = self.value
            if self.stage == 0:
                base = jnp.where(self.low, self.keep, self.crossed)
            self.value = (base.astype(F32) + got.astype(F32)).astype(base.dtype)
        else:
            here = (self.place == ends[0]) | (self.place == ends[1])
            self.value = jnp.where(here, got, self.value)
        self.far = None
        self.stage += 1

    def pieces(self):
        return (self.value, self.other)


class Scatter:
    held = ("value", "near")
    hops = (0, 1)

    def __init__(self, near, far, t):
        self.near, self.value, self.low = near, far, t == 0
        self.moving = self.far = None
        self.stage = 0

    def busy(self):
        return self.stage < 2

    def start(self):
        self.moving = lax.ppermute(self.value, ("branch", "tensor")[self.stage], SWAP)

    def finish(self):
        got, self.moving = self.moving, None
        if self.stage == 0:
            total = self.near + got.astype(F32)
            low, high = jnp.split(total, 2, axis=1)
            self.value = jnp.where(self.low, high, low).astype(BF16)
            self.near = jnp.where(self.low, low, high)
        else:
            self.near = self.near + got.astype(F32)
        self.stage += 1


class Steps:
    def __init__(self):
        self.before = []

    def run(self, finish, start, compute=None, *operands, extra=None):
        for c in finish:
            c.finish()
        if extra is not None:
            chain, rows = extra
            chain.value = jnp.concatenate([chain.value, rows.astype(BF16)], 0)
        touched = list({id(c): c for c in [*finish, *start]}.values())
        held = [(c, name) for c in touched for name in c.held if getattr(c, name) is not None]
        values, operands, _ = lax.optimization_barrier(
            ([getattr(c, name) for c, name in held], operands, self.before)
        )
        for (c, name), v in zip(held, values):
            setattr(c, name, v)
        for c in start:
            c.start()
        out = compute(*operands) if compute is not None else ()
        self.before = list(out)
        return out


def place_kernel(emit, count, flag_ref, *refs):
    own, other, outs = refs[:count], refs[count : 2 * count], refs[2 * count :]
    k, s = pl.program_id(0), pl.program_id(1)
    for c in range(count):
        pl.when((s == c) & (k == flag_ref[0]))(functools.partial(emit, own[c], outs))
        pl.when((s == c) & (k != flag_ref[0]))(functools.partial(emit, other[c], outs))


def place(emit, flag, pieces, out_shapes, out_blocks, maps, name):
    count = len(pieces)
    arrays = [p[0] for p in pieces] + [p[1] for p in pieces]
    grid_spec = pltpu.PrefetchScalarGridSpec(
        num_scalar_prefetch=1,
        grid=(2, count),
        in_specs=[pl.BlockSpec(a.shape, lambda k, s, f: (0, 0)) for a in arrays],
        out_specs=[pl.BlockSpec(blk, m) for blk, m in zip(out_blocks, maps)],
    )
    return pl.pallas_call(
        functools.partial(place_kernel, emit, count),
        grid_spec=grid_spec,
        out_shape=[jax.ShapeDtypeStruct(o, F32) for o in out_shapes],
        compiler_params=pltpu.CompilerParams(vmem_limit_bytes=48 << 20),
        cost_estimate=pl.CostEstimate(
            flops=0, bytes_accessed=6 * 2 * count * arrays[0].size, transcendentals=0
        ),
        name=name,
    )(flag.reshape(1).astype(jnp.int32), *arrays)


def emit_plain(src, outs):
    outs[0][...] = src[...].astype(F32)


def emit_late(src, outs):
    rows = outs[0].shape[1]
    for j in range(3):
        outs[0][j] = src[:rows, j * PAIR : (j + 1) * PAIR].astype(F32)
    outs[1][...] = src[:rows, 3 * PAIR :].astype(F32).T


def shards(
    dp_size,
    inputs,
    cotangent,
    seg_ids,
    pad_mask,
    positions,
    ln_gain,
    ln_bias,
    w_qkv,
    w_attn_out,
    w_up,
    b_up,
    w_down,
    b_down,
):
    b = lax.axis_index("branch")
    t = lax.axis_index("tensor")
    dp = lax.axis_index("dp")
    x_id, ring_id = lax.rem(dp, 2), dp // 2
    rows, quarter = inputs.shape
    half = 2 * quarter
    full = 4 * quarter
    heads_w = w_qkv.shape[2] // 2
    units = w_up.shape[1] // 2
    ids = jnp.stack([t, b]).astype(jnp.int32)

    def over_branch(v):
        return lax.ppermute(v, "branch", SWAP)

    def over_tensor(v):
        return lax.ppermute(v, "tensor", SWAP)

    def part(w, axis, index, size):
        return lax.dynamic_slice_in_dim(w, index * size, size, axis)

    x_got, x_far = over_tensor(inputs), over_branch(inputs)
    g_own, _ = lax.optimization_barrier((cotangent, x_far))
    g_got = over_tensor(g_own)
    aux = jnp.concatenate([ln_gain[None], ln_bias[None], jnp.zeros((14, quarter), BF16)], 0)
    aux_got = over_tensor(aux)
    w_three = jnp.transpose(w_qkv, (1, 0, 2))
    far_q = over_branch(part(w_three, 2, 1 - b, heads_w))
    far_u = over_branch(part(w_up, 1, 1 - b, units))
    bias_up = b_up.reshape(1, 2 * units)
    cosines, sines = rotary_tables(positions)
    aux_got, cosines, sines = lax.optimization_barrier((aux_got, cosines, sines))
    aux_half = jnp.where(
        t == 0, jnp.concatenate([aux, aux_got], 1), jnp.concatenate([aux_got, aux], 1)
    )
    aux_all = jnp.concatenate([aux_half, over_branch(aux_half)], 1)
    (x_got, x_far, aux_all, far_q, far_u, bias_up, cosines, sines) = lax.optimization_barrier(
        (x_got, x_far, aux_all, far_q, far_u, bias_up, cosines, sines)
    )
    x_pieces = (inputs, x_got, x_far, over_branch(x_got))
    normed, active, slope, qkv, stat = enter(
        ids, x_pieces, aux_all, w_three, far_q, w_up, far_u, bias_up, cosines, sines
    )
    g_far = over_branch(cotangent)
    far_a = over_branch(part(w_attn_out, 0, 1 - b, heads_w))
    far_d = over_branch(part(w_down, 0, 1 - b, units))
    g_got, g_far, far_a, far_d, active = lax.optimization_barrier(
        (g_got, g_far, far_a, far_d, active)
    )
    g_pieces = (cotangent, g_got, g_far, over_branch(g_got))
    g_all, d_mixed, down_near, down_send = down_grads(ids, g_pieces, active, w_attn_out, far_a)

    def chained(near, far):
        return Chain(near, far, dp_size, x_id, ring_id)

    def attend(pair):
        return lambda *v: attention(*v, cosines, sines, positions, pair)

    steps = Steps()
    down = chained(down_near, down_send)
    d_hidden, up_near, up_send, bup = steps.run(
        [], [down], lambda *v: up_grads(ids, *v, w_down, far_d), g_all, normed, slope
    )
    up = chained(up_near, up_send)
    mixed0, d_joint0, near0, send0 = steps.run(
        [down], [up, down], attend(0), qkv, d_mixed, normed, g_all
    )
    late0 = chained(near0, send0)
    mixed1, d_joint1, near1, send1 = steps.run(
        [up, down], [late0, down, up], attend(1), qkv, d_mixed, normed, g_all
    )
    late1 = chained(near1, send1)

    def finish(ac, m0, m1, dj0, dj1, dh):
        return leave(
            ids,
            x_pieces,
            stat,
            aux_all,
            (dj0, dj1),
            dh,
            w_three,
            far_q,
            w_up,
            far_u,
            (m0, m1),
            w_attn_out,
            far_a,
            ac,
            w_down,
            far_d,
        )

    d_near, d_far, row_sums, sums, term_near, term_far = steps.run(
        [late0, down, up],
        [late1, late0, down, up],
        finish,
        active,
        mixed0,
        mixed1,
        d_joint0,
        d_joint1,
        d_hidden,
    )
    g_float = cotangent.astype(F32)
    terms, grads = Scatter(term_near, term_far, t), Scatter(d_near, d_far, t)
    moving = [late1, late0, down, up]

    def spread(rs):
        return (rs + over_branch(rs),)

    chains = [down, up, late1, late0]
    small = jnp.concatenate(
        [
            sums.reshape(4, half),
            bup.reshape(units // half, half),
            jnp.pad(jnp.sum(g_float, axis=0), (0, quarter))[None],
            jnp.zeros((9, half), F32),
        ]
    )
    (row_sums,) = steps.run(
        chains,
        [*(c for c in chains if c.stage + 1 < len(c.hops)), terms, grads],
        spread,
        row_sums,
        extra=(late1, small),
    )
    flag = b ^ x_id
    gradients = {}

    def lay(*operands):
        if down.other is not None and "down" not in gradients:
            gradients["down"] = place(
                emit_plain,
                flag,
                [down.pieces()],
                [(2 * units, half)],
                [(units, half)],
                [lambda k, s, f: (k, 0)],
                "place_down",
            )[0]
        if up.other is not None and "up" not in gradients:
            gradients["up"] = place(
                emit_plain,
                flag,
                [up.pieces()],
                [(half, 2 * units)],
                [(half, units)],
                [lambda k, s, f: (0, k)],
                "place_up",
            )[0]
        return [v + over_tensor(v) for v in operands]

    for turn in itertools.count(1):
        begin = [terms if turn == 1 else grads]
        operands = [row_sums] if turn == 1 else []
        moving = [c for c in (*chains, terms, grads) if c.moving is not None]
        ready = [c for c in (*chains, *begin) if c.stage + (c in moving) < len(c.hops)]
        if turn > 2 and not ready:
            break
        out = steps.run(moving, ready, lay, *operands)
        if turn == 1:
            (row_sums,) = out
    for c in (*chains, terms, grads):
        if c.moving is not None:
            c.finish()
    lay()

    row_sums = row_sums * (1.0 / full)
    output = (inputs.astype(F32) + terms.near + b_down.astype(F32)).astype(BF16)
    d_own = grads.near
    mean, inv_root = stat[:, 0:1], stat[:, 1:2]
    unit_own = (inputs.astype(F32) - mean) * inv_root
    input_grad = g_float + inv_root * (
        d_own * ln_gain.astype(F32)
        - row_sums[:, 0, :].reshape(rows, 1)
        - unit_own * row_sums[:, 1, :].reshape(rows, 1)
    )
    small = late1.value[half : half + 8].astype(F32) + late1.other[half : half + 8].astype(F32)
    sums = small[:4].reshape(2, full)
    own = part(sums, 1, t, quarter)
    for k, v in (
        (1, part(sums, 1, 1 - t, quarter)),
        (2, part(sums, 1, 2 + t, quarter)),
        (3, part(sums, 1, 3 - t, quarter)),
    ):
        own = own + lax.ppermute(v, ("branch", "tensor"), [(i, i ^ k) for i in range(4)])
    bup = small[4:6].reshape(units)
    bup_far = over_branch(bup)
    grad_bup = jnp.where(b == 0, jnp.concatenate([bup, bup_far]), jnp.concatenate([bup_far, bup]))

    grad_qkv, grad_aout = place(
        emit_late,
        flag,
        [c.pieces() for c in (late0, late1)],
        [(3, half, 2 * heads_w), (2 * heads_w, half)],
        [(3, half, PAIR), (PAIR, half)],
        [lambda k, s, f: (0, 0, 2 * k + s), lambda k, s, f: (2 * k + s, 0)],
        "place_late",
    )
    return (
        output,
        input_grad,
        own[0],
        own[1],
        jnp.transpose(grad_qkv, (1, 0, 2)),
        grad_aout,
        gradients["up"],
        grad_bup,
        gradients["down"],
        small[6, :quarter],
    )


def solution(mesh):
    features = ("branch", "tensor")
    in_specs = (
        P("dp", features),
        P("dp", features),
        P("dp"),
        P("dp"),
        P("dp"),
        P(features),
        P(features),
        P("branch", None, "tensor"),
        P("tensor", "branch"),
        P("branch", "tensor"),
        P("tensor"),
        P("tensor", "branch"),
        P(features),
    )
    out_specs = (
        P("dp", features),
        P("dp", features),
        P(features),
        P(features),
        P("branch", None, "tensor"),
        P("tensor", "branch"),
        P("branch", "tensor"),
        P("tensor"),
        P("tensor", "branch"),
        P(features),
    )
    return jax.shard_map(
        functools.partial(shards, mesh.shape["dp"]),
        mesh=mesh,
        in_specs=in_specs,
        out_specs=out_specs,
        check_vma=False,
    )
```

```python
import functools
import itertools

import jax
import jax.numpy as jnp
from jax import lax
from jax.experimental import pallas as pl
from jax.experimental.pallas import tpu as pltpu
from jax.sharding import PartitionSpec as P

HEAD_DIM = 64
ROTARY = 32
PAIR = 2 * HEAD_DIM
QB = 128
KC = 256
LONGEST = 1024
EPS = 1e-05
NEG = -1e30
F32 = jnp.float32
BF16 = jnp.bfloat16
SWAP = [(0, 1), (1, 0)]
GELU_A = 0.7978845608028654
GELU_B = 0.044715


def nn(a, b):
    return lax.dot_general(a, b, (((1,), (0,)), ((), ())), preferred_element_type=F32)


def nt(a, b):
    return lax.dot_general(a, b, (((1,), (1,)), ((), ())), preferred_element_type=F32)


def tn(a, b):
    return lax.dot_general(a, b, (((0,), (0,)), ((), ())), preferred_element_type=F32)


def partner(x, even):
    width = x.shape[1]
    return jnp.where(even, pltpu.roll(x, width - 1, 1), pltpu.roll(x, 1, 1))


def cols(pair, part):
    return slice((3 * pair + part) * PAIR, (3 * pair + part + 1) * PAIR)


def attention_kernel(
    pair,
    most,
    span_ref,
    start_ref,
    qkv_hbm,
    dmix_hbm,
    cos_hbm,
    sin_hbm,
    normed_hbm,
    g_hbm,
    mixed_ref,
    dj_ref,
    near_ref,
    far_ref,
    q_s,
    qt_s,
    g_s,
    gt_s,
    k_s,
    v_s,
    kt_s,
    vt_s,
    s_s,
    d_s,
    p_s,
    e_s,
    dk_s,
    dv_s,
    qkv_ref,
    dmix_ref,
    cos_ref,
    sin_ref,
    normed_s,
    ct_s,
    arrived,
):
    pairs = 1
    rows = qkv_ref.shape[0]
    fetch = [
        pltpu.make_async_copy(src, dst, arrived.at[n])
        for n, (src, dst) in enumerate(
            (
                (qkv_hbm.at[:, 3 * pair * PAIR : 3 * (pair + 1) * PAIR], qkv_ref),
                (dmix_hbm.at[:, pair * PAIR : (pair + 1) * PAIR], dmix_ref),
                (cos_hbm, cos_ref),
                (sin_hbm, sin_ref),
                (normed_hbm, normed_s),
                (g_hbm, ct_s),
            )
        )
    ]
    for copy in fetch:
        copy.start()
    fetch[0].wait()
    fetch[1].wait()
    rows = qkv_ref.shape[0]
    lane = lax.broadcasted_iota(jnp.int32, (QB, PAIR), 1)
    even = lane % 2 == 0
    first = lane < HEAD_DIM
    top = lax.broadcasted_iota(jnp.int32, (PAIR, QB), 0) < HEAD_DIM
    scale = HEAD_DIM**-0.5

    for p in range(pairs):
        k_s[p, :QB, :] = jnp.zeros((QB, PAIR), BF16)
        v_s[p, :QB, :] = jnp.zeros((QB, PAIR), BF16)
        kt_s[p, :, :QB] = jnp.zeros((PAIR, QB), BF16)
        vt_s[p, :, :QB] = jnp.zeros((PAIR, QB), BF16)
        dk_s[p, :QB, :] = jnp.zeros((QB, PAIR), F32)
        dv_s[p, :QB, :] = jnp.zeros((QB, PAIR), F32)

    @pl.loop(0, rows // QB)
    def _(i):
        at = pl.ds(pl.multiple_of(i * QB, QB), QB)
        to = pl.ds(pl.multiple_of(i * QB + QB, QB), QB)
        for p in range(pairs):
            q = qkv_ref[at, cols(p, 0)].astype(F32)
            k = qkv_ref[at, cols(p, 1)]
            v = qkv_ref[at, cols(p, 2)]
            g = dmix_ref[at, p * PAIR : (p + 1) * PAIR].astype(F32)
            q_s[p, i, :QB, :] = jnp.where(first, q, 0.0).astype(BF16)
            q_s[p, i, QB:, :] = jnp.where(first, 0.0, q).astype(BF16)
            g_s[p, i, :QB, :] = jnp.where(first, g, 0.0).astype(BF16)
            g_s[p, i, QB:, :] = jnp.where(first, 0.0, g).astype(BF16)
            q, g = q.T, g.T
            qt_s[p, i, :, :QB] = jnp.where(top, q, 0.0).astype(BF16)
            qt_s[p, i, :, QB:] = jnp.where(top, 0.0, q).astype(BF16)
            gt_s[p, i, :, :QB] = jnp.where(top, g, 0.0).astype(BF16)
            gt_s[p, i, :, QB:] = jnp.where(top, 0.0, g).astype(BF16)
            k_s[p, to, :] = k
            v_s[p, to, :] = v
            kt_s[p, :, to] = k.astype(F32).T.astype(BF16)
            vt_s[p, :, to] = v.astype(F32).T.astype(BF16)
            dk_s[p, to, :] = jnp.zeros((QB, PAIR), F32)
            dv_s[p, to, :] = jnp.zeros((QB, PAIR), F32)

    fetch[2].wait()
    fetch[3].wait()
    key_slot = lax.broadcasted_iota(jnp.int32, (KC, 2 * QB), 0)
    query_slot = lax.broadcasted_iota(jnp.int32, (1, 2 * QB), 1) % QB

    def block(i, n):
        base = (i + 2) * QB - n * KC
        spots = [pl.ds(pl.multiple_of(base + j * KC, QB), KC) for j in range(n)]
        whole = pl.ds(pl.multiple_of(base, QB), n * KC)
        query = query_slot + (i * QB + QB - base)
        start = start_ref[i] + (QB - base)
        here = pl.ds(pl.multiple_of(i * QB, QB), QB)
        pr = range(pairs)
        peak = [None] * pairs
        for j in range(n):
            ok = (key_slot >= start - j * KC) & (key_slot <= query - j * KC)
            for p in pr:
                s = jnp.where(ok, nn(k_s[p, spots[j], :], qt_s[p, i]), NEG)
                s_s[p, j] = s
                m = jnp.max(s.reshape(KC // 8, 8, 2 * QB), axis=0)
                peak[p] = m if peak[p] is None else jnp.maximum(peak[p], m)
        for j in range(n):
            for p in pr:
                d_s[p, j] = nn(v_s[p, spots[j], :], gt_s[p, i])
        peak = [jnp.max(m, axis=0, keepdims=True) for m in peak]
        total = [0.0] * pairs
        delta = [0.0] * pairs
        for j in range(n):
            for p in pr:
                e = jnp.exp(s_s[p, j] - peak[p])
                s_s[p, j] = e
                total[p] += jnp.sum(e.reshape(KC // 8, 8, 2 * QB), axis=0)
                delta[p] += jnp.sum((e * d_s[p, j]).reshape(KC // 8, 8, 2 * QB), axis=0)
        inverse = [1.0 / jnp.sum(x, axis=0, keepdims=True) for x in total]
        delta = [jnp.sum(x, axis=0, keepdims=True) * r for x, r in zip(delta, inverse)]
        for j in range(n):
            for p in pr:
                prob = s_s[p, j] * inverse[p]
                p_s[p, j * KC : (j + 1) * KC, :] = prob.astype(BF16)
                e_s[p, j * KC : (j + 1) * KC, :] = (prob * (d_s[p, j] - delta[p])).astype(BF16)
        for p in pr:
            o = nn(vt_s[p, :, whole], p_s[p, : n * KC, :])
            mixed_ref[here, p * PAIR : (p + 1) * PAIR] = (
                jnp.where(top, o[:, :QB], o[:, QB:]).T.astype(BF16)
            )
            dv_s[p, whole, :] += nn(p_s[p, : n * KC, :], g_s[p, i])
            dk_s[p, whole, :] += nn(e_s[p, : n * KC, :], q_s[p, i])
            d = nn(kt_s[p, :, whole], e_s[p, : n * KC, :])
            d = (jnp.where(top, d[:, :QB], d[:, QB:]) * scale).T
            d = d * cos_ref[here, :] - partner(d, even) * sin_ref[here, :]
            dj_ref[here, cols(p, 0)] = d.astype(BF16)

    @pl.loop(0, rows // QB)
    def _(i):
        for n in range(1, most + 1):
            pl.when(span_ref[i] == n)(functools.partial(block, i, n))

    @pl.loop(0, rows // QB)
    def _(i):
        at = pl.ds(pl.multiple_of(i * QB, QB), QB)
        to = pl.ds(pl.multiple_of(i * QB + QB, QB), QB)
        cosines = cos_ref[at, :]
        sines = sin_ref[at, :]
        for p in range(pairs):
            d = dk_s[p, to, :]
            d = d * cosines - partner(d, even) * sines
            dj_ref[at, cols(p, 1)] = d.astype(BF16)
            dj_ref[at, cols(p, 2)] = dv_s[p, to, :].astype(BF16)

    fetch[4].wait()
    fetch[5].wait()
    half, split = normed_s.shape[1] // 2, 3 * PAIR
    for p in range(pairs):
        at_p = p * 4 * PAIR
        for at, out in ((slice(half, 2 * half), far_ref), (slice(0, half), near_ref)):
            out[:half, at_p : at_p + split] = tn(
                normed_s[:, at], dj_ref[:, p * split : (p + 1) * split]
            ).astype(BF16)
            out[:half, at_p + split : at_p + 4 * PAIR] = tn(
                ct_s[:, at], mixed_ref[:, p * PAIR : (p + 1) * PAIR]
            ).astype(BF16)


def spans(positions):
    rows = positions.shape[0]
    blocks = rows // QB
    start = (jnp.arange(rows, dtype=jnp.int32) - positions).reshape(blocks, 1, QB)
    span = (jnp.arange(blocks, dtype=jnp.int32) - start[:, 0, 0] // QB + 2) // 2
    return span, jnp.concatenate([start, start], axis=2)


def attention(pair, qkv, dmix, normed, g_all, cosines, sines, span, start):
    rows = qkv.shape[0]
    blocks = rows // QB
    padded = rows + QB
    most = LONGEST // KC + 1
    half = normed.shape[1] // 2
    vmem = pl.BlockSpec(memory_space=pltpu.VMEM)
    smem = pl.BlockSpec(memory_space=pltpu.SMEM)
    return pl.pallas_call(
        functools.partial(attention_kernel, pair, most),
        out_shape=[
            jax.ShapeDtypeStruct((rows, PAIR), BF16),
            jax.ShapeDtypeStruct((rows, 3 * PAIR), BF16),
        ]
        + [jax.ShapeDtypeStruct((half, 4 * PAIR), BF16)] * 2,
        in_specs=[smem, vmem] + [pl.BlockSpec(memory_space=pl.ANY)] * 6,
        out_specs=[vmem] * 4,
        scratch_shapes=[
            pltpu.VMEM((1, blocks, 2 * QB, PAIR), BF16),
            pltpu.VMEM((1, blocks, PAIR, 2 * QB), BF16),
            pltpu.VMEM((1, blocks, 2 * QB, PAIR), BF16),
            pltpu.VMEM((1, blocks, PAIR, 2 * QB), BF16),
            pltpu.VMEM((1, padded, PAIR), BF16),
            pltpu.VMEM((1, padded, PAIR), BF16),
            pltpu.VMEM((1, PAIR, padded), BF16),
            pltpu.VMEM((1, PAIR, padded), BF16),
            pltpu.VMEM((1, most, KC, 2 * QB), F32),
            pltpu.VMEM((1, most, KC, 2 * QB), F32),
            pltpu.VMEM((1, most * KC, 2 * QB), BF16),
            pltpu.VMEM((1, most * KC, 2 * QB), BF16),
            pltpu.VMEM((1, padded, PAIR), F32),
            pltpu.VMEM((1, padded, PAIR), F32),
            pltpu.VMEM((rows, 3 * PAIR), BF16),
            pltpu.VMEM((rows, PAIR), BF16),
            pltpu.VMEM(cosines.shape, F32),
            pltpu.VMEM(sines.shape, F32),
            pltpu.VMEM(normed.shape, BF16),
            pltpu.VMEM(g_all.shape, BF16),
            pltpu.SemaphoreType.DMA((6,)),
        ],
        compiler_params=pltpu.CompilerParams(vmem_limit_bytes=40 << 20),
        cost_estimate=pl.CostEstimate(flops=0, bytes_accessed=0, transcendentals=0),
        name="attention",
    )(span, start, qkv, dmix, cosines, sines, normed, g_all)


def picked(first, own, got, far_own, far_got):
    own, got, far_own, far_got = (v[...].astype(F32) for v in (own, got, far_own, far_got))
    return jnp.concatenate(
        [
            jnp.where(first, own, got),
            jnp.where(first, got, own),
            jnp.where(first, far_own, far_got),
            jnp.where(first, far_got, far_own),
        ],
        1,
    )


def resident(shape):
    return pl.BlockSpec(shape, lambda i: (0,) * len(shape), pipeline_mode=pl.Buffered(1))


def enter_kernel(
    ids,
    own,
    got,
    far_own,
    far_got,
    aux_ref,
    near_q,
    far_q,
    near_u,
    far_u,
    bias_ref,
    cos_ref,
    sin_ref,
    normed_ref,
    active_ref,
    slope_ref,
    qkv_ref,
    stat_ref,
):
    x = picked(ids[0] == 0, own, got, far_own, far_got)
    rows, full = x.shape
    half = full // 2
    mean = jnp.mean(x, axis=1, keepdims=True)
    center = x - mean
    inv_root = lax.rsqrt(jnp.mean(center * center, axis=1, keepdims=True) + EPS)
    normed = (
        center * inv_root * aux_ref[0:1, :].astype(F32) + aux_ref[1:2, :].astype(F32)
    ).astype(BF16)
    normed_ref[...] = normed
    lane = lax.broadcasted_iota(jnp.int32, (rows, PAIR), 1)
    stat_ref[...] = jnp.where(lane == 0, mean, inv_root)
    near, far = normed[:, :half], normed[:, half:]
    hidden = nn(near, near_u[...]) + nn(far, far_u[...]) + bias_ref[0:1, :].astype(F32)
    square = hidden * hidden
    bend = jnp.tanh(GELU_A * hidden * (1.0 + GELU_B * square))
    up = 0.5 * (1.0 + bend)
    active = (hidden * up).astype(BF16)
    active_ref[...] = active
    slope_ref[...] = up + (0.5 * GELU_A) * hidden * (1.0 - bend * bend) * (
        1.0 + 3.0 * GELU_B * square
    )
    even = lane % 2 == 0
    cosines, sines = cos_ref[...], sin_ref[...]
    for j in range(3):
        joint = nn(near, near_q[j]) + nn(far, far_q[j])
        for p in range(joint.shape[1] // PAIR):
            v = joint[:, p * PAIR : (p + 1) * PAIR]
            if j < 2:
                v = v * cosines + partner(v, even) * sines
            if j == 0:
                v = v * HEAD_DIM**-0.5
            at = (3 * p + j) * PAIR
            qkv_ref[:, at : at + PAIR] = v.astype(BF16)


def rows_of(step, width):
    return pl.BlockSpec((step, width), lambda i, ids: (i, 0))


def fixed(shape, index=None):
    if index is None:
        return pl.BlockSpec(
            shape, lambda i, ids: (0,) * len(shape), pipeline_mode=pl.Buffered(1)
        )
    return pl.BlockSpec(shape, lambda i, ids: index(ids), pipeline_mode=pl.Buffered(1))


def by_rows(kernel, steps, ids, ins, outs, name, scratch=()):
    return pl.pallas_call(
        kernel,
        grid_spec=pltpu.PrefetchScalarGridSpec(
            num_scalar_prefetch=1,
            grid=(steps,),
            in_specs=[s for _, s in ins],
            out_specs=[s for _, _, s in outs],
            scratch_shapes=scratch,
        ),
        out_shape=[jax.ShapeDtypeStruct(s, d) for s, d, _ in outs],
        compiler_params=pltpu.CompilerParams(vmem_limit_bytes=50 << 20),
        cost_estimate=pl.CostEstimate(flops=0, bytes_accessed=0, transcendentals=0),
        name=name,
    )(ids, *[a for a, _ in ins])


def enter(ids, pieces, aux, w_three, far_q, w_up, far_u, bias, cosines, sines):
    rows, quarter = pieces[0].shape
    full, half = 4 * quarter, 2 * quarter
    units, heads_w = far_u.shape[1], far_q.shape[2]
    step = rows // 8
    ins = [(v, rows_of(step, quarter)) for v in pieces] + [
        (aux, fixed(aux.shape)),
        (w_three, fixed((3, half, heads_w), lambda ids: (0, 0, ids[1]))),
        (far_q, fixed(far_q.shape)),
        (w_up, fixed((half, units), lambda ids: (0, ids[1]))),
        (far_u, fixed(far_u.shape)),
        (bias, fixed((1, units), lambda ids: (0, ids[1]))),
        (cosines, rows_of(step, PAIR)),
        (sines, rows_of(step, PAIR)),
    ]
    outs = [
        ((rows, full), BF16, rows_of(step, full)),
        ((rows, units), BF16, rows_of(step, units)),
        ((rows, units), F32, rows_of(step, units)),
        ((rows, 3 * heads_w), BF16, rows_of(step, 3 * heads_w)),
        ((rows, PAIR), F32, rows_of(step, PAIR)),
    ]
    return by_rows(enter_kernel, 8, ids, ins, outs, "enter")


def down_kernel(
    ids,
    own,
    got,
    far_own,
    far_got,
    active_ref,
    g_ref,
    near_ref,
    far_ref,
    total_s,
):
    i = pl.program_id(0)
    g = picked(ids[0] == 0, own, got, far_own, far_got).astype(BF16)
    half = g.shape[1] // 2
    g_ref[...] = g

    @pl.when(i == 0)
    def _():
        total_s[...] = tn(active_ref[...], g)

    @pl.when(i > 0)
    def _():
        total_s[...] += tn(active_ref[...], g)

    @pl.when(i == pl.num_programs(0) - 1)
    def _():
        near_ref[...] = total_s[:, :half].astype(BF16)
        far_ref[...] = total_s[:, half:].astype(BF16)


def down_grads(ids, pieces, active):
    rows, quarter = pieces[0].shape
    full, half, units = 4 * quarter, 2 * quarter, active.shape[1]
    step = rows // 4
    ins = [(v, rows_of(step, quarter)) for v in pieces] + [
        (active, rows_of(step, units)),
    ]
    outs = [
        ((rows, full), BF16, rows_of(step, full)),
        ((units, half), BF16, fixed((units, half))),
        ((units, half), BF16, fixed((units, half))),
    ]
    return by_rows(
        down_kernel,
        4,
        ids,
        ins,
        outs,
        "down_grads",
        [pltpu.VMEM((units, full), F32)],
    )


def up_kernel(
    ids,
    g_ref,
    normed_ref,
    slope_ref,
    near_d,
    far_d,
    near_a,
    far_a,
    dh_ref,
    dm_ref,
    near_ref,
    far_ref,
    sum_ref,
    total_s,
):
    i = pl.program_id(0)
    half = g_ref.shape[1] // 2
    da = nt(g_ref[:, :half], near_d[...]) + nt(g_ref[:, half:], far_d[...])
    dm_ref[...] = (nt(g_ref[:, :half], near_a[...]) + nt(g_ref[:, half:], far_a[...])).astype(BF16)
    dh = (da * slope_ref[...]).astype(BF16)
    dh_ref[...] = dh
    sums = jnp.sum(dh.astype(F32), axis=0, keepdims=True)

    @pl.when(i == 0)
    def _():
        total_s[...] = tn(normed_ref[...], dh)
        sum_ref[...] = sums

    @pl.when(i > 0)
    def _():
        total_s[...] += tn(normed_ref[...], dh)
        sum_ref[...] += sums

    @pl.when(i == pl.num_programs(0) - 1)
    def _():
        near_ref[...] = total_s[:half, :].astype(BF16)
        far_ref[...] = total_s[half:, :].astype(BF16)


def up_grads(ids, g_all, normed, slope, w_down, far_d, w_attn_out, far_a):
    rows, full = g_all.shape
    half, units = full // 2, slope.shape[1]
    heads_w = far_a.shape[0]
    step = rows // 4
    ins = [
        (g_all, rows_of(step, full)),
        (normed, rows_of(step, full)),
        (slope, rows_of(step, units)),
        (w_down, fixed((units, half), lambda ids: (ids[1], 0))),
        (far_d, fixed(far_d.shape)),
        (w_attn_out, fixed((heads_w, half), lambda ids: (ids[1], 0))),
        (far_a, fixed(far_a.shape)),
    ]
    outs = [
        ((rows, units), BF16, rows_of(step, units)),
        ((rows, heads_w), BF16, rows_of(step, heads_w)),
        ((half, units), BF16, fixed((half, units))),
        ((half, units), BF16, fixed((half, units))),
        ((1, units), F32, fixed((1, units))),
    ]
    return by_rows(
        up_kernel,
        4,
        ids,
        ins,
        outs,
        "up_grads",
        [pltpu.VMEM((full, units), F32)],
    )


def leave_kernel(
    ids,
    own,
    got,
    far_own,
    far_got,
    stat_ref,
    aux_ref,
    dj0_ref,
    dj1_ref,
    dh_ref,
    near_q,
    far_q,
    near_u,
    far_u,
    mixed0_ref,
    mixed1_ref,
    near_a,
    far_a,
    active_ref,
    near_d,
    far_d,
    near_ref,
    far_ref,
    row_ref,
    sum_ref,
    term_near,
    term_far,
):
    i = pl.program_id(0)
    mixed = jnp.concatenate([mixed0_ref[...], mixed1_ref[...]], 1)
    active = active_ref[...]
    term_near[...] = nn(active, near_d[...]) + nn(mixed, near_a[...])
    term_far[...] = (nn(active, far_d[...]) + nn(mixed, far_a[...])).astype(BF16)
    x = picked(ids[0] == 0, own, got, far_own, far_got)
    unit = (x - stat_ref[:, 0:1]) * stat_ref[:, 1:2]
    dh = dh_ref[...]
    near = nt(dh, near_u[...])
    far = nt(dh, far_u[...])
    for j in range(3):
        cut = slice(j * PAIR, (j + 1) * PAIR)
        dj = jnp.concatenate([dj0_ref[:, cut], dj1_ref[:, cut]], 1)
        near += nt(dj, near_q[j])
        far += nt(dj, far_q[j])
    near_ref[...] = near
    far_ref[...] = far.astype(BF16)
    both = jnp.concatenate([near, far], 1)
    scaled = both * aux_ref[0:1, :].astype(F32)
    first = jnp.sum(scaled, axis=1, keepdims=True)
    second = jnp.sum(scaled * unit, axis=1, keepdims=True)
    lane = lax.broadcasted_iota(jnp.int32, (x.shape[0], PAIR), 1)
    row_ref[0] = jnp.where(lane == 0, first, second).T[:8]
    sums = jnp.concatenate(
        [
            jnp.sum(both * unit, axis=0, keepdims=True),
            jnp.sum(both, axis=0, keepdims=True),
        ],
        0,
    )

    @pl.when(i == 0)
    def _():
        sum_ref[...] = sums

    @pl.when(i > 0)
    def _():
        sum_ref[...] += sums


def leave(
    ids,
    pieces,
    stat,
    aux,
    d_joints,
    d_hidden,
    w_three,
    far_q,
    w_up,
    far_u,
    mixed,
    w_attn_out,
    far_a,
    active,
    w_down,
    far_d,
):
    rows, quarter = pieces[0].shape
    full, half = 4 * quarter, 2 * quarter
    units, heads_w = far_u.shape[1], far_q.shape[2]
    step = rows // 4
    ins = (
        [(v, rows_of(step, quarter)) for v in pieces]
        + [(stat, rows_of(step, PAIR)), (aux, fixed(aux.shape))]
        + [(d, rows_of(step, 3 * PAIR)) for d in d_joints]
        + [
            (d_hidden, rows_of(step, units)),
            (w_three, fixed((3, half, heads_w), lambda ids: (0, 0, ids[1]))),
            (far_q, fixed(far_q.shape)),
            (w_up, fixed((half, units), lambda ids: (0, ids[1]))),
            (far_u, fixed(far_u.shape)),
        ]
        + [(m, rows_of(step, PAIR)) for m in mixed]
        + [
            (w_attn_out, fixed((heads_w, half), lambda ids: (ids[1], 0))),
            (far_a, fixed(far_a.shape)),
            (active, rows_of(step, units)),
            (w_down, fixed((units, half), lambda ids: (ids[1], 0))),
            (far_d, fixed(far_d.shape)),
        ]
    )
    outs = [
        ((rows, half), F32, rows_of(step, half)),
        ((rows, half), BF16, rows_of(step, half)),
        ((4, 8, step), F32, pl.BlockSpec((1, 8, step), lambda i, ids: (i, 0, 0))),
        ((2, full), F32, fixed((2, full))),
        ((rows, half), F32, rows_of(step, half)),
        ((rows, half), BF16, rows_of(step, half)),
    ]
    return by_rows(leave_kernel, 4, ids, ins, outs, "leave")


def rotary_tables(positions):
    lane = jnp.arange(PAIR, dtype=jnp.int32)
    feature = lane % HEAD_DIM
    inverse = 10000.0 ** (-(2.0 * (feature // 2).astype(F32)) / ROTARY)
    angle = positions.astype(F32)[:, None] * inverse[None, :]
    turned = (feature < ROTARY)[None, :]
    sign = jnp.where(feature % 2 == 0, -1.0, 1.0)[None, :]
    cosines = jnp.where(turned, jnp.cos(angle), 1.0)
    sines = jnp.where(turned, jnp.sin(angle) * sign, 0.0)
    return cosines, sines


class Chain:
    held = ("value", "other", "far")

    def __init__(self, value, far, size, x_id, place):
        self.low, self.place = x_id == 0, place
        self.value, self.far, self.keep = jnp.where(self.low, far, value), far, value
        self.moving = self.other = self.crossed = None
        line = size // 2
        steps = line // 2 - 1

        def perm(pairs):
            return [(2 * i + x, 2 * j + x) for i, j in pairs for x in range(2)]

        self.pair = [(i, i ^ 1) for i in range(size)]
        self.hops = [(self.pair, None)]
        if line > 1:
            for k in range(steps):
                self.hops.append((perm([(k, k + 1), (line - 1 - k, line - 2 - k)]), None))
            mid = line // 2
            self.hops.append((perm([(mid - 1, mid), (mid, mid - 1)]), None))
            for k in reversed(range(steps)):
                self.hops.append((perm([(k + 1, k), (line - 2 - k, line - 1 - k)]), (k, line - 1 - k)))
        self.hops.append((self.pair, None))
        self.stage = 0
        self.cross = [
            (2 * i + c, 2 * (i ^ 1) + (c if i % 2 else 1 - c)) for i in range(size) for c in range(2)
        ]
        self.trade = [(2 * i + c, 2 * i + 1 - c) for i in range(1, size, 2) for c in range(2)]

    def busy(self):
        return self.stage < len(self.hops)

    def start(self):
        if self.stage == 0:
            self.moving = lax.ppermute(self.value, ("dp", "branch"), self.cross)
            self.crossed = lax.ppermute(self.far, ("dp", "branch"), self.trade)
        else:
            self.moving = lax.ppermute(self.value, "dp", self.hops[self.stage][0])

    def finish(self):
        got, self.moving = self.moving, None
        ends = self.hops[self.stage][1]
        if self.stage == len(self.hops) - 1:
            self.other = got
        elif ends is None:
            base = self.value
            if self.stage == 0:
                base = jnp.where(self.low, self.keep, self.crossed)
            self.value = (base.astype(F32) + got.astype(F32)).astype(base.dtype)
        else:
            here = (self.place == ends[0]) | (self.place == ends[1])
            self.value = jnp.where(here, got, self.value)
        self.far = None
        self.stage += 1

    def pieces(self):
        return (self.value, self.other)


class Scatter:
    held = ("value", "near")
    hops = (0, 1)

    def __init__(self, near, far, t):
        self.near, self.value, self.low = near, far, t == 0
        self.moving = self.far = None
        self.stage = 0

    def busy(self):
        return self.stage < 2

    def start(self):
        self.moving = lax.ppermute(self.value, ("branch", "tensor")[self.stage], SWAP)

    def finish(self):
        got, self.moving = self.moving, None
        if self.stage == 0:
            total = self.near + got.astype(F32)
            low, high = jnp.split(total, 2, axis=1)
            self.value = jnp.where(self.low, high, low).astype(BF16)
            self.near = jnp.where(self.low, low, high)
        else:
            self.near = self.near + got.astype(F32)
        self.stage += 1


class Steps:
    def __init__(self):
        self.before = []

    def run(self, finish, start, compute=None, *operands, extra=None):
        for c in finish:
            c.finish()
        if extra is not None:
            chain, rows = extra
            chain.value = jnp.concatenate([chain.value, rows.astype(BF16)], 0)
        touched = list({id(c): c for c in [*finish, *start]}.values())
        held = [(c, name) for c in touched for name in c.held if getattr(c, name) is not None]
        values, operands, _ = lax.optimization_barrier(
            ([getattr(c, name) for c, name in held], operands, self.before)
        )
        for (c, name), v in zip(held, values):
            setattr(c, name, v)
        for c in start:
            c.start()
        out = compute(*operands) if compute is not None else ()
        self.before = list(out)
        return out


def place_kernel(emit, count, flag_ref, *refs):
    own, other, outs = refs[:count], refs[count : 2 * count], refs[2 * count :]
    k, s = pl.program_id(0), pl.program_id(1)
    for c in range(count):
        pl.when((s == c) & (k == flag_ref[0]))(functools.partial(emit, own[c], outs))
        pl.when((s == c) & (k != flag_ref[0]))(functools.partial(emit, other[c], outs))


def place(emit, flag, pieces, out_shapes, out_blocks, maps, name):
    count = len(pieces)
    arrays = [p[0] for p in pieces] + [p[1] for p in pieces]
    grid_spec = pltpu.PrefetchScalarGridSpec(
        num_scalar_prefetch=1,
        grid=(2, count),
        in_specs=[pl.BlockSpec(a.shape, lambda k, s, f: (0, 0)) for a in arrays],
        out_specs=[pl.BlockSpec(blk, m) for blk, m in zip(out_blocks, maps)],
    )
    return pl.pallas_call(
        functools.partial(place_kernel, emit, count),
        grid_spec=grid_spec,
        out_shape=[jax.ShapeDtypeStruct(o, F32) for o in out_shapes],
        compiler_params=pltpu.CompilerParams(vmem_limit_bytes=48 << 20),
        cost_estimate=pl.CostEstimate(
            flops=0, bytes_accessed=6 * 2 * count * arrays[0].size, transcendentals=0
        ),
        name=name,
    )(flag.reshape(1).astype(jnp.int32), *arrays)


def emit_plain(src, outs):
    outs[0][...] = src[...].astype(F32)


def emit_late(src, outs):
    rows = outs[0].shape[1]
    for j in range(3):
        outs[0][j] = src[:rows, j * PAIR : (j + 1) * PAIR].astype(F32)
    outs[1][...] = src[:rows, 3 * PAIR :].astype(F32).T


def shards(
    dp_size,
    inputs,
    cotangent,
    seg_ids,
    pad_mask,
    positions,
    ln_gain,
    ln_bias,
    w_qkv,
    w_attn_out,
    w_up,
    b_up,
    w_down,
    b_down,
):
    b = lax.axis_index("branch")
    t = lax.axis_index("tensor")
    dp = lax.axis_index("dp")
    x_id, ring_id = lax.rem(dp, 2), dp // 2
    rows, quarter = inputs.shape
    half = 2 * quarter
    full = 4 * quarter
    heads_w = w_qkv.shape[2] // 2
    units = w_up.shape[1] // 2
    ids = jnp.stack([t, b]).astype(jnp.int32)

    def over_branch(v):
        return lax.ppermute(v, "branch", SWAP)

    def over_tensor(v):
        return lax.ppermute(v, "tensor", SWAP)

    def part(w, axis, index, size):
        return lax.dynamic_slice_in_dim(w, index * size, size, axis)

    x_got, x_far = over_tensor(inputs), over_branch(inputs)
    g_own, _ = lax.optimization_barrier((cotangent, x_far))
    g_got = over_tensor(g_own)
    aux = jnp.concatenate([ln_gain[None], ln_bias[None], jnp.zeros((14, quarter), BF16)], 0)
    aux_got = over_tensor(aux)
    w_three = jnp.transpose(w_qkv, (1, 0, 2))
    far_q = over_branch(part(w_three, 2, 1 - b, heads_w))
    far_u = over_branch(part(w_up, 1, 1 - b, units))
    bias_up = b_up.reshape(1, 2 * units)
    cosines, sines = rotary_tables(positions)
    span, start = spans(positions)
    aux_got, cosines, sines, span, start = lax.optimization_barrier(
        (aux_got, cosines, sines, span, start)
    )
    aux_half = jnp.where(
        t == 0, jnp.concatenate([aux, aux_got], 1), jnp.concatenate([aux_got, aux], 1)
    )
    aux_all = jnp.concatenate([aux_half, over_branch(aux_half)], 1)
    (x_got, x_far, aux_all, far_q, far_u, bias_up, cosines, sines) = lax.optimization_barrier(
        (x_got, x_far, aux_all, far_q, far_u, bias_up, cosines, sines)
    )
    x_pieces = (inputs, x_got, x_far, over_branch(x_got))
    normed, active, slope, qkv, stat = enter(
        ids, x_pieces, aux_all, w_three, far_q, w_up, far_u, bias_up, cosines, sines
    )
    g_far = over_branch(cotangent)
    far_a = over_branch(part(w_attn_out, 0, 1 - b, heads_w))
    far_d = over_branch(part(w_down, 0, 1 - b, units))
    g_got, g_far, far_a, far_d, active = lax.optimization_barrier(
        (g_got, g_far, far_a, far_d, active)
    )
    g_pieces = (cotangent, g_got, g_far, over_branch(g_got))
    g_all, down_near, down_send = down_grads(ids, g_pieces, active)

    def chained(near, far):
        return Chain(near, far, dp_size, x_id, ring_id)

    def attend(pair):
        return lambda *v: attention(pair, *v, cosines, sines, span, start)

    steps = Steps()
    down = chained(down_near, down_send)
    d_hidden, d_mixed, up_near, up_send, bup = steps.run(
        [], [down], lambda *v: up_grads(ids, *v, w_down, far_d, w_attn_out, far_a), g_all, normed, slope
    )
    up = chained(up_near, up_send)
    mixed0, d_joint0, near0, send0 = steps.run(
        [down], [up, down], attend(0), qkv, d_mixed, normed, g_all
    )
    late0 = chained(near0, send0)
    mixed1, d_joint1, near1, send1 = steps.run(
        [up, down], [late0, down, up], attend(1), qkv, d_mixed, normed, g_all
    )
    late1 = chained(near1, send1)

    def finish(ac, m0, m1, dj0, dj1, dh):
        return leave(
            ids,
            x_pieces,
            stat,
            aux_all,
            (dj0, dj1),
            dh,
            w_three,
            far_q,
            w_up,
            far_u,
            (m0, m1),
            w_attn_out,
            far_a,
            ac,
            w_down,
            far_d,
        )

    d_near, d_far, row_sums, sums, term_near, term_far = steps.run(
        [late0, down, up],
        [late1, late0, down, up],
        finish,
        active,
        mixed0,
        mixed1,
        d_joint0,
        d_joint1,
        d_hidden,
    )
    g_float = cotangent.astype(F32)
    terms, grads = Scatter(term_near, term_far, t), Scatter(d_near, d_far, t)
    moving = [late1, late0, down, up]

    def spread(rs):
        return (rs + over_branch(rs),)

    chains = [down, up, late1, late0]
    small = jnp.concatenate(
        [
            sums.reshape(4, half),
            bup.reshape(units // half, half),
            jnp.pad(jnp.sum(g_float, axis=0), (0, quarter))[None],
            jnp.zeros((9, half), F32),
        ]
    )
    (row_sums,) = steps.run(
        chains,
        [*(c for c in chains if c.stage + 1 < len(c.hops)), terms, grads],
        spread,
        row_sums,
        extra=(late1, small),
    )
    flag = b ^ x_id
    gradients = {}

    def lay(*operands):
        if down.other is not None and "down" not in gradients:
            gradients["down"] = place(
                emit_plain,
                flag,
                [down.pieces()],
                [(2 * units, half)],
                [(units, half)],
                [lambda k, s, f: (k, 0)],
                "place_down",
            )[0]
        if up.other is not None and "up" not in gradients:
            gradients["up"] = place(
                emit_plain,
                flag,
                [up.pieces()],
                [(half, 2 * units)],
                [(half, units)],
                [lambda k, s, f: (0, k)],
                "place_up",
            )[0]
        return [v + over_tensor(v) for v in operands]

    for turn in itertools.count(1):
        begin = [terms if turn == 1 else grads]
        operands = [row_sums] if turn == 1 else []
        moving = [c for c in (*chains, terms, grads) if c.moving is not None]
        ready = [c for c in (*chains, *begin) if c.stage + (c in moving) < len(c.hops)]
        if turn > 2 and not ready:
            break
        out = steps.run(moving, ready, lay, *operands)
        if turn == 1:
            (row_sums,) = out
    for c in (*chains, terms, grads):
        if c.moving is not None:
            c.finish()
    lay()

    row_sums = row_sums * (1.0 / full)
    output = (inputs.astype(F32) + terms.near + b_down.astype(F32)).astype(BF16)
    d_own = grads.near
    mean, inv_root = stat[:, 0:1], stat[:, 1:2]
    unit_own = (inputs.astype(F32) - mean) * inv_root
    input_grad = g_float + inv_root * (
        d_own * ln_gain.astype(F32)
        - row_sums[:, 0, :].reshape(rows, 1)
        - unit_own * row_sums[:, 1, :].reshape(rows, 1)
    )
    output, input_grad, gradients["down"], gradients["up"], late1.other = lax.optimization_barrier(
        (output, input_grad, gradients["down"], gradients["up"], late1.other)
    )
    small = late1.value[half : half + 8].astype(F32) + late1.other[half : half + 8].astype(F32)
    sums = small[:4].reshape(2, full)
    own = part(sums, 1, t, quarter)
    for k, v in (
        (1, part(sums, 1, 1 - t, quarter)),
        (2, part(sums, 1, 2 + t, quarter)),
        (3, part(sums, 1, 3 - t, quarter)),
    ):
        own = own + lax.ppermute(v, ("branch", "tensor"), [(i, i ^ k) for i in range(4)])
    bup = small[4:6].reshape(units)
    bup_far = over_branch(bup)
    grad_bup = jnp.where(b == 0, jnp.concatenate([bup, bup_far]), jnp.concatenate([bup_far, bup]))

    grad_qkv, grad_aout = place(
        emit_late,
        flag,
        [c.pieces() for c in (late0, late1)],
        [(3, half, 2 * heads_w), (2 * heads_w, half)],
        [(3, half, PAIR), (PAIR, half)],
        [lambda k, s, f: (0, 0, 2 * k + s), lambda k, s, f: (2 * k + s, 0)],
        "place_late",
    )
    return (
        output,
        input_grad,
        own[0],
        own[1],
        jnp.transpose(grad_qkv, (1, 0, 2)),
        grad_aout,
        gradients["up"],
        grad_bup,
        gradients["down"],
        small[6, :quarter],
    )


def solution(mesh):
    features = ("branch", "tensor")
    in_specs = (
        P("dp", features),
        P("dp", features),
        P("dp"),
        P("dp"),
        P("dp"),
        P(features),
        P(features),
        P("branch", None, "tensor"),
        P("tensor", "branch"),
        P("branch", "tensor"),
        P("tensor"),
        P("tensor", "branch"),
        P(features),
    )
    out_specs = (
        P("dp", features),
        P("dp", features),
        P(features),
        P(features),
        P("branch", None, "tensor"),
        P("tensor", "branch"),
        P("branch", "tensor"),
        P("tensor"),
        P("tensor", "branch"),
        P(features),
    )
    return jax.shard_map(
        functools.partial(shards, mesh.shape["dp"]),
        mesh=mesh,
        in_specs=in_specs,
        out_specs=out_specs,
        check_vma=False,
    )
```

```python
import functools
import itertools

import jax
import jax.numpy as jnp
from jax import lax
from jax.experimental import pallas as pl
from jax.experimental.pallas import tpu as pltpu
from jax.sharding import PartitionSpec as P

HEAD_DIM = 64
ROTARY = 32
PAIR = 2 * HEAD_DIM
QB = 128
KC = 256
LONGEST = 1024
EPS = 1e-05
NEG = -1e30
F32 = jnp.float32
BF16 = jnp.bfloat16
SWAP = [(0, 1), (1, 0)]
GELU_A = 0.7978845608028654
GELU_B = 0.044715


def nn(a, b):
    return lax.dot_general(a, b, (((1,), (0,)), ((), ())), preferred_element_type=F32)


def nt(a, b):
    return lax.dot_general(a, b, (((1,), (1,)), ((), ())), preferred_element_type=F32)


def tn(a, b):
    return lax.dot_general(a, b, (((0,), (0,)), ((), ())), preferred_element_type=F32)


def partner(x, even):
    width = x.shape[1]
    return jnp.where(even, pltpu.roll(x, width - 1, 1), pltpu.roll(x, 1, 1))


def cols(pair, part):
    return slice((3 * pair + part) * PAIR, (3 * pair + part + 1) * PAIR)


def attention_kernel(
    pair,
    most,
    span_ref,
    start_ref,
    qkv_hbm,
    dmix_hbm,
    cos_hbm,
    sin_hbm,
    normed_hbm,
    g_hbm,
    mixed_ref,
    dj_ref,
    near_ref,
    far_ref,
    q_s,
    qt_s,
    g_s,
    gt_s,
    k_s,
    v_s,
    kt_s,
    vt_s,
    s_s,
    d_s,
    p_s,
    e_s,
    dk_s,
    dv_s,
    qkv_ref,
    dmix_ref,
    cos_ref,
    sin_ref,
    normed_s,
    ct_s,
    arrived,
):
    pairs = 1
    rows = qkv_ref.shape[0]
    fetch = [
        pltpu.make_async_copy(src, dst, arrived.at[n])
        for n, (src, dst) in enumerate(
            (
                (qkv_hbm.at[:, 3 * pair * PAIR : 3 * (pair + 1) * PAIR], qkv_ref),
                (dmix_hbm.at[:, pair * PAIR : (pair + 1) * PAIR], dmix_ref),
                (cos_hbm, cos_ref),
                (sin_hbm, sin_ref),
                (normed_hbm, normed_s),
                (g_hbm, ct_s),
            )
        )
    ]
    for copy in fetch:
        copy.start()
    fetch[0].wait()
    fetch[1].wait()
    rows = qkv_ref.shape[0]
    lane = lax.broadcasted_iota(jnp.int32, (QB, PAIR), 1)
    even = lane % 2 == 0
    first = lane < HEAD_DIM
    top = lax.broadcasted_iota(jnp.int32, (PAIR, QB), 0) < HEAD_DIM
    scale = HEAD_DIM**-0.5

    for p in range(pairs):
        k_s[p, :QB, :] = jnp.zeros((QB, PAIR), BF16)
        v_s[p, :QB, :] = jnp.zeros((QB, PAIR), BF16)
        kt_s[p, :, :QB] = jnp.zeros((PAIR, QB), BF16)
        vt_s[p, :, :QB] = jnp.zeros((PAIR, QB), BF16)
        dk_s[p, :QB, :] = jnp.zeros((QB, PAIR), F32)
        dv_s[p, :QB, :] = jnp.zeros((QB, PAIR), F32)

    @pl.loop(0, rows // QB)
    def _(i):
        at = pl.ds(pl.multiple_of(i * QB, QB), QB)
        to = pl.ds(pl.multiple_of(i * QB + QB, QB), QB)
        for p in range(pairs):
            q = qkv_ref[at, cols(p, 0)].astype(F32)
            k = qkv_ref[at, cols(p, 1)]
            v = qkv_ref[at, cols(p, 2)]
            g = dmix_ref[at, p * PAIR : (p + 1) * PAIR].astype(F32)
            q_s[p, i, :QB, :] = jnp.where(first, q, 0.0).astype(BF16)
            q_s[p, i, QB:, :] = jnp.where(first, 0.0, q).astype(BF16)
            g_s[p, i, :QB, :] = jnp.where(first, g, 0.0).astype(BF16)
            g_s[p, i, QB:, :] = jnp.where(first, 0.0, g).astype(BF16)
            q, g = q.T, g.T
            qt_s[p, i, :, :QB] = jnp.where(top, q, 0.0).astype(BF16)
            qt_s[p, i, :, QB:] = jnp.where(top, 0.0, q).astype(BF16)
            gt_s[p, i, :, :QB] = jnp.where(top, g, 0.0).astype(BF16)
            gt_s[p, i, :, QB:] = jnp.where(top, 0.0, g).astype(BF16)
            k_s[p, to, :] = k
            v_s[p, to, :] = v
            kt_s[p, :, to] = k.astype(F32).T.astype(BF16)
            vt_s[p, :, to] = v.astype(F32).T.astype(BF16)
            dk_s[p, to, :] = jnp.zeros((QB, PAIR), F32)
            dv_s[p, to, :] = jnp.zeros((QB, PAIR), F32)

    fetch[2].wait()
    fetch[3].wait()
    key_slot = lax.broadcasted_iota(jnp.int32, (KC, 2 * QB), 0)
    query_slot = lax.broadcasted_iota(jnp.int32, (1, 2 * QB), 1) % QB

    def block(i, n):
        base = (i + 2) * QB - n * KC
        spots = [pl.ds(pl.multiple_of(base + j * KC, QB), KC) for j in range(n)]
        whole = pl.ds(pl.multiple_of(base, QB), n * KC)
        query = query_slot + (i * QB + QB - base)
        start = start_ref[i] + (QB - base)
        here = pl.ds(pl.multiple_of(i * QB, QB), QB)
        pr = range(pairs)
        peak = [None] * pairs
        for j in range(n):
            ok = (key_slot >= start - j * KC) & (key_slot <= query - j * KC)
            for p in pr:
                s = jnp.where(ok, nn(k_s[p, spots[j], :], qt_s[p, i]), NEG)
                s_s[p, j] = s
                m = jnp.max(s.reshape(KC // 8, 8, 2 * QB), axis=0)
                peak[p] = m if peak[p] is None else jnp.maximum(peak[p], m)
        for j in range(n):
            for p in pr:
                d_s[p, j] = nn(v_s[p, spots[j], :], gt_s[p, i])
        peak = [jnp.max(m, axis=0, keepdims=True) for m in peak]
        total = [0.0] * pairs
        delta = [0.0] * pairs
        for j in range(n):
            for p in pr:
                e = jnp.exp(s_s[p, j] - peak[p])
                s_s[p, j] = e
                total[p] += jnp.sum(e.reshape(KC // 8, 8, 2 * QB), axis=0)
                delta[p] += jnp.sum((e * d_s[p, j]).reshape(KC // 8, 8, 2 * QB), axis=0)
        inverse = [1.0 / jnp.sum(x, axis=0, keepdims=True) for x in total]
        delta = [jnp.sum(x, axis=0, keepdims=True) * r for x, r in zip(delta, inverse)]
        for j in range(n):
            for p in pr:
                prob = s_s[p, j] * inverse[p]
                p_s[p, j * KC : (j + 1) * KC, :] = prob.astype(BF16)
                e_s[p, j * KC : (j + 1) * KC, :] = (prob * (d_s[p, j] - delta[p])).astype(BF16)
        for p in pr:
            o = nn(vt_s[p, :, whole], p_s[p, : n * KC, :])
            mixed_ref[here, p * PAIR : (p + 1) * PAIR] = (
                jnp.where(top, o[:, :QB], o[:, QB:]).T.astype(BF16)
            )
            dv_s[p, whole, :] += nn(p_s[p, : n * KC, :], g_s[p, i])
            dk_s[p, whole, :] += nn(e_s[p, : n * KC, :], q_s[p, i])
            d = nn(kt_s[p, :, whole], e_s[p, : n * KC, :])
            d = (jnp.where(top, d[:, :QB], d[:, QB:]) * scale).T
            d = d * cos_ref[here, :] - partner(d, even) * sin_ref[here, :]
            dj_ref[here, cols(p, 0)] = d.astype(BF16)

    @pl.loop(0, rows // QB)
    def _(i):
        for n in range(1, most + 1):
            pl.when(span_ref[i] == n)(functools.partial(block, i, n))

    @pl.loop(0, rows // QB)
    def _(i):
        at = pl.ds(pl.multiple_of(i * QB, QB), QB)
        to = pl.ds(pl.multiple_of(i * QB + QB, QB), QB)
        cosines = cos_ref[at, :]
        sines = sin_ref[at, :]
        for p in range(pairs):
            d = dk_s[p, to, :]
            d = d * cosines - partner(d, even) * sines
            dj_ref[at, cols(p, 1)] = d.astype(BF16)
            dj_ref[at, cols(p, 2)] = dv_s[p, to, :].astype(BF16)

    fetch[4].wait()
    fetch[5].wait()
    half, split = normed_s.shape[1] // 2, 3 * PAIR
    for p in range(pairs):
        at_p = p * 4 * PAIR
        for at, out in ((slice(half, 2 * half), far_ref), (slice(0, half), near_ref)):
            out[:half, at_p : at_p + split] = tn(
                normed_s[:, at], dj_ref[:, p * split : (p + 1) * split]
            ).astype(BF16)
            out[:half, at_p + split : at_p + 4 * PAIR] = tn(
                ct_s[:, at], mixed_ref[:, p * PAIR : (p + 1) * PAIR]
            ).astype(BF16)


def spans(positions):
    rows = positions.shape[0]
    blocks = rows // QB
    start = (jnp.arange(rows, dtype=jnp.int32) - positions).reshape(blocks, 1, QB)
    span = (jnp.arange(blocks, dtype=jnp.int32) - start[:, 0, 0] // QB + 2) // 2
    return span, jnp.concatenate([start, start], axis=2)


def attention(pair, qkv, dmix, normed, g_all, cosines, sines, span, start):
    rows = qkv.shape[0]
    blocks = rows // QB
    padded = rows + QB
    most = LONGEST // KC + 1
    half = normed.shape[1] // 2
    vmem = pl.BlockSpec(memory_space=pltpu.VMEM)
    smem = pl.BlockSpec(memory_space=pltpu.SMEM)
    return pl.pallas_call(
        functools.partial(attention_kernel, pair, most),
        out_shape=[
            jax.ShapeDtypeStruct((rows, PAIR), BF16),
            jax.ShapeDtypeStruct((rows, 3 * PAIR), BF16),
        ]
        + [jax.ShapeDtypeStruct((half, 4 * PAIR), BF16)] * 2,
        in_specs=[smem, vmem] + [pl.BlockSpec(memory_space=pl.ANY)] * 6,
        out_specs=[vmem] * 4,
        scratch_shapes=[
            pltpu.VMEM((1, blocks, 2 * QB, PAIR), BF16),
            pltpu.VMEM((1, blocks, PAIR, 2 * QB), BF16),
            pltpu.VMEM((1, blocks, 2 * QB, PAIR), BF16),
            pltpu.VMEM((1, blocks, PAIR, 2 * QB), BF16),
            pltpu.VMEM((1, padded, PAIR), BF16),
            pltpu.VMEM((1, padded, PAIR), BF16),
            pltpu.VMEM((1, PAIR, padded), BF16),
            pltpu.VMEM((1, PAIR, padded), BF16),
            pltpu.VMEM((1, most, KC, 2 * QB), F32),
            pltpu.VMEM((1, most, KC, 2 * QB), F32),
            pltpu.VMEM((1, most * KC, 2 * QB), BF16),
            pltpu.VMEM((1, most * KC, 2 * QB), BF16),
            pltpu.VMEM((1, padded, PAIR), F32),
            pltpu.VMEM((1, padded, PAIR), F32),
            pltpu.VMEM((rows, 3 * PAIR), BF16),
            pltpu.VMEM((rows, PAIR), BF16),
            pltpu.VMEM(cosines.shape, F32),
            pltpu.VMEM(sines.shape, F32),
            pltpu.VMEM(normed.shape, BF16),
            pltpu.VMEM(g_all.shape, BF16),
            pltpu.SemaphoreType.DMA((6,)),
        ],
        compiler_params=pltpu.CompilerParams(vmem_limit_bytes=40 << 20),
        cost_estimate=pl.CostEstimate(flops=0, bytes_accessed=0, transcendentals=0),
        name="attention",
    )(span, start, qkv, dmix, cosines, sines, normed, g_all)


def picked(first, own, got, far_own, far_got):
    own, got, far_own, far_got = (v[...].astype(F32) for v in (own, got, far_own, far_got))
    return jnp.concatenate(
        [
            jnp.where(first, own, got),
            jnp.where(first, got, own),
            jnp.where(first, far_own, far_got),
            jnp.where(first, far_got, far_own),
        ],
        1,
    )


def resident(shape):
    return pl.BlockSpec(shape, lambda i: (0,) * len(shape), pipeline_mode=pl.Buffered(1))


def enter_kernel(
    ids,
    own,
    got,
    far_own,
    far_got,
    aux_ref,
    near_q,
    far_q,
    near_u,
    far_u,
    bias_ref,
    cos_ref,
    sin_ref,
    normed_ref,
    active_ref,
    slope_ref,
    qkv_ref,
    stat_ref,
):
    x = picked(ids[0] == 0, own, got, far_own, far_got)
    rows, full = x.shape
    half = full // 2
    mean = jnp.mean(x, axis=1, keepdims=True)
    center = x - mean
    inv_root = lax.rsqrt(jnp.mean(center * center, axis=1, keepdims=True) + EPS)
    normed = (
        center * inv_root * aux_ref[0:1, :].astype(F32) + aux_ref[1:2, :].astype(F32)
    ).astype(BF16)
    normed_ref[...] = normed
    lane = lax.broadcasted_iota(jnp.int32, (rows, PAIR), 1)
    stat_ref[...] = jnp.where(lane == 0, mean, inv_root)
    near, far = normed[:, :half], normed[:, half:]
    hidden = nn(near, near_u[...]) + nn(far, far_u[...]) + bias_ref[0:1, :].astype(F32)
    square = hidden * hidden
    bend = jnp.tanh(GELU_A * hidden * (1.0 + GELU_B * square))
    up = 0.5 * (1.0 + bend)
    active = (hidden * up).astype(BF16)
    active_ref[...] = active
    slope_ref[...] = up + (0.5 * GELU_A) * hidden * (1.0 - bend * bend) * (
        1.0 + 3.0 * GELU_B * square
    )
    even = lane % 2 == 0
    cosines, sines = cos_ref[...], sin_ref[...]
    for j in range(3):
        joint = nn(near, near_q[j]) + nn(far, far_q[j])
        for p in range(joint.shape[1] // PAIR):
            v = joint[:, p * PAIR : (p + 1) * PAIR]
            if j < 2:
                v = v * cosines + partner(v, even) * sines
            if j == 0:
                v = v * HEAD_DIM**-0.5
            at = (3 * p + j) * PAIR
            qkv_ref[:, at : at + PAIR] = v.astype(BF16)


def rows_of(step, width):
    return pl.BlockSpec((step, width), lambda i, ids: (i, 0))


def fixed(shape, index=None):
    if index is None:
        return pl.BlockSpec(
            shape, lambda i, ids: (0,) * len(shape), pipeline_mode=pl.Buffered(1)
        )
    return pl.BlockSpec(shape, lambda i, ids: index(ids), pipeline_mode=pl.Buffered(1))


def by_rows(kernel, steps, ids, ins, outs, name, scratch=()):
    return pl.pallas_call(
        kernel,
        grid_spec=pltpu.PrefetchScalarGridSpec(
            num_scalar_prefetch=1,
            grid=(steps,),
            in_specs=[s for _, s in ins],
            out_specs=[s for _, _, s in outs],
            scratch_shapes=scratch,
        ),
        out_shape=[jax.ShapeDtypeStruct(s, d) for s, d, _ in outs],
        compiler_params=pltpu.CompilerParams(vmem_limit_bytes=50 << 20),
        cost_estimate=pl.CostEstimate(flops=0, bytes_accessed=0, transcendentals=0),
        name=name,
    )(ids, *[a for a, _ in ins])


def enter(ids, pieces, aux, w_three, far_q, w_up, far_u, bias, cosines, sines):
    rows, quarter = pieces[0].shape
    full, half = 4 * quarter, 2 * quarter
    units, heads_w = far_u.shape[1], far_q.shape[2]
    step = rows // 8
    ins = [(v, rows_of(step, quarter)) for v in pieces] + [
        (aux, fixed(aux.shape)),
        (w_three, fixed((3, half, heads_w), lambda ids: (0, 0, ids[1]))),
        (far_q, fixed(far_q.shape)),
        (w_up, fixed((half, units), lambda ids: (0, ids[1]))),
        (far_u, fixed(far_u.shape)),
        (bias, fixed((1, units), lambda ids: (0, ids[1]))),
        (cosines, rows_of(step, PAIR)),
        (sines, rows_of(step, PAIR)),
    ]
    outs = [
        ((rows, full), BF16, rows_of(step, full)),
        ((rows, units), BF16, rows_of(step, units)),
        ((rows, units), F32, rows_of(step, units)),
        ((rows, 3 * heads_w), BF16, rows_of(step, 3 * heads_w)),
        ((rows, PAIR), F32, rows_of(step, PAIR)),
    ]
    return by_rows(enter_kernel, 8, ids, ins, outs, "enter")


def down_kernel(
    ids,
    own,
    got,
    far_own,
    far_got,
    active_ref,
    g_ref,
    near_ref,
    far_ref,
    total_s,
):
    i = pl.program_id(0)
    g = picked(ids[0] == 0, own, got, far_own, far_got).astype(BF16)
    half = g.shape[1] // 2
    g_ref[...] = g

    @pl.when(i == 0)
    def _():
        total_s[...] = tn(active_ref[...], g)

    @pl.when(i > 0)
    def _():
        total_s[...] += tn(active_ref[...], g)

    @pl.when(i == pl.num_programs(0) - 1)
    def _():
        near_ref[...] = total_s[:, :half].astype(BF16)
        far_ref[...] = total_s[:, half:].astype(BF16)


def down_grads(ids, pieces, active):
    rows, quarter = pieces[0].shape
    full, half, units = 4 * quarter, 2 * quarter, active.shape[1]
    step = rows // 4
    ins = [(v, rows_of(step, quarter)) for v in pieces] + [
        (active, rows_of(step, units)),
    ]
    outs = [
        ((rows, full), BF16, rows_of(step, full)),
        ((units, half), BF16, fixed((units, half))),
        ((units, half), BF16, fixed((units, half))),
    ]
    return by_rows(
        down_kernel,
        4,
        ids,
        ins,
        outs,
        "down_grads",
        [pltpu.VMEM((units, full), F32)],
    )


def up_kernel(
    ids,
    g_ref,
    normed_ref,
    slope_ref,
    near_d,
    far_d,
    near_a,
    far_a,
    dh_ref,
    dm_ref,
    near_ref,
    far_ref,
    sum_ref,
    total_s,
):
    i = pl.program_id(0)
    half = g_ref.shape[1] // 2
    da = nt(g_ref[:, :half], near_d[...]) + nt(g_ref[:, half:], far_d[...])
    dm_ref[...] = (nt(g_ref[:, :half], near_a[...]) + nt(g_ref[:, half:], far_a[...])).astype(BF16)
    dh = (da * slope_ref[...]).astype(BF16)
    dh_ref[...] = dh
    sums = jnp.sum(dh.astype(F32), axis=0, keepdims=True)

    @pl.when(i == 0)
    def _():
        total_s[...] = tn(normed_ref[...], dh)
        sum_ref[...] = sums

    @pl.when(i > 0)
    def _():
        total_s[...] += tn(normed_ref[...], dh)
        sum_ref[...] += sums

    @pl.when(i == pl.num_programs(0) - 1)
    def _():
        near_ref[...] = total_s[:half, :].astype(BF16)
        far_ref[...] = total_s[half:, :].astype(BF16)


def up_grads(ids, g_all, normed, slope, w_down, far_d, w_attn_out, far_a):
    rows, full = g_all.shape
    half, units = full // 2, slope.shape[1]
    heads_w = far_a.shape[0]
    step = rows // 4
    ins = [
        (g_all, rows_of(step, full)),
        (normed, rows_of(step, full)),
        (slope, rows_of(step, units)),
        (w_down, fixed((units, half), lambda ids: (ids[1], 0))),
        (far_d, fixed(far_d.shape)),
        (w_attn_out, fixed((heads_w, half), lambda ids: (ids[1], 0))),
        (far_a, fixed(far_a.shape)),
    ]
    outs = [
        ((rows, units), BF16, rows_of(step, units)),
        ((rows, heads_w), BF16, rows_of(step, heads_w)),
        ((half, units), BF16, fixed((half, units))),
        ((half, units), BF16, fixed((half, units))),
        ((1, units), F32, fixed((1, units))),
    ]
    return by_rows(
        up_kernel,
        4,
        ids,
        ins,
        outs,
        "up_grads",
        [pltpu.VMEM((full, units), F32)],
    )


def leave_kernel(
    ids,
    own,
    got,
    far_own,
    far_got,
    stat_ref,
    aux_ref,
    dj0_ref,
    dj1_ref,
    dh_ref,
    near_q,
    far_q,
    near_u,
    far_u,
    mixed0_ref,
    mixed1_ref,
    near_a,
    far_a,
    term_ref,
    near_ref,
    far_ref,
    row_ref,
    sum_ref,
    term_near,
    term_far,
):
    i = pl.program_id(0)
    mixed = jnp.concatenate([mixed0_ref[...], mixed1_ref[...]], 1)
    half = near_ref.shape[1]
    term_near[...] = term_ref[:, :half] + nn(mixed, near_a[...])
    term_far[...] = (term_ref[:, half:] + nn(mixed, far_a[...])).astype(BF16)
    x = picked(ids[0] == 0, own, got, far_own, far_got)
    unit = (x - stat_ref[:, 0:1]) * stat_ref[:, 1:2]
    dh = dh_ref[...]
    near = nt(dh, near_u[...])
    far = nt(dh, far_u[...])
    for j in range(3):
        cut = slice(j * PAIR, (j + 1) * PAIR)
        dj = jnp.concatenate([dj0_ref[:, cut], dj1_ref[:, cut]], 1)
        near += nt(dj, near_q[j])
        far += nt(dj, far_q[j])
    near_ref[...] = near
    far_ref[...] = far.astype(BF16)
    both = jnp.concatenate([near, far], 1)
    scaled = both * aux_ref[0:1, :].astype(F32)
    first = jnp.sum(scaled, axis=1, keepdims=True)
    second = jnp.sum(scaled * unit, axis=1, keepdims=True)
    lane = lax.broadcasted_iota(jnp.int32, (x.shape[0], PAIR), 1)
    row_ref[0] = jnp.where(lane == 0, first, second).T[:8]
    sums = jnp.concatenate(
        [
            jnp.sum(both * unit, axis=0, keepdims=True),
            jnp.sum(both, axis=0, keepdims=True),
        ],
        0,
    )

    @pl.when(i == 0)
    def _():
        sum_ref[...] = sums

    @pl.when(i > 0)
    def _():
        sum_ref[...] += sums


def term_kernel(ids, active_ref, near_d, far_d, term_ref):
    half = near_d.shape[1]
    term_ref[:, :half] = nn(active_ref[...], near_d[...])
    term_ref[:, half:] = nn(active_ref[...], far_d[...])


def forward_term(ids, active, w_down, far_d):
    rows, units = active.shape
    half = far_d.shape[1]
    step = rows // 4
    ins = [
        (active, rows_of(step, units)),
        (w_down, fixed((units, half), lambda ids: (ids[1], 0))),
        (far_d, fixed(far_d.shape)),
    ]
    outs = [((rows, 2 * half), F32, rows_of(step, 2 * half))]
    return by_rows(term_kernel, 4, ids, ins, outs, "forward_term")


def leave(
    ids,
    pieces,
    stat,
    aux,
    d_joints,
    d_hidden,
    w_three,
    far_q,
    w_up,
    far_u,
    mixed,
    w_attn_out,
    far_a,
    term,
):
    rows, quarter = pieces[0].shape
    full, half = 4 * quarter, 2 * quarter
    units, heads_w = far_u.shape[1], far_q.shape[2]
    step = rows // 4
    ins = (
        [(v, rows_of(step, quarter)) for v in pieces]
        + [(stat, rows_of(step, PAIR)), (aux, fixed(aux.shape))]
        + [(d, rows_of(step, 3 * PAIR)) for d in d_joints]
        + [
            (d_hidden, rows_of(step, units)),
            (w_three, fixed((3, half, heads_w), lambda ids: (0, 0, ids[1]))),
            (far_q, fixed(far_q.shape)),
            (w_up, fixed((half, units), lambda ids: (0, ids[1]))),
            (far_u, fixed(far_u.shape)),
        ]
        + [(m, rows_of(step, PAIR)) for m in mixed]
        + [
            (w_attn_out, fixed((heads_w, half), lambda ids: (ids[1], 0))),
            (far_a, fixed(far_a.shape)),
            (term, rows_of(step, full)),
        ]
    )
    outs = [
        ((rows, half), F32, rows_of(step, half)),
        ((rows, half), BF16, rows_of(step, half)),
        ((4, 8, step), F32, pl.BlockSpec((1, 8, step), lambda i, ids: (i, 0, 0))),
        ((2, full), F32, fixed((2, full))),
        ((rows, half), F32, rows_of(step, half)),
        ((rows, half), BF16, rows_of(step, half)),
    ]
    return by_rows(leave_kernel, 4, ids, ins, outs, "leave")


def rotary_tables(positions):
    lane = jnp.arange(PAIR, dtype=jnp.int32)
    feature = lane % HEAD_DIM
    inverse = 10000.0 ** (-(2.0 * (feature // 2).astype(F32)) / ROTARY)
    angle = positions.astype(F32)[:, None] * inverse[None, :]
    turned = (feature < ROTARY)[None, :]
    sign = jnp.where(feature % 2 == 0, -1.0, 1.0)[None, :]
    cosines = jnp.where(turned, jnp.cos(angle), 1.0)
    sines = jnp.where(turned, jnp.sin(angle) * sign, 0.0)
    return cosines, sines


class Chain:
    held = ("value", "other", "far")

    def __init__(self, value, far, size, x_id, place):
        self.low, self.place = x_id == 0, place
        self.value, self.far, self.keep = jnp.where(self.low, far, value), far, value
        self.moving = self.other = self.crossed = None
        line = size // 2
        steps = line // 2 - 1

        def perm(pairs):
            return [(2 * i + x, 2 * j + x) for i, j in pairs for x in range(2)]

        self.pair = [(i, i ^ 1) for i in range(size)]
        self.hops = [(self.pair, None)]
        if line > 1:
            for k in range(steps):
                self.hops.append((perm([(k, k + 1), (line - 1 - k, line - 2 - k)]), None))
            mid = line // 2
            self.hops.append((perm([(mid - 1, mid), (mid, mid - 1)]), None))
            for k in reversed(range(steps)):
                self.hops.append((perm([(k + 1, k), (line - 2 - k, line - 1 - k)]), (k, line - 1 - k)))
        self.hops.append((self.pair, None))
        self.stage = 0
        self.cross = [
            (2 * i + c, 2 * (i ^ 1) + (c if i % 2 else 1 - c)) for i in range(size) for c in range(2)
        ]
        self.trade = [(2 * i + c, 2 * i + 1 - c) for i in range(1, size, 2) for c in range(2)]

    def busy(self):
        return self.stage < len(self.hops)

    def start(self):
        if self.stage == 0:
            self.moving = lax.ppermute(self.value, ("dp", "branch"), self.cross)
            self.crossed = lax.ppermute(self.far, ("dp", "branch"), self.trade)
        else:
            self.moving = lax.ppermute(self.value, "dp", self.hops[self.stage][0])

    def finish(self):
        got, self.moving = self.moving, None
        ends = self.hops[self.stage][1]
        if self.stage == len(self.hops) - 1:
            self.other = got
        elif ends is None:
            base = self.value
            if self.stage == 0:
                base = jnp.where(self.low, self.keep, self.crossed)
            self.value = (base.astype(F32) + got.astype(F32)).astype(base.dtype)
        else:
            here = (self.place == ends[0]) | (self.place == ends[1])
            self.value = jnp.where(here, got, self.value)
        self.far = None
        self.stage += 1

    def pieces(self):
        return (self.value, self.other)


class Scatter:
    held = ("value", "near")
    hops = (0, 1)

    def __init__(self, near, far, t):
        self.near, self.value, self.low = near, far, t == 0
        self.moving = self.far = None
        self.stage = 0

    def busy(self):
        return self.stage < 2

    def start(self):
        self.moving = lax.ppermute(self.value, ("branch", "tensor")[self.stage], SWAP)

    def finish(self):
        got, self.moving = self.moving, None
        if self.stage == 0:
            total = self.near + got.astype(F32)
            low, high = jnp.split(total, 2, axis=1)
            self.value = jnp.where(self.low, high, low).astype(BF16)
            self.near = jnp.where(self.low, low, high)
        else:
            self.near = self.near + got.astype(F32)
        self.stage += 1


class Steps:
    def __init__(self):
        self.before = []

    def run(self, finish, start, compute=None, *operands, extra=None):
        for c in finish:
            c.finish()
        if extra is not None:
            chain, rows = extra
            chain.value = jnp.concatenate([chain.value, rows.astype(BF16)], 0)
        touched = list({id(c): c for c in [*finish, *start]}.values())
        held = [(c, name) for c in touched for name in c.held if getattr(c, name) is not None]
        values, operands, _ = lax.optimization_barrier(
            ([getattr(c, name) for c, name in held], operands, self.before)
        )
        for (c, name), v in zip(held, values):
            setattr(c, name, v)
        for c in start:
            c.start()
        out = compute(*operands) if compute is not None else ()
        self.before = list(out)
        return out


def place_kernel(emit, count, flag_ref, *refs):
    own, other, outs = refs[:count], refs[count : 2 * count], refs[2 * count :]
    k, s = pl.program_id(0), pl.program_id(1)
    for c in range(count):
        pl.when((s == c) & (k == flag_ref[0]))(functools.partial(emit, own[c], outs))
        pl.when((s == c) & (k != flag_ref[0]))(functools.partial(emit, other[c], outs))


def place(emit, flag, pieces, out_shapes, out_blocks, maps, name):
    count = len(pieces)
    arrays = [p[0] for p in pieces] + [p[1] for p in pieces]
    grid_spec = pltpu.PrefetchScalarGridSpec(
        num_scalar_prefetch=1,
        grid=(2, count),
        in_specs=[pl.BlockSpec(a.shape, lambda k, s, f: (0, 0)) for a in arrays],
        out_specs=[pl.BlockSpec(blk, m) for blk, m in zip(out_blocks, maps)],
    )
    return pl.pallas_call(
        functools.partial(place_kernel, emit, count),
        grid_spec=grid_spec,
        out_shape=[jax.ShapeDtypeStruct(o, F32) for o in out_shapes],
        compiler_params=pltpu.CompilerParams(vmem_limit_bytes=48 << 20),
        cost_estimate=pl.CostEstimate(
            flops=0, bytes_accessed=6 * 2 * count * arrays[0].size, transcendentals=0
        ),
        name=name,
    )(flag.reshape(1).astype(jnp.int32), *arrays)


def emit_plain(src, outs):
    outs[0][...] = src[...].astype(F32)


def emit_late(src, outs):
    rows = outs[0].shape[1]
    for j in range(3):
        outs[0][j] = src[:rows, j * PAIR : (j + 1) * PAIR].astype(F32)
    outs[1][...] = src[:rows, 3 * PAIR :].astype(F32).T


def shards(
    dp_size,
    inputs,
    cotangent,
    seg_ids,
    pad_mask,
    positions,
    ln_gain,
    ln_bias,
    w_qkv,
    w_attn_out,
    w_up,
    b_up,
    w_down,
    b_down,
):
    b = lax.axis_index("branch")
    t = lax.axis_index("tensor")
    dp = lax.axis_index("dp")
    x_id, ring_id = lax.rem(dp, 2), dp // 2
    rows, quarter = inputs.shape
    half = 2 * quarter
    full = 4 * quarter
    heads_w = w_qkv.shape[2] // 2
    units = w_up.shape[1] // 2
    ids = jnp.stack([t, b]).astype(jnp.int32)

    def over_branch(v):
        return lax.ppermute(v, "branch", SWAP)

    def over_tensor(v):
        return lax.ppermute(v, "tensor", SWAP)

    def part(w, axis, index, size):
        return lax.dynamic_slice_in_dim(w, index * size, size, axis)

    x_got, x_far = over_tensor(inputs), over_branch(inputs)
    g_own, _ = lax.optimization_barrier((cotangent, x_far))
    g_got = over_tensor(g_own)
    aux = jnp.concatenate([ln_gain[None], ln_bias[None], jnp.zeros((14, quarter), BF16)], 0)
    aux_got = over_tensor(aux)
    w_three = jnp.transpose(w_qkv, (1, 0, 2))
    far_q = over_branch(part(w_three, 2, 1 - b, heads_w))
    far_u = over_branch(part(w_up, 1, 1 - b, units))
    bias_up = b_up.reshape(1, 2 * units)
    cosines, sines = rotary_tables(positions)
    span, start = spans(positions)
    aux_got, cosines, sines, span, start = lax.optimization_barrier(
        (aux_got, cosines, sines, span, start)
    )
    aux_half = jnp.where(
        t == 0, jnp.concatenate([aux, aux_got], 1), jnp.concatenate([aux_got, aux], 1)
    )
    aux_all = jnp.concatenate([aux_half, over_branch(aux_half)], 1)
    (x_got, x_far, aux_all, far_q, far_u, bias_up, cosines, sines) = lax.optimization_barrier(
        (x_got, x_far, aux_all, far_q, far_u, bias_up, cosines, sines)
    )
    x_pieces = (inputs, x_got, x_far, over_branch(x_got))
    normed, active, slope, qkv, stat = enter(
        ids, x_pieces, aux_all, w_three, far_q, w_up, far_u, bias_up, cosines, sines
    )
    g_far = over_branch(cotangent)
    far_a = over_branch(part(w_attn_out, 0, 1 - b, heads_w))
    far_d = over_branch(part(w_down, 0, 1 - b, units))
    g_got, g_far, far_a, far_d, active = lax.optimization_barrier(
        (g_got, g_far, far_a, far_d, active)
    )
    g_pieces = (cotangent, g_got, g_far, over_branch(g_got))
    g_all, down_near, down_send = down_grads(ids, g_pieces, active)

    def chained(near, far):
        return Chain(near, far, dp_size, x_id, ring_id)

    def attend(pair):
        return lambda *v: attention(pair, *v, cosines, sines, span, start)

    steps = Steps()
    down = chained(down_near, down_send)
    def spent(g, n, sl, ac):
        return [
            *up_grads(ids, g, n, sl, w_down, far_d, w_attn_out, far_a),
            *forward_term(ids, ac, w_down, far_d),
        ]

    d_hidden, d_mixed, up_near, up_send, bup, term = steps.run(
        [], [down], spent, g_all, normed, slope, active
    )
    up = chained(up_near, up_send)
    mixed0, d_joint0, near0, send0 = steps.run(
        [down], [up, down], attend(0), qkv, d_mixed, normed, g_all
    )
    late0 = chained(near0, send0)
    mixed1, d_joint1, near1, send1 = steps.run(
        [up, down], [late0, down, up], attend(1), qkv, d_mixed, normed, g_all
    )
    late1 = chained(near1, send1)

    def finish(ac, m0, m1, dj0, dj1, dh):
        return leave(
            ids,
            x_pieces,
            stat,
            aux_all,
            (dj0, dj1),
            dh,
            w_three,
            far_q,
            w_up,
            far_u,
            (m0, m1),
            w_attn_out,
            far_a,
            ac,
        )

    d_near, d_far, row_sums, sums, term_near, term_far = steps.run(
        [late0, down, up],
        [late1, late0, down, up],
        finish,
        term,
        mixed0,
        mixed1,
        d_joint0,
        d_joint1,
        d_hidden,
    )
    g_float = cotangent.astype(F32)
    terms, grads = Scatter(term_near, term_far, t), Scatter(d_near, d_far, t)
    moving = [late1, late0, down, up]

    def spread(rs):
        return (rs + over_branch(rs),)

    chains = [down, up, late1, late0]
    small = jnp.concatenate(
        [
            sums.reshape(4, half),
            bup.reshape(units // half, half),
            jnp.pad(jnp.sum(g_float, axis=0), (0, quarter))[None],
            jnp.zeros((9, half), F32),
        ]
    )
    (row_sums,) = steps.run(
        chains,
        [*(c for c in chains if c.stage + 1 < len(c.hops)), terms, grads],
        spread,
        row_sums,
        extra=(late1, small),
    )
    flag = b ^ x_id
    gradients = {}

    def lay(*operands):
        if down.other is not None and "down" not in gradients:
            gradients["down"] = place(
                emit_plain,
                flag,
                [down.pieces()],
                [(2 * units, half)],
                [(units, half)],
                [lambda k, s, f: (k, 0)],
                "place_down",
            )[0]
        if up.other is not None and "up" not in gradients:
            gradients["up"] = place(
                emit_plain,
                flag,
                [up.pieces()],
                [(half, 2 * units)],
                [(half, units)],
                [lambda k, s, f: (0, k)],
                "place_up",
            )[0]
        return [v + over_tensor(v) for v in operands]

    for turn in itertools.count(1):
        begin = [terms if turn == 1 else grads]
        operands = [row_sums] if turn == 1 else []
        moving = [c for c in (*chains, terms, grads) if c.moving is not None]
        ready = [c for c in (*chains, *begin) if c.stage + (c in moving) < len(c.hops)]
        if turn > 2 and not ready:
            break
        out = steps.run(moving, ready, lay, *operands)
        if turn == 1:
            (row_sums,) = out
    for c in (*chains, terms, grads):
        if c.moving is not None:
            c.finish()
    lay()

    row_sums = row_sums * (1.0 / full)
    output = (inputs.astype(F32) + terms.near + b_down.astype(F32)).astype(BF16)
    d_own = grads.near
    mean, inv_root = stat[:, 0:1], stat[:, 1:2]
    unit_own = (inputs.astype(F32) - mean) * inv_root
    input_grad = g_float + inv_root * (
        d_own * ln_gain.astype(F32)
        - row_sums[:, 0, :].reshape(rows, 1)
        - unit_own * row_sums[:, 1, :].reshape(rows, 1)
    )
    output, input_grad, gradients["down"], gradients["up"], late1.other = lax.optimization_barrier(
        (output, input_grad, gradients["down"], gradients["up"], late1.other)
    )
    small = late1.value[half : half + 8].astype(F32) + late1.other[half : half + 8].astype(F32)
    sums = small[:4].reshape(2, full)
    own = part(sums, 1, t, quarter)
    for k, v in (
        (1, part(sums, 1, 1 - t, quarter)),
        (2, part(sums, 1, 2 + t, quarter)),
        (3, part(sums, 1, 3 - t, quarter)),
    ):
        own = own + lax.ppermute(v, ("branch", "tensor"), [(i, i ^ k) for i in range(4)])
    bup = small[4:6].reshape(units)
    bup_far = over_branch(bup)
    grad_bup = jnp.where(b == 0, jnp.concatenate([bup, bup_far]), jnp.concatenate([bup_far, bup]))

    grad_qkv, grad_aout = place(
        emit_late,
        flag,
        [c.pieces() for c in (late0, late1)],
        [(3, half, 2 * heads_w), (2 * heads_w, half)],
        [(3, half, PAIR), (PAIR, half)],
        [lambda k, s, f: (0, 0, 2 * k + s), lambda k, s, f: (2 * k + s, 0)],
        "place_late",
    )
    return (
        output,
        input_grad,
        own[0],
        own[1],
        jnp.transpose(grad_qkv, (1, 0, 2)),
        grad_aout,
        gradients["up"],
        grad_bup,
        gradients["down"],
        small[6, :quarter],
    )


def solution(mesh):
    features = ("branch", "tensor")
    in_specs = (
        P("dp", features),
        P("dp", features),
        P("dp"),
        P("dp"),
        P("dp"),
        P(features),
        P(features),
        P("branch", None, "tensor"),
        P("tensor", "branch"),
        P("branch", "tensor"),
        P("tensor"),
        P("tensor", "branch"),
        P(features),
    )
    out_specs = (
        P("dp", features),
        P("dp", features),
        P(features),
        P(features),
        P("branch", None, "tensor"),
        P("tensor", "branch"),
        P("branch", "tensor"),
        P("tensor"),
        P("tensor", "branch"),
        P(features),
    )
    return jax.shard_map(
        functools.partial(shards, mesh.shape["dp"]),
        mesh=mesh,
        in_specs=in_specs,
        out_specs=out_specs,
        check_vma=False,
    )
```

```python
import functools
import itertools

import jax
import jax.numpy as jnp
from jax import lax
from jax.experimental import pallas as pl
from jax.experimental.pallas import tpu as pltpu
from jax.sharding import PartitionSpec as P

HEAD_DIM = 64
ROTARY = 32
PAIR = 2 * HEAD_DIM
QB = 128
KC = 256
LONGEST = 1024
EPS = 1e-05
NEG = -1e30
F32 = jnp.float32
BF16 = jnp.bfloat16
SWAP = [(0, 1), (1, 0)]
GELU_A = 0.7978845608028654
GELU_B = 0.044715


def nn(a, b):
    return lax.dot_general(a, b, (((1,), (0,)), ((), ())), preferred_element_type=F32)


def nt(a, b):
    return lax.dot_general(a, b, (((1,), (1,)), ((), ())), preferred_element_type=F32)


def tn(a, b):
    return lax.dot_general(a, b, (((0,), (0,)), ((), ())), preferred_element_type=F32)


def partner(x, even):
    width = x.shape[1]
    return jnp.where(even, pltpu.roll(x, width - 1, 1), pltpu.roll(x, 1, 1))


def cols(pair, part):
    return slice((3 * pair + part) * PAIR, (3 * pair + part + 1) * PAIR)


def attention_kernel(
    pair,
    most,
    span_ref,
    start_ref,
    qkv_hbm,
    dmix_hbm,
    cos_hbm,
    sin_hbm,
    normed_hbm,
    g_hbm,
    mixed_ref,
    dj_ref,
    near_ref,
    far_ref,
    q_s,
    qt_s,
    g_s,
    gt_s,
    k_s,
    v_s,
    kt_s,
    vt_s,
    s_s,
    d_s,
    p_s,
    e_s,
    dk_s,
    dv_s,
    qkv_ref,
    dmix_ref,
    cos_ref,
    sin_ref,
    normed_s,
    ct_s,
    arrived,
):
    pairs = 1
    rows = qkv_ref.shape[0]
    fetch = [
        pltpu.make_async_copy(src, dst, arrived.at[n])
        for n, (src, dst) in enumerate(
            (
                (qkv_hbm.at[:, 3 * pair * PAIR : 3 * (pair + 1) * PAIR], qkv_ref),
                (dmix_hbm.at[:, pair * PAIR : (pair + 1) * PAIR], dmix_ref),
                (cos_hbm, cos_ref),
                (sin_hbm, sin_ref),
                (normed_hbm, normed_s),
                (g_hbm, ct_s),
            )
        )
    ]
    for copy in fetch:
        copy.start()
    fetch[0].wait()
    fetch[1].wait()
    rows = qkv_ref.shape[0]
    lane = lax.broadcasted_iota(jnp.int32, (QB, PAIR), 1)
    even = lane % 2 == 0
    first = lane < HEAD_DIM
    top = lax.broadcasted_iota(jnp.int32, (PAIR, QB), 0) < HEAD_DIM
    scale = HEAD_DIM**-0.5

    for p in range(pairs):
        k_s[p, :QB, :] = jnp.zeros((QB, PAIR), BF16)
        v_s[p, :QB, :] = jnp.zeros((QB, PAIR), BF16)
        kt_s[p, :, :QB] = jnp.zeros((PAIR, QB), BF16)
        vt_s[p, :, :QB] = jnp.zeros((PAIR, QB), BF16)
        dk_s[p, :QB, :] = jnp.zeros((QB, PAIR), F32)
        dv_s[p, :QB, :] = jnp.zeros((QB, PAIR), F32)

    @pl.loop(0, rows // QB)
    def _(i):
        at = pl.ds(pl.multiple_of(i * QB, QB), QB)
        to = pl.ds(pl.multiple_of(i * QB + QB, QB), QB)
        for p in range(pairs):
            q = qkv_ref[at, cols(p, 0)].astype(F32)
            k = qkv_ref[at, cols(p, 1)]
            v = qkv_ref[at, cols(p, 2)]
            g = dmix_ref[at, p * PAIR : (p + 1) * PAIR].astype(F32)
            q_s[p, i, :QB, :] = jnp.where(first, q, 0.0).astype(BF16)
            q_s[p, i, QB:, :] = jnp.where(first, 0.0, q).astype(BF16)
            g_s[p, i, :QB, :] = jnp.where(first, g, 0.0).astype(BF16)
            g_s[p, i, QB:, :] = jnp.where(first, 0.0, g).astype(BF16)
            q, g = q.T, g.T
            qt_s[p, i, :, :QB] = jnp.where(top, q, 0.0).astype(BF16)
            qt_s[p, i, :, QB:] = jnp.where(top, 0.0, q).astype(BF16)
            gt_s[p, i, :, :QB] = jnp.where(top, g, 0.0).astype(BF16)
            gt_s[p, i, :, QB:] = jnp.where(top, 0.0, g).astype(BF16)
            k_s[p, to, :] = k
            v_s[p, to, :] = v
            kt_s[p, :, to] = k.astype(F32).T.astype(BF16)
            vt_s[p, :, to] = v.astype(F32).T.astype(BF16)
            dk_s[p, to, :] = jnp.zeros((QB, PAIR), F32)
            dv_s[p, to, :] = jnp.zeros((QB, PAIR), F32)

    fetch[2].wait()
    fetch[3].wait()
    key_slot = lax.broadcasted_iota(jnp.int32, (KC, 2 * QB), 0)
    query_slot = lax.broadcasted_iota(jnp.int32, (1, 2 * QB), 1) % QB

    def block(i, n):
        base = (i + 2) * QB - n * KC
        spots = [pl.ds(pl.multiple_of(base + j * KC, QB), KC) for j in range(n)]
        whole = pl.ds(pl.multiple_of(base, QB), n * KC)
        query = query_slot + (i * QB + QB - base)
        start = start_ref[i] + (QB - base)
        here = pl.ds(pl.multiple_of(i * QB, QB), QB)
        pr = range(pairs)
        peak = [None] * pairs
        for j in range(n):
            ok = (key_slot >= start - j * KC) & (key_slot <= query - j * KC)
            for p in pr:
                s = jnp.where(ok, nn(k_s[p, spots[j], :], qt_s[p, i]), NEG)
                s_s[p, j] = s
                m = jnp.max(s.reshape(KC // 8, 8, 2 * QB), axis=0)
                peak[p] = m if peak[p] is None else jnp.maximum(peak[p], m)
        for j in range(n):
            for p in pr:
                d_s[p, j] = nn(v_s[p, spots[j], :], gt_s[p, i])
        peak = [jnp.max(m, axis=0, keepdims=True) for m in peak]
        total = [0.0] * pairs
        delta = [0.0] * pairs
        for j in range(n):
            for p in pr:
                e = jnp.exp(s_s[p, j] - peak[p])
                s_s[p, j] = e
                total[p] += jnp.sum(e.reshape(KC // 8, 8, 2 * QB), axis=0)
                delta[p] += jnp.sum((e * d_s[p, j]).reshape(KC // 8, 8, 2 * QB), axis=0)
        inverse = [1.0 / jnp.sum(x, axis=0, keepdims=True) for x in total]
        delta = [jnp.sum(x, axis=0, keepdims=True) * r for x, r in zip(delta, inverse)]
        for j in range(n):
            for p in pr:
                prob = s_s[p, j] * inverse[p]
                p_s[p, j * KC : (j + 1) * KC, :] = prob.astype(BF16)
                e_s[p, j * KC : (j + 1) * KC, :] = (prob * (d_s[p, j] - delta[p])).astype(BF16)
        for p in pr:
            o = nn(vt_s[p, :, whole], p_s[p, : n * KC, :])
            mixed_ref[here, p * PAIR : (p + 1) * PAIR] = (
                jnp.where(top, o[:, :QB], o[:, QB:]).T.astype(BF16)
            )
            dv_s[p, whole, :] += nn(p_s[p, : n * KC, :], g_s[p, i])
            dk_s[p, whole, :] += nn(e_s[p, : n * KC, :], q_s[p, i])
            d = nn(kt_s[p, :, whole], e_s[p, : n * KC, :])
            d = (jnp.where(top, d[:, :QB], d[:, QB:]) * scale).T
            d = d * cos_ref[here, :] - partner(d, even) * sin_ref[here, :]
            dj_ref[here, cols(p, 0)] = d.astype(BF16)

    @pl.loop(0, rows // QB)
    def _(i):
        for n in range(1, most + 1):
            pl.when(span_ref[i] == n)(functools.partial(block, i, n))

    @pl.loop(0, rows // QB)
    def _(i):
        at = pl.ds(pl.multiple_of(i * QB, QB), QB)
        to = pl.ds(pl.multiple_of(i * QB + QB, QB), QB)
        cosines = cos_ref[at, :]
        sines = sin_ref[at, :]
        for p in range(pairs):
            d = dk_s[p, to, :]
            d = d * cosines - partner(d, even) * sines
            dj_ref[at, cols(p, 1)] = d.astype(BF16)
            dj_ref[at, cols(p, 2)] = dv_s[p, to, :].astype(BF16)

    fetch[4].wait()
    fetch[5].wait()
    half, split = normed_s.shape[1] // 2, 3 * PAIR
    for p in range(pairs):
        at_p = p * 4 * PAIR
        for at, out in ((slice(half, 2 * half), far_ref), (slice(0, half), near_ref)):
            out[:half, at_p : at_p + split] = tn(
                normed_s[:, at], dj_ref[:, p * split : (p + 1) * split]
            ).astype(BF16)
            out[:half, at_p + split : at_p + 4 * PAIR] = tn(
                ct_s[:, at], mixed_ref[:, p * PAIR : (p + 1) * PAIR]
            ).astype(BF16)


def spans(positions):
    rows = positions.shape[0]
    blocks = rows // QB
    start = (jnp.arange(rows, dtype=jnp.int32) - positions).reshape(blocks, 1, QB)
    span = (jnp.arange(blocks, dtype=jnp.int32) - start[:, 0, 0] // QB + 2) // 2
    return span, jnp.concatenate([start, start], axis=2)


def attention(pair, qkv, dmix, normed, g_all, cosines, sines, span, start):
    rows = qkv.shape[0]
    blocks = rows // QB
    padded = rows + QB
    most = LONGEST // KC + 1
    half = normed.shape[1] // 2
    vmem = pl.BlockSpec(memory_space=pltpu.VMEM)
    smem = pl.BlockSpec(memory_space=pltpu.SMEM)
    return pl.pallas_call(
        functools.partial(attention_kernel, pair, most),
        out_shape=[
            jax.ShapeDtypeStruct((rows, PAIR), BF16),
            jax.ShapeDtypeStruct((rows, 3 * PAIR), BF16),
        ]
        + [jax.ShapeDtypeStruct((half, 4 * PAIR), BF16)] * 2,
        in_specs=[smem, vmem] + [pl.BlockSpec(memory_space=pl.ANY)] * 6,
        out_specs=[vmem] * 4,
        scratch_shapes=[
            pltpu.VMEM((1, blocks, 2 * QB, PAIR), BF16),
            pltpu.VMEM((1, blocks, PAIR, 2 * QB), BF16),
            pltpu.VMEM((1, blocks, 2 * QB, PAIR), BF16),
            pltpu.VMEM((1, blocks, PAIR, 2 * QB), BF16),
            pltpu.VMEM((1, padded, PAIR), BF16),
            pltpu.VMEM((1, padded, PAIR), BF16),
            pltpu.VMEM((1, PAIR, padded), BF16),
            pltpu.VMEM((1, PAIR, padded), BF16),
            pltpu.VMEM((1, most, KC, 2 * QB), F32),
            pltpu.VMEM((1, most, KC, 2 * QB), F32),
            pltpu.VMEM((1, most * KC, 2 * QB), BF16),
            pltpu.VMEM((1, most * KC, 2 * QB), BF16),
            pltpu.VMEM((1, padded, PAIR), F32),
            pltpu.VMEM((1, padded, PAIR), F32),
            pltpu.VMEM((rows, 3 * PAIR), BF16),
            pltpu.VMEM((rows, PAIR), BF16),
            pltpu.VMEM(cosines.shape, F32),
            pltpu.VMEM(sines.shape, F32),
            pltpu.VMEM(normed.shape, BF16),
            pltpu.VMEM(g_all.shape, BF16),
            pltpu.SemaphoreType.DMA((6,)),
        ],
        compiler_params=pltpu.CompilerParams(vmem_limit_bytes=40 << 20),
        cost_estimate=pl.CostEstimate(flops=0, bytes_accessed=0, transcendentals=0),
        name="attention",
    )(span, start, qkv, dmix, cosines, sines, normed, g_all)


def picked(first, own, got, far_own, far_got):
    own, got, far_own, far_got = (v[...].astype(F32) for v in (own, got, far_own, far_got))
    return jnp.concatenate(
        [
            jnp.where(first, own, got),
            jnp.where(first, got, own),
            jnp.where(first, far_own, far_got),
            jnp.where(first, far_got, far_own),
        ],
        1,
    )


def resident(shape):
    return pl.BlockSpec(shape, lambda i: (0,) * len(shape), pipeline_mode=pl.Buffered(1))


def enter_kernel(
    ids,
    own,
    got,
    far_own,
    far_got,
    aux_ref,
    near_q,
    far_q,
    near_u,
    far_u,
    bias_ref,
    cos_ref,
    sin_ref,
    normed_ref,
    active_ref,
    slope_ref,
    qkv_ref,
    stat_ref,
):
    x = picked(ids[0] == 0, own, got, far_own, far_got)
    rows, full = x.shape
    half = full // 2
    mean = jnp.mean(x, axis=1, keepdims=True)
    center = x - mean
    inv_root = lax.rsqrt(jnp.mean(center * center, axis=1, keepdims=True) + EPS)
    normed = (
        center * inv_root * aux_ref[0:1, :].astype(F32) + aux_ref[1:2, :].astype(F32)
    ).astype(BF16)
    normed_ref[...] = normed
    lane = lax.broadcasted_iota(jnp.int32, (rows, PAIR), 1)
    stat_ref[...] = jnp.where(lane == 0, mean, inv_root)
    near, far = normed[:, :half], normed[:, half:]
    hidden = nn(near, near_u[...]) + nn(far, far_u[...]) + bias_ref[0:1, :].astype(F32)
    square = hidden * hidden
    bend = jnp.tanh(GELU_A * hidden * (1.0 + GELU_B * square))
    up = 0.5 * (1.0 + bend)
    active = (hidden * up).astype(BF16)
    active_ref[...] = active
    slope_ref[...] = up + (0.5 * GELU_A) * hidden * (1.0 - bend * bend) * (
        1.0 + 3.0 * GELU_B * square
    )
    even = lane % 2 == 0
    cosines, sines = cos_ref[...], sin_ref[...]
    for j in range(3):
        joint = nn(near, near_q[j]) + nn(far, far_q[j])
        for p in range(joint.shape[1] // PAIR):
            v = joint[:, p * PAIR : (p + 1) * PAIR]
            if j < 2:
                v = v * cosines + partner(v, even) * sines
            if j == 0:
                v = v * HEAD_DIM**-0.5
            at = (3 * p + j) * PAIR
            qkv_ref[:, at : at + PAIR] = v.astype(BF16)


def rows_of(step, width):
    return pl.BlockSpec((step, width), lambda i, ids: (i, 0))


def fixed(shape, index=None):
    if index is None:
        return pl.BlockSpec(
            shape, lambda i, ids: (0,) * len(shape), pipeline_mode=pl.Buffered(1)
        )
    return pl.BlockSpec(shape, lambda i, ids: index(ids), pipeline_mode=pl.Buffered(1))


def by_rows(kernel, steps, ids, ins, outs, name, scratch=()):
    return pl.pallas_call(
        kernel,
        grid_spec=pltpu.PrefetchScalarGridSpec(
            num_scalar_prefetch=1,
            grid=(steps,),
            in_specs=[s for _, s in ins],
            out_specs=[s for _, _, s in outs],
            scratch_shapes=scratch,
        ),
        out_shape=[jax.ShapeDtypeStruct(s, d) for s, d, _ in outs],
        compiler_params=pltpu.CompilerParams(vmem_limit_bytes=50 << 20),
        cost_estimate=pl.CostEstimate(flops=0, bytes_accessed=0, transcendentals=0),
        name=name,
    )(ids, *[a for a, _ in ins])


def enter(ids, pieces, aux, w_three, far_q, w_up, far_u, bias, cosines, sines):
    rows, quarter = pieces[0].shape
    full, half = 4 * quarter, 2 * quarter
    units, heads_w = far_u.shape[1], far_q.shape[2]
    step = rows // 8
    ins = [(v, rows_of(step, quarter)) for v in pieces] + [
        (aux, fixed(aux.shape)),
        (w_three, fixed((3, half, heads_w), lambda ids: (0, 0, ids[1]))),
        (far_q, fixed(far_q.shape)),
        (w_up, fixed((half, units), lambda ids: (0, ids[1]))),
        (far_u, fixed(far_u.shape)),
        (bias, fixed((1, units), lambda ids: (0, ids[1]))),
        (cosines, rows_of(step, PAIR)),
        (sines, rows_of(step, PAIR)),
    ]
    outs = [
        ((rows, full), BF16, rows_of(step, full)),
        ((rows, units), BF16, rows_of(step, units)),
        ((rows, units), F32, rows_of(step, units)),
        ((rows, 3 * heads_w), BF16, rows_of(step, 3 * heads_w)),
        ((rows, PAIR), F32, rows_of(step, PAIR)),
    ]
    return by_rows(enter_kernel, 8, ids, ins, outs, "enter")


def down_kernel(
    ids,
    own,
    got,
    far_own,
    far_got,
    active_ref,
    g_ref,
    near_ref,
    far_ref,
    total_s,
):
    i = pl.program_id(0)
    g = picked(ids[0] == 0, own, got, far_own, far_got).astype(BF16)
    half = g.shape[1] // 2
    g_ref[...] = g

    @pl.when(i == 0)
    def _():
        total_s[...] = tn(active_ref[...], g)

    @pl.when(i > 0)
    def _():
        total_s[...] += tn(active_ref[...], g)

    @pl.when(i == pl.num_programs(0) - 1)
    def _():
        near_ref[...] = total_s[:, :half].astype(BF16)
        far_ref[...] = total_s[:, half:].astype(BF16)


def down_grads(ids, pieces, active):
    rows, quarter = pieces[0].shape
    full, half, units = 4 * quarter, 2 * quarter, active.shape[1]
    step = rows // 2
    ins = [(v, rows_of(step, quarter)) for v in pieces] + [
        (active, rows_of(step, units)),
    ]
    outs = [
        ((rows, full), BF16, rows_of(step, full)),
        ((units, half), BF16, fixed((units, half))),
        ((units, half), BF16, fixed((units, half))),
    ]
    return by_rows(
        down_kernel,
        2,
        ids,
        ins,
        outs,
        "down_grads",
        [pltpu.VMEM((units, full), F32)],
    )


def up_kernel(
    ids,
    g_ref,
    normed_ref,
    slope_ref,
    near_d,
    far_d,
    near_a,
    far_a,
    dh_ref,
    dm_ref,
    near_ref,
    far_ref,
    sum_ref,
    total_s,
):
    i = pl.program_id(0)
    half = g_ref.shape[1] // 2
    da = nt(g_ref[:, :half], near_d[...]) + nt(g_ref[:, half:], far_d[...])
    dm_ref[...] = (nt(g_ref[:, :half], near_a[...]) + nt(g_ref[:, half:], far_a[...])).astype(BF16)
    dh = (da * slope_ref[...]).astype(BF16)
    dh_ref[...] = dh
    sums = jnp.sum(dh.astype(F32), axis=0, keepdims=True)

    @pl.when(i == 0)
    def _():
        total_s[...] = tn(normed_ref[...], dh)
        sum_ref[...] = sums

    @pl.when(i > 0)
    def _():
        total_s[...] += tn(normed_ref[...], dh)
        sum_ref[...] += sums

    @pl.when(i == pl.num_programs(0) - 1)
    def _():
        near_ref[...] = total_s[:half, :].astype(BF16)
        far_ref[...] = total_s[half:, :].astype(BF16)


def up_grads(ids, g_all, normed, slope, w_down, far_d, w_attn_out, far_a):
    rows, full = g_all.shape
    half, units = full // 2, slope.shape[1]
    heads_w = far_a.shape[0]
    step = rows // 4
    ins = [
        (g_all, rows_of(step, full)),
        (normed, rows_of(step, full)),
        (slope, rows_of(step, units)),
        (w_down, fixed((units, half), lambda ids: (ids[1], 0))),
        (far_d, fixed(far_d.shape)),
        (w_attn_out, fixed((heads_w, half), lambda ids: (ids[1], 0))),
        (far_a, fixed(far_a.shape)),
    ]
    outs = [
        ((rows, units), BF16, rows_of(step, units)),
        ((rows, heads_w), BF16, rows_of(step, heads_w)),
        ((half, units), BF16, fixed((half, units))),
        ((half, units), BF16, fixed((half, units))),
        ((1, units), F32, fixed((1, units))),
    ]
    return by_rows(
        up_kernel,
        4,
        ids,
        ins,
        outs,
        "up_grads",
        [pltpu.VMEM((full, units), F32)],
    )


def leave_kernel(
    ids,
    own,
    got,
    far_own,
    far_got,
    stat_ref,
    aux_ref,
    dj0_ref,
    dj1_ref,
    dh_ref,
    near_q,
    far_q,
    near_u,
    far_u,
    mixed0_ref,
    mixed1_ref,
    near_a,
    far_a,
    term_ref,
    near_ref,
    far_ref,
    row_ref,
    sum_ref,
    term_near,
    term_far,
):
    i = pl.program_id(0)
    mixed = jnp.concatenate([mixed0_ref[...], mixed1_ref[...]], 1)
    half = near_ref.shape[1]
    term_near[...] = term_ref[:, :half] + nn(mixed, near_a[...])
    term_far[...] = (term_ref[:, half:] + nn(mixed, far_a[...])).astype(BF16)
    x = picked(ids[0] == 0, own, got, far_own, far_got)
    unit = (x - stat_ref[:, 0:1]) * stat_ref[:, 1:2]
    dh = dh_ref[...]
    near = nt(dh, near_u[...])
    far = nt(dh, far_u[...])
    for j in range(3):
        cut = slice(j * PAIR, (j + 1) * PAIR)
        dj = jnp.concatenate([dj0_ref[:, cut], dj1_ref[:, cut]], 1)
        near += nt(dj, near_q[j])
        far += nt(dj, far_q[j])
    near_ref[...] = near
    far_ref[...] = far.astype(BF16)
    both = jnp.concatenate([near, far], 1)
    scaled = both * aux_ref[0:1, :].astype(F32)
    first = jnp.sum(scaled, axis=1, keepdims=True)
    second = jnp.sum(scaled * unit, axis=1, keepdims=True)
    lane = lax.broadcasted_iota(jnp.int32, (x.shape[0], PAIR), 1)
    row_ref[0] = jnp.where(lane == 0, first, second).T[:8]
    sums = jnp.concatenate(
        [
            jnp.sum(both * unit, axis=0, keepdims=True),
            jnp.sum(both, axis=0, keepdims=True),
        ],
        0,
    )

    @pl.when(i == 0)
    def _():
        sum_ref[...] = sums

    @pl.when(i > 0)
    def _():
        sum_ref[...] += sums


def term_kernel(ids, active_ref, near_d, far_d, term_ref):
    half = near_d.shape[1]
    term_ref[:, :half] = nn(active_ref[...], near_d[...])
    term_ref[:, half:] = nn(active_ref[...], far_d[...])


def forward_term(ids, active, w_down, far_d):
    rows, units = active.shape
    half = far_d.shape[1]
    step = rows // 4
    ins = [
        (active, rows_of(step, units)),
        (w_down, fixed((units, half), lambda ids: (ids[1], 0))),
        (far_d, fixed(far_d.shape)),
    ]
    outs = [((rows, 2 * half), F32, rows_of(step, 2 * half))]
    return by_rows(term_kernel, 4, ids, ins, outs, "forward_term")


def leave(
    ids,
    pieces,
    stat,
    aux,
    d_joints,
    d_hidden,
    w_three,
    far_q,
    w_up,
    far_u,
    mixed,
    w_attn_out,
    far_a,
    term,
):
    rows, quarter = pieces[0].shape
    full, half = 4 * quarter, 2 * quarter
    units, heads_w = far_u.shape[1], far_q.shape[2]
    step = rows // 4
    ins = (
        [(v, rows_of(step, quarter)) for v in pieces]
        + [(stat, rows_of(step, PAIR)), (aux, fixed(aux.shape))]
        + [(d, rows_of(step, 3 * PAIR)) for d in d_joints]
        + [
            (d_hidden, rows_of(step, units)),
            (w_three, fixed((3, half, heads_w), lambda ids: (0, 0, ids[1]))),
            (far_q, fixed(far_q.shape)),
            (w_up, fixed((half, units), lambda ids: (0, ids[1]))),
            (far_u, fixed(far_u.shape)),
        ]
        + [(m, rows_of(step, PAIR)) for m in mixed]
        + [
            (w_attn_out, fixed((heads_w, half), lambda ids: (ids[1], 0))),
            (far_a, fixed(far_a.shape)),
            (term, rows_of(step, full)),
        ]
    )
    outs = [
        ((rows, half), F32, rows_of(step, half)),
        ((rows, half), BF16, rows_of(step, half)),
        ((4, 8, step), F32, pl.BlockSpec((1, 8, step), lambda i, ids: (i, 0, 0))),
        ((2, full), F32, fixed((2, full))),
        ((rows, half), F32, rows_of(step, half)),
        ((rows, half), BF16, rows_of(step, half)),
    ]
    return by_rows(leave_kernel, 4, ids, ins, outs, "leave")


def rotary_tables(positions):
    lane = jnp.arange(PAIR, dtype=jnp.int32)
    feature = lane % HEAD_DIM
    inverse = 10000.0 ** (-(2.0 * (feature // 2).astype(F32)) / ROTARY)
    angle = positions.astype(F32)[:, None] * inverse[None, :]
    turned = (feature < ROTARY)[None, :]
    sign = jnp.where(feature % 2 == 0, -1.0, 1.0)[None, :]
    cosines = jnp.where(turned, jnp.cos(angle), 1.0)
    sines = jnp.where(turned, jnp.sin(angle) * sign, 0.0)
    return cosines, sines


class Chain:
    held = ("value", "other", "far")

    def __init__(self, value, far, size, x_id, place):
        self.low, self.place = x_id == 0, place
        self.value, self.far, self.keep = jnp.where(self.low, far, value), far, value
        self.moving = self.other = self.crossed = None
        line = size // 2
        steps = line // 2 - 1

        def perm(pairs):
            return [(2 * i + x, 2 * j + x) for i, j in pairs for x in range(2)]

        self.pair = [(i, i ^ 1) for i in range(size)]
        self.hops = [(self.pair, None)]
        if line > 1:
            for k in range(steps):
                self.hops.append((perm([(k, k + 1), (line - 1 - k, line - 2 - k)]), None))
            mid = line // 2
            self.hops.append((perm([(mid - 1, mid), (mid, mid - 1)]), None))
            for k in reversed(range(steps)):
                self.hops.append((perm([(k + 1, k), (line - 2 - k, line - 1 - k)]), (k, line - 1 - k)))
        self.hops.append((self.pair, None))
        self.stage = 0
        self.cross = [
            (2 * i + c, 2 * (i ^ 1) + (c if i % 2 else 1 - c)) for i in range(size) for c in range(2)
        ]
        self.trade = [(2 * i + c, 2 * i + 1 - c) for i in range(1, size, 2) for c in range(2)]

    def busy(self):
        return self.stage < len(self.hops)

    def start(self):
        if self.stage == 0:
            self.moving = lax.ppermute(self.value, ("dp", "branch"), self.cross)
            self.crossed = lax.ppermute(self.far, ("dp", "branch"), self.trade)
        else:
            self.moving = lax.ppermute(self.value, "dp", self.hops[self.stage][0])

    def finish(self):
        got, self.moving = self.moving, None
        ends = self.hops[self.stage][1]
        if self.stage == len(self.hops) - 1:
            self.other = got
        elif ends is None:
            base = self.value
            if self.stage == 0:
                base = jnp.where(self.low, self.keep, self.crossed)
            self.value = (base.astype(F32) + got.astype(F32)).astype(base.dtype)
        else:
            here = (self.place == ends[0]) | (self.place == ends[1])
            self.value = jnp.where(here, got, self.value)
        self.far = None
        self.stage += 1

    def pieces(self):
        return (self.value, self.other)


class Scatter:
    held = ("value", "near")
    hops = (0, 1)

    def __init__(self, near, far, t):
        self.near, self.value, self.low = near, far, t == 0
        self.moving = self.far = None
        self.stage = 0

    def busy(self):
        return self.stage < 2

    def start(self):
        self.moving = lax.ppermute(self.value, ("branch", "tensor")[self.stage], SWAP)

    def finish(self):
        got, self.moving = self.moving, None
        if self.stage == 0:
            total = self.near + got.astype(F32)
            low, high = jnp.split(total, 2, axis=1)
            self.value = jnp.where(self.low, high, low).astype(BF16)
            self.near = jnp.where(self.low, low, high)
        else:
            self.near = self.near + got.astype(F32)
        self.stage += 1


class Steps:
    def __init__(self):
        self.before = []

    def run(self, finish, start, compute=None, *operands, extra=None):
        for c in finish:
            c.finish()
        if extra is not None:
            chain, rows = extra
            chain.value = jnp.concatenate([chain.value, rows.astype(BF16)], 0)
        touched = list({id(c): c for c in [*finish, *start]}.values())
        held = [(c, name) for c in touched for name in c.held if getattr(c, name) is not None]
        values, operands, _ = lax.optimization_barrier(
            ([getattr(c, name) for c, name in held], operands, self.before)
        )
        for (c, name), v in zip(held, values):
            setattr(c, name, v)
        for c in start:
            c.start()
        out = compute(*operands) if compute is not None else ()
        self.before = list(out)
        return out


def place_kernel(emit, count, flag_ref, *refs):
    own, other, outs = refs[:count], refs[count : 2 * count], refs[2 * count :]
    k, s = pl.program_id(0), pl.program_id(1)
    for c in range(count):
        pl.when((s == c) & (k == flag_ref[0]))(functools.partial(emit, own[c], outs))
        pl.when((s == c) & (k != flag_ref[0]))(functools.partial(emit, other[c], outs))


def place(emit, flag, pieces, out_shapes, out_blocks, maps, name):
    count = len(pieces)
    arrays = [p[0] for p in pieces] + [p[1] for p in pieces]
    grid_spec = pltpu.PrefetchScalarGridSpec(
        num_scalar_prefetch=1,
        grid=(2, count),
        in_specs=[pl.BlockSpec(a.shape, lambda k, s, f: (0, 0)) for a in arrays],
        out_specs=[pl.BlockSpec(blk, m) for blk, m in zip(out_blocks, maps)],
    )
    return pl.pallas_call(
        functools.partial(place_kernel, emit, count),
        grid_spec=grid_spec,
        out_shape=[jax.ShapeDtypeStruct(o, F32) for o in out_shapes],
        compiler_params=pltpu.CompilerParams(vmem_limit_bytes=48 << 20),
        cost_estimate=pl.CostEstimate(
            flops=0, bytes_accessed=6 * 2 * count * arrays[0].size, transcendentals=0
        ),
        name=name,
    )(flag.reshape(1).astype(jnp.int32), *arrays)


def emit_plain(src, outs):
    outs[0][...] = src[...].astype(F32)


def emit_late(src, outs):
    rows = outs[0].shape[1]
    for j in range(3):
        outs[0][j] = src[:rows, j * PAIR : (j + 1) * PAIR].astype(F32)
    outs[1][...] = src[:rows, 3 * PAIR :].astype(F32).T


def shards(
    dp_size,
    inputs,
    cotangent,
    seg_ids,
    pad_mask,
    positions,
    ln_gain,
    ln_bias,
    w_qkv,
    w_attn_out,
    w_up,
    b_up,
    w_down,
    b_down,
):
    b = lax.axis_index("branch")
    t = lax.axis_index("tensor")
    dp = lax.axis_index("dp")
    x_id, ring_id = lax.rem(dp, 2), dp // 2
    rows, quarter = inputs.shape
    half = 2 * quarter
    full = 4 * quarter
    heads_w = w_qkv.shape[2] // 2
    units = w_up.shape[1] // 2
    ids = jnp.stack([t, b]).astype(jnp.int32)

    def over_branch(v):
        return lax.ppermute(v, "branch", SWAP)

    def over_tensor(v):
        return lax.ppermute(v, "tensor", SWAP)

    def part(w, axis, index, size):
        return lax.dynamic_slice_in_dim(w, index * size, size, axis)

    x_got, x_far = over_tensor(inputs), over_branch(inputs)
    g_own, _ = lax.optimization_barrier((cotangent, x_far))
    g_got = over_tensor(g_own)
    aux = jnp.concatenate([ln_gain[None], ln_bias[None], jnp.zeros((14, quarter), BF16)], 0)
    aux_got = over_tensor(aux)
    w_three = jnp.transpose(w_qkv, (1, 0, 2))
    far_q = over_branch(part(w_three, 2, 1 - b, heads_w))
    far_u = over_branch(part(w_up, 1, 1 - b, units))
    bias_up = b_up.reshape(1, 2 * units)
    cosines, sines = rotary_tables(positions)
    span, start = spans(positions)
    aux_got, cosines, sines, span, start = lax.optimization_barrier(
        (aux_got, cosines, sines, span, start)
    )
    aux_half = jnp.where(
        t == 0, jnp.concatenate([aux, aux_got], 1), jnp.concatenate([aux_got, aux], 1)
    )
    aux_all = jnp.concatenate([aux_half, over_branch(aux_half)], 1)
    (x_got, x_far, aux_all, far_q, far_u, bias_up, cosines, sines) = lax.optimization_barrier(
        (x_got, x_far, aux_all, far_q, far_u, bias_up, cosines, sines)
    )
    x_pieces = (inputs, x_got, x_far, over_branch(x_got))
    normed, active, slope, qkv, stat = enter(
        ids, x_pieces, aux_all, w_three, far_q, w_up, far_u, bias_up, cosines, sines
    )
    g_far = over_branch(cotangent)
    far_a = over_branch(part(w_attn_out, 0, 1 - b, heads_w))
    far_d = over_branch(part(w_down, 0, 1 - b, units))
    g_got, g_far, far_a, far_d, active = lax.optimization_barrier(
        (g_got, g_far, far_a, far_d, active)
    )
    g_pieces = (cotangent, g_got, g_far, over_branch(g_got))
    g_all, down_near, down_send = down_grads(ids, g_pieces, active)

    def chained(near, far):
        return Chain(near, far, dp_size, x_id, ring_id)

    def attend(pair):
        return lambda *v: attention(pair, *v, cosines, sines, span, start)

    steps = Steps()
    down = chained(down_near, down_send)
    def spent(g, n, sl, ac):
        return [
            *up_grads(ids, g, n, sl, w_down, far_d, w_attn_out, far_a),
            *forward_term(ids, ac, w_down, far_d),
        ]

    d_hidden, d_mixed, up_near, up_send, bup, term = steps.run(
        [], [down], spent, g_all, normed, slope, active
    )
    up = chained(up_near, up_send)
    mixed0, d_joint0, near0, send0 = steps.run(
        [down], [up, down], attend(0), qkv, d_mixed, normed, g_all
    )
    late0 = chained(near0, send0)
    mixed1, d_joint1, near1, send1 = steps.run(
        [up, down], [late0, down, up], attend(1), qkv, d_mixed, normed, g_all
    )
    late1 = chained(near1, send1)

    def finish(ac, m0, m1, dj0, dj1, dh):
        return leave(
            ids,
            x_pieces,
            stat,
            aux_all,
            (dj0, dj1),
            dh,
            w_three,
            far_q,
            w_up,
            far_u,
            (m0, m1),
            w_attn_out,
            far_a,
            ac,
        )

    d_near, d_far, row_sums, sums, term_near, term_far = steps.run(
        [late0, down, up],
        [late1, late0, down, up],
        finish,
        term,
        mixed0,
        mixed1,
        d_joint0,
        d_joint1,
        d_hidden,
    )
    g_float = cotangent.astype(F32)
    terms, grads = Scatter(term_near, term_far, t), Scatter(d_near, d_far, t)
    moving = [late1, late0, down, up]

    def spread(rs):
        return (rs + over_branch(rs),)

    chains = [down, up, late1, late0]
    small = jnp.concatenate(
        [
            sums.reshape(4, half),
            bup.reshape(units // half, half),
            jnp.pad(jnp.sum(g_float, axis=0), (0, quarter))[None],
            jnp.zeros((9, half), F32),
        ]
    )
    (row_sums,) = steps.run(
        chains,
        [*(c for c in chains if c.stage + 1 < len(c.hops)), terms, grads],
        spread,
        row_sums,
        extra=(late1, small),
    )
    flag = b ^ x_id
    gradients = {}

    def lay(*operands):
        if down.other is not None and "down" not in gradients:
            gradients["down"] = place(
                emit_plain,
                flag,
                [down.pieces()],
                [(2 * units, half)],
                [(units, half)],
                [lambda k, s, f: (k, 0)],
                "place_down",
            )[0]
        if up.other is not None and "up" not in gradients:
            gradients["up"] = place(
                emit_plain,
                flag,
                [up.pieces()],
                [(half, 2 * units)],
                [(half, units)],
                [lambda k, s, f: (0, k)],
                "place_up",
            )[0]
        return [v + over_tensor(v) for v in operands]

    for turn in itertools.count(1):
        begin = [terms if turn == 1 else grads]
        operands = [row_sums] if turn == 1 else []
        moving = [c for c in (*chains, terms, grads) if c.moving is not None]
        ready = [c for c in (*chains, *begin) if c.stage + (c in moving) < len(c.hops)]
        if turn > 2 and not ready:
            break
        out = steps.run(moving, ready, lay, *operands)
        if turn == 1:
            (row_sums,) = out
    for c in (*chains, terms, grads):
        if c.moving is not None:
            c.finish()
    lay()

    row_sums = row_sums * (1.0 / full)
    output = (inputs.astype(F32) + terms.near + b_down.astype(F32)).astype(BF16)
    d_own = grads.near
    mean, inv_root = stat[:, 0:1], stat[:, 1:2]
    unit_own = (inputs.astype(F32) - mean) * inv_root
    input_grad = g_float + inv_root * (
        d_own * ln_gain.astype(F32)
        - row_sums[:, 0, :].reshape(rows, 1)
        - unit_own * row_sums[:, 1, :].reshape(rows, 1)
    )
    output, input_grad, gradients["down"], gradients["up"], late1.other = lax.optimization_barrier(
        (output, input_grad, gradients["down"], gradients["up"], late1.other)
    )
    small = late1.value[half : half + 8].astype(F32) + late1.other[half : half + 8].astype(F32)
    sums = small[:4].reshape(2, full)
    own = part(sums, 1, t, quarter)
    for k, v in (
        (1, part(sums, 1, 1 - t, quarter)),
        (2, part(sums, 1, 2 + t, quarter)),
        (3, part(sums, 1, 3 - t, quarter)),
    ):
        own = own + lax.ppermute(v, ("branch", "tensor"), [(i, i ^ k) for i in range(4)])
    bup = small[4:6].reshape(units)
    bup_far = over_branch(bup)
    grad_bup = jnp.where(b == 0, jnp.concatenate([bup, bup_far]), jnp.concatenate([bup_far, bup]))

    grad_qkv, grad_aout = place(
        emit_late,
        flag,
        [c.pieces() for c in (late0, late1)],
        [(3, half, 2 * heads_w), (2 * heads_w, half)],
        [(3, half, PAIR), (PAIR, half)],
        [lambda k, s, f: (0, 0, 2 * k + s), lambda k, s, f: (2 * k + s, 0)],
        "place_late",
    )
    return (
        output,
        input_grad,
        own[0],
        own[1],
        jnp.transpose(grad_qkv, (1, 0, 2)),
        grad_aout,
        gradients["up"],
        grad_bup,
        gradients["down"],
        small[6, :quarter],
    )


def solution(mesh):
    features = ("branch", "tensor")
    in_specs = (
        P("dp", features),
        P("dp", features),
        P("dp"),
        P("dp"),
        P("dp"),
        P(features),
        P(features),
        P("branch", None, "tensor"),
        P("tensor", "branch"),
        P("branch", "tensor"),
        P("tensor"),
        P("tensor", "branch"),
        P(features),
    )
    out_specs = (
        P("dp", features),
        P("dp", features),
        P(features),
        P(features),
        P("branch", None, "tensor"),
        P("tensor", "branch"),
        P("branch", "tensor"),
        P("tensor"),
        P("tensor", "branch"),
        P(features),
    )
    return jax.shard_map(
        functools.partial(shards, mesh.shape["dp"]),
        mesh=mesh,
        in_specs=in_specs,
        out_specs=out_specs,
        check_vma=False,
    )
```
